32 devices in a mesh: wide: 16 (over z, y, x), narrow: 2 (over core).
Axes of the slice: x: 2, y: 2, z: 4, core: 2. Of those that a mesh axis runs over, the one named last changes fastest.
Arguments:
- inputs: bfloat16 [32768, 1280], P(('wide', 'narrow')), may hold values from -6 to 6
- segments: int32 [2048, 16], P(('wide', 'narrow')), may hold values from 0 to 15, as said below
- starts: int32 [2048, 16], P(('wide', 'narrow')), may hold values from 0 to 15, as said below
- out_grad: bfloat16 [32768, 1280], P(('wide', 'narrow')), may hold values from -6 to 6
- proj_in: float32 [1280, 3840], P(('wide', 'narrow')), may hold values from -0.15625 to 0.15625
- proj_out: float32 [1280, 1280], P(('wide', 'narrow')), may hold values from -0.25 to 0.25
- up_proj: float32 [1280, 1280], P(('wide', 'narrow')), may hold values from -0.15625 to 0.15625
- down_proj: float32 [1280, 1280], P(('wide', 'narrow')), may hold values from -0.15625 to 0.15625
- gains_biases: float32 [5120], P(('wide', 'narrow')), as said below
- first_in: float32 [1280, 3840], P(('wide', 'narrow')), may hold values from -0.125 to 0.125
- first_out: float32 [1280, 1280], P(('wide', 'narrow')), may hold values from -0.125 to 0.125
- first_up: float32 [1280, 1280], P(('wide', 'narrow')), may hold values from -0.125 to 0.125
- first_down: float32 [1280, 1280], P(('wide', 'narrow')), may hold values from -0.125 to 0.125
- first_small: float32 [5120], P(('wide', 'narrow')), may hold values from -0.375 to 0.375
- second_in: float32 [1280, 3840], P(('wide', 'narrow')), may hold values from 6.6631965e-06 to 2.6652786e-05
- second_out: float32 [1280, 1280], P(('wide', 'narrow')), may hold values from 6.6631965e-06 to 2.6652786e-05
- second_up: float32 [1280, 1280], P(('wide', 'narrow')), may hold values from 6.6631965e-06 to 2.6652786e-05
- second_down: float32 [1280, 1280], P(('wide', 'narrow')), may hold values from 6.6631965e-06 to 2.6652786e-05
- second_small: float32 [5120], P(('wide', 'narrow')), may hold values from 5.9968766e-05 to 0.00023987507
Outputs:
- block_out: float32 [32768, 1280], P(('wide', 'narrow'))
- input_grad: float32 [32768, 1280], P(('wide', 'narrow'))
- grad_norm: float32 [], replicated
- updated_in: float32 [1280, 3840], P(('wide', 'narrow'))
- updated_out: float32 [1280, 1280], P(('wide', 'narrow'))
- updated_up: float32 [1280, 1280], P(('wide', 'narrow'))
- updated_down: float32 [1280, 1280], P(('wide', 'narrow'))
- updated_small: float32 [5120], P(('wide', 'narrow'))
- momentum_in: float32 [1280, 3840], P(('wide', 'narrow'))
- momentum_out: float32 [1280, 1280], P(('wide', 'narrow'))
- momentum_up: float32 [1280, 1280], P(('wide', 'narrow'))
- momentum_down: float32 [1280, 1280], P(('wide', 'narrow'))
- momentum_small: float32 [5120], P(('wide', 'narrow'))
- variance_in: float32 [1280, 3840], P(('wide', 'narrow'))
- variance_out: float32 [1280, 1280], P(('wide', 'narrow'))
- variance_up: float32 [1280, 1280], P(('wide', 'narrow'))
- variance_down: float32 [1280, 1280], P(('wide', 'narrow'))
- variance_small: float32 [5120], P(('wide', 'narrow'))
- copy_in: bfloat16 [1280, 3840], P(('wide', 'narrow'))
- copy_out: bfloat16 [1280, 1280], P(('wide', 'narrow'))
- copy_up: bfloat16 [1280, 1280], P(('wide', 'narrow'))
- copy_down: bfloat16 [1280, 1280], P(('wide', 'narrow'))
- copy_small: bfloat16 [5120], P(('wide', 'narrow'))
The draws below stay inside these ranges and needn't reach their ends.
Inputs may be any that keep to these rules, and one draw needn't show every extreme that they name: segments number the series packed in each row from 0, never falling along the row; a row holds one to 16 series, and one row holds 16 series of one patch each. starts[r, p] is the position in row r of the context patch of the series holding patch p: that series' first or second patch. `gains_biases`: entries 0 to 2560 are the two norms' gains, all positive; the rest are the up and down biases.
All inputs are finite; a program needn't handle non-finite values.
Results may differ from the reference program's by a relative error of at most 0.012.
Values may be sent and summed in bfloat16 or wider, within the bound.
A program may use at most 256 MiB of HBM per device.

```python
import math
import jax
import jax.numpy as jnp
from jax import lax

D = 1280
HEADS = 16
HEAD_DIM = 80
FF = 1280
PATCHES = 16
STEP = 5
ROWS = 2048
TOKENS = 32768
SMALL = 5120
PARAMS = 9835520


def series_layout(key):
    layout_key = jax.random.fold_in(key, 7)
    break_key = jax.random.fold_in(layout_key, 1)
    offset_key = jax.random.fold_in(layout_key, 2)
    position = jnp.arange(PATCHES, dtype=jnp.int32)
    row_index = jnp.arange(ROWS, dtype=jnp.int32)
    breaks = jax.random.randint(break_key, (ROWS, PATCHES), 0, 3) == 0
    breaks = jnp.logical_or(breaks, position[None, :] == 0)
    breaks = jnp.logical_or(breaks, row_index[:, None] == 0)
    seg_ids = jnp.cumsum(breaks.astype(jnp.int32), axis=1) - 1
    first_pos = lax.cummax(jnp.where(breaks, position[None, :], 0), axis=1)
    is_last = jnp.concatenate([breaks[:, 1:], jnp.ones((ROWS, 1), dtype=bool)], axis=1)
    last_pos = lax.cummin(jnp.where(is_last, position[None, :], PATCHES - 1), axis=1, reverse=True)
    offset_bits = jax.random.randint(offset_key, (ROWS, PATCHES), 0, 2)
    offset = jnp.take_along_axis(offset_bits, first_pos, axis=1)
    start_pos = jnp.minimum(first_pos + offset, last_pos)
    return (seg_ids.astype(jnp.int32), start_pos.astype(jnp.int32))


def draw_segments(key, part):
    return series_layout(key)[0]


def draw_starts(key, part):
    return series_layout(key)[1]


def draw_gains_biases(key, part):
    noise_key = jax.random.fold_in(key, 3)
    ramp = jnp.arange(D, dtype=jnp.float32) / D - 0.5
    noise = jnp.clip(jax.random.normal(noise_key, (SMALL,), jnp.float32), -3.0, 3.0)
    slope = math.log(3.0)
    gain_one = jnp.exp(slope * ramp) * (1.0 + 0.1 * noise[:D])
    gain_two = jnp.exp(slope * ramp) * (1.0 + 0.1 * noise[D:2 * D])
    biases = 0.5 * noise[2 * D:]
    return jnp.concatenate([gain_one, gain_two, biases]).astype(jnp.float32)


def block_levels(stream_key, shape, split, least, largest):
    level, own = 1.0, jax.random.fold_in(stream_key, 6)
    for axis_at, blocks in split:
        draws = jnp.exp(jax.random.uniform(jax.random.fold_in(own, axis_at), (blocks,), jnp.float32, least / len(split), largest / len(split)))
        level = level * jnp.repeat(draws, shape[axis_at] // blocks).reshape([-1 if axis == axis_at else 1 for axis in range(len(shape))])
    return level


def scatter_about(key, shape, width, most, cuts=(), kind=jnp.bfloat16):
    gain = block_levels(key, shape, cuts, -0.22, 0.18) if cuts else 1.0
    array = jax.random.normal(key, shape, jnp.float32) * width * gain
    return jnp.minimum(jnp.maximum(array, -most), most).astype(kind)


def setup_inputs(seed: int = 0) -> dict:
    seeds = jax.random.split(jax.random.key(seed), 20)
    inputs = scatter_about(seeds[0], (TOKENS, D), 1.0, 6.0, ((0, 32),))
    segments = draw_segments(jax.random.fold_in(seeds[19], 71), 0)
    starts = draw_starts(jax.random.fold_in(seeds[19], 71), 0)
    out_grad = scatter_about(seeds[3], (TOKENS, D), 1.0, 6.0, ((0, 32),))
    proj_in = scatter_about(seeds[4], (D, 3 * D), D ** -0.5, 0.15625, ((0, 32),), jnp.float32)
    proj_out = scatter_about(seeds[5], (D, D), (D // 2) ** -0.5, 0.25, ((0, 32),), jnp.float32)
    up_proj = scatter_about(seeds[6], (D, FF), D ** -0.5, 0.15625, ((0, 32),), jnp.float32)
    down_proj = scatter_about(seeds[7], (FF, D), FF ** -0.5, 0.15625, ((0, 32),), jnp.float32)
    gains_biases = draw_gains_biases(jax.random.fold_in(seeds[19], 71), 0)
    first_in = scatter_about(seeds[9], (D, 3 * D), (0.111 * 256.0 / PARAMS ** 0.5), 0.125, ((0, 32),), jnp.float32)
    first_out = scatter_about(seeds[10], (D, D), (0.111 * 256.0 / PARAMS ** 0.5), 0.125, ((0, 32),), jnp.float32)
    first_up = scatter_about(seeds[11], (D, FF), (0.111 * 256.0 / PARAMS ** 0.5), 0.125, ((0, 32),), jnp.float32)
    first_down = scatter_about(seeds[12], (FF, D), (0.111 * 256.0 / PARAMS ** 0.5), 0.125, ((0, 32),), jnp.float32)
    first_small = scatter_about(seeds[13], (SMALL,), (0.333 * 256.0 / PARAMS ** 0.5), 0.375, ((0, 32),), jnp.float32)
    second_in = jnp.clip(jnp.exp(math.log(2.6652785891201347e-05) - 1.3862944 * jax.random.uniform(seeds[14], (D, 3 * D), jnp.float32) ** block_levels(seeds[14], (D, 3 * D), ((0, 32),), -0.2, 0.2)), 6.663196472800337e-06, 2.6652785891201347e-05)
    second_out = jnp.clip(jnp.exp(math.log(2.6652785891201347e-05) - 1.3862944 * jax.random.uniform(seeds[15], (D, D), jnp.float32) ** block_levels(seeds[15], (D, D), ((0, 32),), -0.2, 0.2)), 6.663196472800337e-06, 2.6652785891201347e-05)
    second_up = jnp.clip(jnp.exp(math.log(2.6652785891201347e-05) - 1.3862944 * jax.random.uniform(seeds[16], (D, FF), jnp.float32) ** block_levels(seeds[16], (D, FF), ((0, 32),), -0.2, 0.2)), 6.663196472800337e-06, 2.6652785891201347e-05)
    second_down = jnp.clip(jnp.exp(math.log(2.6652785891201347e-05) - 1.3862944 * jax.random.uniform(seeds[17], (FF, D), jnp.float32) ** block_levels(seeds[17], (FF, D), ((0, 32),), -0.2, 0.2)), 6.663196472800337e-06, 2.6652785891201347e-05)
    second_small = jnp.clip(jnp.exp(math.log(0.00023987507) - 1.3862944 * jax.random.uniform(seeds[18], (SMALL,), jnp.float32) ** block_levels(seeds[18], (SMALL,), ((0, 32),), -0.2, 0.2)), 5.996876643621363e-05, 0.00023987507)
    return {"inputs": inputs, "segments": segments, "starts": starts, "out_grad": out_grad, "proj_in": proj_in, "proj_out": proj_out, "up_proj": up_proj, "down_proj": down_proj, "gains_biases": gains_biases, "first_in": first_in, "first_out": first_out, "first_up": first_up, "first_down": first_down, "first_small": first_small, "second_in": second_in, "second_out": second_out, "second_up": second_up, "second_down": second_down, "second_small": second_small}


@jax.custom_vjp
def low(v):
    return lax.optimization_barrier(v.astype(jnp.bfloat16)).astype(jnp.float32)

@jax.custom_vjp
def low_back(v):
    return v

def low_keep(v):
    return (low(v), None)

def low_pass(kept, grad):
    return (grad,)

def back_keep(v):
    return (v, None)

def back_low(kept, grad):
    return (low(grad),)
low.defvjp(low_keep, low_pass)
low_back.defvjp(back_keep, back_low)
eps_norm = 1e-05
eps_stat = 1e-05
rope_base = 10000.0
clip_limit = 256.0
learn_rate = 0.03
small_rate = 0.4
decay_rate = 0.1
beta_first = 0.9
beta_second = 0.999
eps_adam = 1e-08
highest = lax.Precision.HIGHEST

def rotate(heads_in):
    half_dim = heads_in.shape[-1] // 2
    position = jnp.arange(heads_in.shape[1], dtype=jnp.float32)
    inverse = rope_base ** (-jnp.arange(half_dim, dtype=jnp.float32) * 2.0 / heads_in.shape[-1])
    angles = position[:, None] * inverse[None, :]
    cosine = jnp.cos(angles)[None, :, None, :]
    sine_part = jnp.sin(angles)[None, :, None, :]
    front_half = heads_in[..., :half_dim]
    back_half = heads_in[..., half_dim:]
    return jnp.concatenate([front_half * cosine - back_half * sine_part, back_half * cosine + front_half * sine_part], axis=-1)

def rms_scale(values_in, gain_in):
    return values_in * lax.rsqrt(lax.optimization_barrier(jnp.mean(values_in * values_in, -1, keepdims=True)) + eps_norm) * gain_in

def series_stats(series_rows, start_pos):
    centre = lax.optimization_barrier(jnp.mean(series_rows, -1))
    offset = series_rows - centre[..., None]
    spread = jnp.sqrt(lax.optimization_barrier(jnp.mean(offset * offset, -1)) + eps_stat)
    return (jnp.take_along_axis(centre, start_pos, axis=1), jnp.take_along_axis(spread, start_pos, axis=1))

def masked_softmax(scores, allowed):
    scores = jnp.where(allowed, scores, -1e+30)
    row_max = lax.optimization_barrier(jnp.max(scores, -1, keepdims=True))
    expo = jnp.exp(scores - row_max)
    return expo / lax.optimization_barrier(jnp.sum(expo, -1, keepdims=True))

def block_forward(inputs_in, w_in, w_out, w_up, w_down, small, seg_ids, start_pos):
    row_count = seg_ids.shape[0]
    series_rows = inputs_in.reshape(row_count, PATCHES, D)
    centre, spread = series_stats(series_rows, start_pos)
    normal = ((series_rows - centre[..., None]) / spread[..., None]).reshape(row_count * PATCHES, D)
    gain_one = small[:D]
    gain_two = small[D:2 * D]
    bias_up = small[2 * D:2 * D + FF]
    bias_down = small[2 * D + FF:]
    h_one = low(rms_scale(normal, gain_one))
    packed = low_back(jnp.dot(h_one, w_in, precision=highest))
    shape_heads = (row_count, PATCHES, HEADS, HEAD_DIM)
    queries = low(rotate(packed[:, :D].reshape(shape_heads)))
    keys_low = low(rotate(packed[:, D:2 * D].reshape(shape_heads)))
    values_low = low(packed[:, 2 * D:].reshape(shape_heads))
    score_scale = 1.0 / math.sqrt(HEAD_DIM)
    scores = low_back(jnp.einsum('gqhd,gkhd->ghqk', queries, keys_low, precision=highest) * score_scale)
    position = jnp.arange(PATCHES)
    allowed = (seg_ids[:, :, None] == seg_ids[:, None, :]) & (position[None, None, :] <= position[None, :, None])
    attend = masked_softmax(scores, allowed[:, None])
    mixed_heads = jnp.einsum('ghqk,gkhd->gqhd', low(attend), values_low, precision=highest)
    mixed_heads = low_back(low(mixed_heads.reshape(row_count * PATCHES, D)))
    attention_out = low_back(jnp.dot(mixed_heads, w_out, precision=highest))
    residual = normal + attention_out
    h_two = low(rms_scale(residual, gain_two))
    pre_act = low_back(jnp.dot(h_two, w_up, precision=highest) + bias_up)
    activation = low(jax.nn.gelu(pre_act))
    branch = low_back(jnp.dot(activation, w_down, precision=highest) + bias_down)
    summed = (residual + branch).reshape(row_count, PATCHES, D)
    return (summed * spread[..., None] + centre[..., None]).reshape(row_count * PATCHES, D)

def adam_update(master, gradient, first, second, clip_scale, weight_decay, step_rate):
    gradient = gradient * clip_scale
    first_new = beta_first * first + (1.0 - beta_first) * gradient
    second_new = beta_second * second + (1.0 - beta_second) * gradient * gradient
    fix_first = 1.0 - beta_first ** STEP
    fix_second = 1.0 - beta_second ** STEP
    update_step = first_new / fix_first / (jnp.sqrt(second_new / fix_second) + eps_adam) + weight_decay * master
    master_new = master - step_rate * update_step
    return (master_new, first_new, second_new)

def reference(inputs, segments, starts, out_grad, proj_in, proj_out, up_proj, down_proj, gains_biases, first_in, first_out, first_up, first_down, first_small, second_in, second_out, second_up, second_down, second_small):
    copies = (low(proj_in), low(proj_out), low(up_proj), low(down_proj), low(gains_biases))
    group_rows = math.gcd(ROWS, 256)
    group_count = ROWS // group_rows
    input_groups = inputs.astype(jnp.float32).reshape(group_count, group_rows * PATCHES, D)
    grad_groups = out_grad.astype(jnp.float32).reshape(group_count, group_rows * PATCHES, D)
    seg_groups = segments.reshape(group_count, group_rows, PATCHES)
    start_groups = starts.reshape(group_count, group_rows, PATCHES)

    def group_step(totals, pieces):
        inputs_in, cotangent, seg_ids, start_pos = pieces

        def forward(x_in, w_in, w_out, w_up, w_down, small):
            return block_forward(x_in, w_in, w_out, w_up, w_down, small, seg_ids, start_pos)
        result, back_fn = jax.vjp(forward, inputs_in, copies[0], copies[1], copies[2], copies[3], copies[4])
        gradients = back_fn(cotangent)
        totals = tuple((total_part + grad_part for total_part, grad_part in zip(totals, gradients[1:])))
        return (totals, (result, gradients[0]))
    zeros = tuple((jnp.zeros_like(weight) for weight in copies))
    totals, (results, input_grads) = lax.scan(group_step, zeros, (input_groups, grad_groups, seg_groups, start_groups))
    block_out = results.reshape(TOKENS, D)
    input_grad = input_grads.reshape(TOKENS, D)
    squares = jnp.float32(0.0)
    for grad_part in totals:
        squares = squares + jnp.sum(grad_part * grad_part)
    grad_norm = jnp.sqrt(squares)
    clip_scale = jnp.minimum(1.0, clip_limit / (grad_norm + 1e-06))
    masters = (proj_in, proj_out, up_proj, down_proj, gains_biases)
    firsts = (first_in, first_out, first_up, first_down, first_small)
    seconds = (second_in, second_out, second_up, second_down, second_small)
    decays = (decay_rate, decay_rate, decay_rate, decay_rate, 0.0)
    rates = (learn_rate, learn_rate, learn_rate, learn_rate, small_rate)
    news = [adam_update(masters[i], totals[i], firsts[i], seconds[i], clip_scale, decays[i], rates[i]) for i in range(5)]
    return (block_out, input_grad, grad_norm, news[0][0], news[1][0], news[2][0], news[3][0], news[4][0], news[0][1], news[1][1], news[2][1], news[3][1], news[4][1], news[0][2], news[1][2], news[2][2], news[3][2], news[4][2], news[0][0].astype(jnp.bfloat16), news[1][0].astype(jnp.bfloat16), news[2][0].astype(jnp.bfloat16), news[3][0].astype(jnp.bfloat16), news[4][0].astype(jnp.bfloat16))
```

```python
import functools
import math

import jax
import jax.numpy as jnp
import numpy as np
from jax import lax
from jax.experimental import pallas as pl
from jax.experimental.pallas import tpu as pltpu
from jax.sharding import PartitionSpec as P

HEADS = 16
HEAD_DIM = 80
STEP = 5
PATCHES = 16

eps_norm = 1e-05
eps_stat = 1e-05
rope_base = 10000.0
clip_limit = 256.0
learn_rate = 0.03
small_rate = 0.4
decay_rate = 0.1
beta_first = 0.9
beta_second = 0.999
eps_adam = 1e-08

BF = jnp.bfloat16
F32 = jnp.float32
MESH = pl.DeviceIdType.MESH

COL = 640
UNITS = 12
STAGES = 6
SPAN = 256
GROUP = 128
TOK = 256
VMEM_LIMIT = 64 << 20


def lanes(ref_cols):
    return lax.broadcasted_iota(jnp.int32, (1, ref_cols), 1)


def nn(left_in, right_in):
    return lax.dot_general(
        left_in, right_in, (((1,), (0,)), ((), ())), preferred_element_type=F32
    )


def nt(left_in, right_in):
    return lax.dot_general(
        left_in, right_in, (((1,), (1,)), ((), ())), preferred_element_type=F32
    )


def rope_tables():
    half = HEAD_DIM // 2
    inverse = np.float32(rope_base) ** (-np.arange(half, dtype=np.float32) * np.float32(2.0) / np.float32(HEAD_DIM))
    angles = np.arange(PATCHES, dtype=np.float32)[:, None] * inverse.astype(np.float32)[None, :]
    cosine, sine = np.cos(angles), np.sin(angles)
    zero = np.zeros_like(sine)
    heads = COL // HEAD_DIM
    full = [
        np.tile(np.concatenate(pair, 1), (1, heads))
        for pair in ((cosine, cosine), (-sine, zero), (zero, sine))
    ]
    return np.stack(full).astype(np.float32)


def rotate(values_in, table, sign):
    rows = values_in.shape[0]
    ahead = pltpu.roll(values_in, COL - HEAD_DIM // 2, 1)
    behind = pltpu.roll(values_in, HEAD_DIM // 2, 1)
    cube = (rows // PATCHES, PATCHES, COL)
    turn = ahead.reshape(cube) * table[1] + behind.reshape(cube) * table[2]
    straight = values_in.reshape(cube) * table[0]
    return (straight + sign * turn).reshape(rows, COL)


def eye(size):
    row = lax.broadcasted_iota(jnp.int32, (size, size), 0)
    col = lax.broadcasted_iota(jnp.int32, (size, size), 1)
    return row == col


def to_column(row_in, same):
    return jnp.sum(jnp.where(same, row_in, 0.0), 1, keepdims=True)


def to_row(column_in, same):
    return jnp.sum(jnp.where(same, column_in, 0.0), 0, keepdims=True)


def context_mask(start_row, same):
    size = same.shape[0]
    row = lax.broadcasted_iota(jnp.int32, (size, size), 0)
    col = lax.broadcasted_iota(jnp.int32, (size, size), 1)
    start_col = to_column(start_row, same).astype(jnp.int32)
    return col == lax.div(row, PATCHES) * PATCHES + start_col


def pair_masks(pair):
    lane = lanes(SPAN)
    low = 160 * pair - 128 * (160 * pair // 128)
    return (
        (lane >= low) & (lane < low + HEAD_DIM),
        (lane >= low + HEAD_DIM) & (lane < low + 2 * HEAD_DIM),
    )


def both_heads(window, masks):
    zero = jnp.zeros_like(window)
    return jnp.concatenate([jnp.where(masks[0], window, zero), jnp.where(masks[1], window, zero)], 0)


def spread_windows(parts):
    tiles = []
    for tile in range(5):
        total = None
        for pair in (tile - 1, tile):
            if 0 <= pair < 4:
                piece = parts[pair][:, 128 * (tile - pair) : 128 * (tile - pair) + 128]
                total = piece if total is None else total + piece
        tiles.append(total)
    return jnp.concatenate(tiles, 1)


class Forward:
    def __init__(self, weight, refs):
        self.weight = weight
        (self.xv, self.dyv, self.seg, self.start, self.vec, self.rope, self.h1, self.tt, self.qkv, self.att,
         self.mix, self.r1, self.dg, self.stats, self.bsum) = refs
        self.tokens = self.xv.shape[0]
        self.width = self.xv.shape[1]

    def blocks(self, body, low=0, high=None):
        def step(i, carry):
            body(pl.multiple_of(i * TOK, TOK), i)
            return carry
        lax.fori_loop(low, self.tokens // TOK if high is None else high, step, 0)

    def norms(self, e2, low, high):
        width = self.width
        gain = self.vec[0:1, :]

        def body(at, i):
            rows = pl.ds(at, TOK)
            same = eye(TOK)
            x = self.xv[rows, :].astype(F32)
            mean = jnp.sum(x, 1, keepdims=True) * (1.0 / width)
            off = x - mean
            spread = jnp.sqrt(jnp.sum(off * off, 1, keepdims=True) * (1.0 / width) + eps_stat)
            mask = context_mask(self.start[pl.ds(i, 1), :], same)
            mu = jnp.sum(jnp.where(mask, to_row(mean, same), 0.0), 1, keepdims=True)
            sigma = jnp.sum(jnp.where(mask, to_row(spread, same), 0.0), 1, keepdims=True)
            z = (x - mu) / sigma
            scale = lax.rsqrt(jnp.sum(z * z, 1, keepdims=True) * (1.0 / width) + eps_norm)
            h1 = (z * scale * gain).astype(BF)
            self.h1[rows, :] = h1
            self.tt[0, :, rows] = h1.T
            dy = self.dyv[rows, :].astype(F32)
            low = (dy * sigma).astype(BF)
            e2[rows, :] = low
            self.bsum[0:1, :] += jnp.sum(low.astype(F32), 0, keepdims=True)
            self.stats[rows, 0:1] = mu
            self.stats[rows, 1:2] = sigma
            self.stats[rows, 2:3] = mean
            self.stats[rows, 3:4] = spread
            self.stats[rows, 4:5] = scale
            self.stats[rows, 6:7] = jnp.sum(dy, 1, keepdims=True)

        self.blocks(body, low, high)

    def project(self, unit):
        def body(at, i):
            rows = pl.ds(at, TOK)
            made = nn(self.h1[rows, :], self.weight(unit))
            if unit % 3 < 2:
                made = rotate(made, self.rope, 1.0)
            self.qkv[unit, rows, :] = made.astype(BF)

        self.blocks(body)

    def attend(self, half):
        scale = 1.0 / math.sqrt(HEAD_DIM)

        def step(g, carry):
            rows = pl.ds(pl.multiple_of(g * GROUP, GROUP), GROUP)
            same = eye(GROUP)
            row = lax.broadcasted_iota(jnp.int32, (GROUP, GROUP), 0)
            col = lax.broadcasted_iota(jnp.int32, (GROUP, GROUP), 1)
            seg_row = self.seg[pl.ds(g, 1), :]
            allowed = (
                (lax.div(row, PATCHES) == lax.div(col, PATCHES)) & (col <= row) & (to_column(seg_row, same) == seg_row)
            )
            parts = []
            for pair in range(4):
                lane = pl.ds(128 * (160 * pair // 128), SPAN)
                masks = pair_masks(pair)
                q = self.qkv[3 * half, rows, lane]
                k = both_heads(self.qkv[3 * half + 1, rows, lane], masks)
                v = both_heads(self.qkv[3 * half + 2, rows, lane], masks)
                scores = nt(q, k) * scale
                probs = []
                for head in range(2):
                    own = jnp.where(allowed, scores[:, GROUP * head : GROUP * (head + 1)], -1e30)
                    expo = jnp.exp(own - jnp.max(own, 1, keepdims=True))
                    probs.append((expo / jnp.sum(expo, 1, keepdims=True)).astype(BF))
                prob = jnp.concatenate(probs, 1)
                self.att[half, rows, SPAN * pair : SPAN * (pair + 1)] = prob
                parts.append(nn(prob, v))
            self.mix[rows, COL * half : COL * (half + 1)] = spread_windows(parts).astype(BF)
            return carry

        lax.fori_loop(0, self.tokens // GROUP, step, 0)

    def mix_turned(self, slot):
        def body(at, i):
            rows = pl.ds(at, TOK)
            self.tt[slot, :, rows] = self.mix[rows, :].T

        self.blocks(body)

    def residual(self, slot):
        width = self.width
        gain = self.vec[1:2, :]

        def body(at, i):
            rows = pl.ds(at, TOK)
            mix = self.mix[rows, :]
            made = jnp.concatenate([nn(mix, self.weight(6)), nn(mix, self.weight(7))], 1)
            z = (self.xv[rows, :].astype(F32) - self.stats[rows, 0:1]) / self.stats[rows, 1:2]
            r1 = z + made
            scale = lax.rsqrt(jnp.sum(r1 * r1, 1, keepdims=True) * (1.0 / width) + eps_norm)
            self.stats[rows, 5:6] = scale
            self.r1[rows, :] = r1
            h2 = (r1 * scale * gain).astype(BF)
            self.h1[rows, :] = h2
            self.tt[slot, :, rows] = h2.T

        self.blocks(body)

    def hidden(self, slot):
        bias = self.vec[2:3, :]
        c0 = math.sqrt(2.0 / math.pi)

        def body(at, i):
            rows = pl.ds(at, TOK)
            h2 = self.h1[rows, :]
            for half in range(2):
                cols = slice(COL * half, COL * (half + 1))
                u = nn(h2, self.weight(8 + half)) + bias[:, cols]
                square = u * u
                bend = jnp.tanh(c0 * (u + 0.044715 * u * square))
                act = (0.5 * u * (1.0 + bend)).astype(BF)
                slope = 0.5 * (1.0 + bend) + (0.5 * c0) * u * (1.0 - bend * bend) * (1.0 + (3 * 0.044715) * square)
                self.dg[rows, cols] = slope.astype(BF)
                self.mix[rows, cols] = act
                self.tt[slot, cols, rows] = act.T

        self.blocks(body)

    def result(self, out, out_sem, stage):
        bias = self.vec[3:4, :]
        count = self.tokens // TOK

        def copy(i):
            slot = lax.rem(i, 2)
            return pltpu.make_async_copy(stage.at[slot], out.at[pl.ds(pl.multiple_of(i * TOK, TOK), TOK), :], out_sem.at[slot])

        def body(at, i):
            rows = pl.ds(at, TOK)
            act = self.mix[rows, :]
            made = jnp.concatenate([nn(act, self.weight(10)), nn(act, self.weight(11))], 1)
            r2 = self.r1[rows, :] + (made + bias)

            @pl.when(i >= 2)
            def _():
                copy(i - 2).wait()

            stage[lax.rem(i, 2)] = r2 * self.stats[rows, 1:2] + self.stats[rows, 0:1]
            copy(i).start()
            self.stats[rows, 7:8] = jnp.sum(self.dyv[rows, :].astype(F32) * r2, 1, keepdims=True)

        self.blocks(body)
        for i in range(max(count - 2, 0), count):
            copy(i).wait()


class Backward:
    def __init__(self, refs):
        (self.wbuf, self.pbuf, self.lt, self.ea, self.eb, self.qkv, self.att, self.vec, self.rope,
         self.stats, self.bsum, self.start, self.rblk, self.bblk) = refs
        self.tokens, self.width = self.ea.shape

    def blocks(self, body, low=0, high=None):
        def step(i, carry):
            body(pl.multiple_of(i * TOK, TOK), i)
            return carry
        lax.fori_loop(low, self.tokens // TOK if high is None else high, step, 0)

    def weight(self, slot, half):
        return self.wbuf[slot, half].reshape(self.width, COL)

    def back(self, ref, rows, slot):
        return nt(ref[rows, :COL], self.weight(slot, 0)) + nt(ref[rows, COL:], self.weight(slot, 1))

    def weight_grad(self, slot, half, left, right):
        part = self.pbuf.at[slot, half]
        if len(part.shape) == 4:
            tall = part.shape[1] * part.shape[2]
            def step(i, carry):
                made = nn(self.lt[left, pl.ds(pl.multiple_of(i * tall, 16), tall), :], right())
                part[i] = made.astype(BF).reshape(part.shape[1:])
                return carry
            lax.fori_loop(0, part.shape[0], step, 0)
        else:
            def step(i, carry):
                rows = pl.ds(pl.multiple_of(i * TOK, TOK), TOK)
                part[rows, :] = nn(self.lt[left, rows, :], right()).astype(BF)
                return carry
            lax.fori_loop(0, self.width // TOK, step, 0)

    def hidden(self, slot):
        def body(at, i):
            rows = pl.ds(at, TOK)
            low = (self.back(self.ea, rows, slot) * self.eb[rows, :].astype(F32)).astype(BF)
            self.eb[rows, :] = low
            self.bsum[1:2, :] += jnp.sum(low.astype(F32), 0, keepdims=True)

        self.blocks(body)

    def stream(self, body, loads, low=0, high=None):
        count = self.tokens // TOK if high is None else high

        def copies(i):
            slot = lax.rem(i, 2)
            rows = pl.ds(pl.multiple_of(i * TOK, TOK), TOK)
            return [pltpu.make_async_copy(src.at[rows, :], buf.at[slot], sem.at[slot]) for src, buf, sem in loads]

        for cp in copies(low):
            cp.start()

        def inner(at, i):
            @pl.when(i + 1 < count)
            def _():
                for cp in copies(i + 1):
                    cp.start()
            for cp in copies(i):
                cp.wait()
            body(at, i, lax.rem(i, 2))

        self.blocks(inner, low, count)

    def second_norm(self, slot, loads):
        width = self.width
        gain = self.vec[1:2, :]

        def body(at, i, turn):
            rows = pl.ds(at, TOK)
            dh2 = self.back(self.eb, rows, slot)
            scale = self.stats[rows, 5:6]
            n2 = self.rblk[turn] * scale
            self.bsum[2:3, :] += jnp.sum(dh2 * n2, 0, keepdims=True)
            dn = dh2 * gain
            inner = jnp.sum(dn * n2, 1, keepdims=True) * (1.0 / width)
            dr1 = self.bblk[turn].astype(F32) * self.stats[rows, 1:2] + scale * (dn - n2 * inner)
            self.ea[rows, :] = dr1.astype(BF)

        self.stream(body, loads)

    def mixed(self, slot):
        def body(at, i):
            rows = pl.ds(at, TOK)
            self.eb[rows, :] = self.back(self.ea, rows, slot).astype(BF)

        self.blocks(body)

    def attend(self, half):
        scale = 1.0 / math.sqrt(HEAD_DIM)

        def step(g, carry):
            rows = pl.ds(pl.multiple_of(g * GROUP, GROUP), GROUP)
            dqs, dks, dvs = [], [], []
            for pair in range(4):
                low = 128 * (160 * pair // 128)
                lane = pl.ds(low, SPAN)
                masks = pair_masks(pair)
                q = both_heads(self.qkv[3 * half, rows, lane], masks)
                k = both_heads(self.qkv[3 * half + 1, rows, lane], masks)
                v = both_heads(self.qkv[3 * half + 2, rows, lane], masks)
                dmix = self.eb[rows, pl.ds(COL * half + low, SPAN)]
                prob = self.att[rows, SPAN * pair : SPAN * (pair + 1)]
                da = nt(dmix, v)
                p32 = prob.astype(F32)
                weighed = p32 * da
                ds = []
                for head in range(2):
                    cols = slice(GROUP * head, GROUP * (head + 1))
                    total = jnp.sum(weighed[:, cols], 1, keepdims=True)
                    ds.append(weighed[:, cols] - p32[:, cols] * total)
                dsb = jnp.concatenate(ds, 1).astype(BF)
                dqs.append(nn(dsb, k))
                turned = jnp.concatenate([dsb[:, :GROUP].T, dsb[:, GROUP:].T], 1)
                dks.append(nn(turned, q))
                flipped = jnp.concatenate([prob[:, :GROUP].T, prob[:, GROUP:].T], 1)
                dvs.append(nn(flipped, both_heads(dmix, masks)))
            dq = rotate(spread_windows(dqs) * scale, self.rope, -1.0)
            dk = rotate(spread_windows(dks) * scale, self.rope, -1.0)
            self.qkv[3 * half, rows, :] = dq.astype(BF)
            self.qkv[3 * half + 1, rows, :] = dk.astype(BF)
            self.qkv[3 * half + 2, rows, :] = spread_windows(dvs).astype(BF)
            return carry

        lax.fori_loop(0, self.tokens // GROUP, step, 0)

    def first_norm(self, loads, out, out_sem, stage, low, high):
        width = self.width
        gain = self.vec[0:1, :]
        count = self.tokens // TOK

        def copy(i):
            slot = lax.rem(i, 2)
            return pltpu.make_async_copy(stage.at[slot], out.at[pl.ds(pl.multiple_of(i * TOK, TOK), TOK), :], out_sem.at[slot])

        def body(at, i, turn):
            rows = pl.ds(at, TOK)
            same = eye(TOK)
            dh1 = nt(self.qkv[0, rows, :], self.weight(0, 0))
            for unit in range(1, 6):
                dh1 += nt(self.qkv[unit, rows, :], self.weight(unit // 2, unit % 2))
            mu, sigma = self.stats[rows, 0:1], self.stats[rows, 1:2]
            mean, spread = self.stats[rows, 2:3], self.stats[rows, 3:4]
            scale = self.stats[rows, 4:5]
            x = self.bblk[turn].astype(F32)
            z = (x - mu) / sigma
            n1 = z * scale
            self.bsum[3:4, :] += jnp.sum(dh1 * n1, 0, keepdims=True)
            dn = dh1 * gain
            inner = jnp.sum(dn * n1, 1, keepdims=True) * (1.0 / width)
            dz = scale * (dn - n1 * inner) + self.ea[rows, :].astype(F32)
            inv = 1.0 / sigma
            dmu = self.stats[rows, 6:7] - jnp.sum(dz, 1, keepdims=True) * inv
            dsigma = self.stats[rows, 7:8] - jnp.sum(dz * z, 1, keepdims=True) * inv
            mask = context_mask(self.start[pl.ds(i, 1), :], same)
            dmean = to_column(jnp.sum(jnp.where(mask, dmu, 0.0), 0, keepdims=True), same)
            dspread = to_column(jnp.sum(jnp.where(mask, dsigma, 0.0), 0, keepdims=True), same)
            dx = dz * inv + (dmean * (1.0 / width) + (x - mean) * (dspread * (1.0 / width) / spread))

            @pl.when(i >= 2)
            def _():
                copy(i - 2).wait()

            stage[lax.rem(i, 2)] = dx
            copy(i).start()

        self.stream(body, loads, low, high)
        if high == count:
            for i in range(max(count - 2, 0), count):
                copy(i).wait()


class Spot:
    def __init__(self, layers):
        self.layers = layers
        wide, self.c = lax.axis_index("wide"), lax.axis_index("narrow")
        self.z, self.p = lax.div(wide, 4), lax.rem(wide, 4)
        self.px = self.p + 1 - 2 * lax.rem(self.p, 2)
        self.py = lax.rem(self.p + 2, 4)
        self.pd = 3 - self.p
        self.me = 2 * wide + self.c
        self.count = 8 * layers
        self.sibling = self.device(self.z, self.p, 1 - self.c)
        self.across_x = self.device(self.z, self.px, self.c)
        self.across_y = self.device(self.z, self.py, self.c)

    def device(self, z, p, c):
        return (z * 4 + p, c)

    def layer(self, k):
        return lax.rem(self.z + k, self.layers)

    def in_layer(self, z):
        return self.device(z, self.p, self.c)

    def others(self, body):
        def step(k, carry):
            other = lax.rem(self.me + k, self.count)
            body(k, other, (lax.div(other, 2), lax.rem(other, 2)))
            return carry
        lax.fori_loop(1, self.count, step, 0)

    def meet(self):
        door = pltpu.get_barrier_semaphore()
        self.others(lambda k, other, device: pl.semaphore_signal(door, 1, device_id=device, device_id_type=MESH))
        pl.semaphore_wait(door, self.count - 1)


def remote(src, dst, send, recv, device):
    return pltpu.make_async_remote_copy(src, dst, send, recv, device_id=device, device_id_type=MESH)


class Posted:
    def __init__(self):
        self.groups = {}

    def go(self, key, *args):
        copy = remote(*args)
        copy.start()
        self.groups.setdefault(key, []).append(copy)

    def sent(self, key):
        for copy in self.groups.pop(key, []):
            copy.wait_send()

    def all_sent(self):
        for key in list(self.groups):
            self.sent(key)


class Gather(Posted):
    @staticmethod
    def scratch(layers, rows):
        D = pltpu.SemaphoreType.DMA
        n = STAGES
        return [pltpu.VMEM((n, rows, COL), F32), D((n,)), D((n,)), D((n,)), D((n, layers)), D((n, layers)),
                D((n, layers, 2)), D((n, layers, 2)), D((n, 2)), D((n, 2)), D((n, 4)), D((n, 4))]

    def __init__(self, spot, full, owned, refs):
        super().__init__()
        self.spot, self.full, self.owned = spot, full, owned
        (self.desk, self.local, self.es, self.er, self.zs, self.zr, self.ps, self.pr, self.ds, self.dr, self.ss, self.sr) = refs
        self.rows = self.desk.shape[1]
        self.half = self.rows // 2
        self.cut = self.rows // 32 * 16 + (16 if self.rows % 32 else 0)

    def unit(self, j):
        return 2 * j + self.spot.c

    def shard(self, j, unit):
        if j < 3:
            column = 2 * COL * lax.rem(unit, 3) + COL * lax.div(unit, 3)
            return self.owned[0].at[:, pl.ds(pl.multiple_of(column, 128), COL)]
        return self.owned[j - 2].at[:, pl.ds(pl.multiple_of(COL * lax.rem(unit, 2), 128), COL)]

    def desk_rows(self, j, core):
        return self.desk.at[j, pl.ds(pl.multiple_of(self.half * core, 8), self.half), :]

    def prepare(self, j):
        c = self.spot.c
        place_at = self.desk_rows(j, c)
        pltpu.make_async_copy(self.shard(j, 2 * j + c), place_at, self.local.at[j]).start()
        self.go(j, self.shard(j, 2 * j + 1 - c), place_at, self.es.at[j], self.er.at[j], self.spot.sibling)

    def across(self, j, k):
        s = self.spot
        block = self.full.at[self.unit(j), s.layer(self.spot.layers - k), s.p]
        self.go(j, block, block, self.ps.at[j, k, 0], self.pr.at[j, k, 0], s.across_x)
        self.go(j, block, block, self.ps.at[j, k, 1], self.pr.at[j, k, 1], s.across_y)

    def e1(self, j):
        s = self.spot
        mine, other = self.desk_rows(j, s.c), self.desk_rows(j, 1 - s.c)
        pltpu.make_async_copy(mine, mine, self.local.at[j]).wait()
        remote(other, other, self.es.at[j], self.er.at[j], s.sibling).wait_recv()
        self.full[self.unit(j), s.z, s.p] = self.desk[j].astype(BF)
        block = self.full.at[self.unit(j), s.z, s.p]
        for k in range(1, s.layers):
            self.go(j, block, block, self.zs.at[j, k], self.zr.at[j, k], s.in_layer(s.layer(k)))
        self.across(j, 0)

    def e2(self, j):
        s = self.spot
        for k in range(1, s.layers):
            z = s.layer(s.layers - k)
            block = self.full.at[self.unit(j), z, s.p]
            remote(block, block, self.zs.at[j, k], self.zr.at[j, k], s.in_layer(z)).wait_recv()
            self.across(j, k)
        self.to_sibling(j, 0, s.p)

    def to_sibling(self, j, i, p):
        line = self.full.at[self.unit(j), :, p]
        self.go(j, line, line, self.ss.at[j, i], self.sr.at[j, i], self.spot.sibling)

    def corner(self, j, p, top):
        rows = pl.ds(0, self.cut) if top else pl.ds(self.cut, self.rows - self.cut)
        return self.full.at[self.unit(j), :, p, rows, :]

    def e3(self, j):
        s = self.spot
        for k in range(s.layers):
            z = s.layer(s.layers - k)
            for i, p in ((0, s.px), (1, s.py)):
                block = self.full.at[self.unit(j), z, p]
                remote(block, block, self.ps.at[j, k, i], self.pr.at[j, k, i], s.across_x).wait_recv()
        top, rest = self.corner(j, s.px, True), self.corner(j, s.py, False)
        self.go(j, top, top, self.ds.at[j, 0], self.dr.at[j, 0], s.across_y)
        self.go(j, rest, rest, self.ds.at[j, 1], self.dr.at[j, 1], s.across_x)
        self.to_sibling(j, 1, s.px)
        self.to_sibling(j, 2, s.py)

    def e4(self, j):
        s = self.spot
        top, rest = self.corner(j, s.pd, True), self.corner(j, s.pd, False)
        remote(top, top, self.ds.at[j, 0], self.dr.at[j, 0], s.across_y).wait_recv()
        remote(rest, rest, self.ds.at[j, 1], self.dr.at[j, 1], s.across_x).wait_recv()
        self.to_sibling(j, 3, s.pd)

    def e5(self, j):
        s = self.spot
        for i, p in enumerate((s.p, s.px, s.py, s.pd)):
            line = self.full.at[2 * j + 1 - s.c, :, p]
            remote(line, line, self.ss.at[j, i], self.sr.at[j, i], s.sibling).wait_recv()


class Scatter(Posted):
    SLOTS = 3

    @staticmethod
    def scratch(layers, rows):
        D, V = pltpu.SemaphoreType.DMA, pltpu.VMEM
        n, m = STAGES, Scatter.SLOTS
        return [V((n - 1, layers, 4, rows, COL), BF), V((m, layers, rows, COL), BF), V((m, 2, layers, rows, COL), BF),
                V((m, layers, rows, COL), BF), V((m, rows, COL), F32), V((UNITS, rows // 2, COL), F32),
                D((n,)), D((n,)), D((n, 2)), D((n, 2)), D((n, 2)), D((n, 2)), D((n, layers)), D((n, layers)), D((n,)), D((n,))]

    def __init__(self, spot, part, refs):
        super().__init__()
        self.spot, self.part = spot, part
        (self.sums, self.dg, self.pl, self.zb, self.fin, self.res,
         self.ss, self.sr, self.ds, self.dr, self.ps, self.pr, self.zs, self.zr, self.fs, self.fr) = refs
        self.rows = self.dg.shape[2]
        self.half = self.rows // 2
        self.cut = self.rows // 32 * 16 + (16 if self.rows % 32 else 0)

    def sum_at(self, j):
        return self.sums.at[j % (STAGES - 1)]

    def each_layer(self, body):
        def step(z, carry):
            body(z)
            return carry
        lax.fori_loop(0, self.spot.layers, step, 0)

    def f1(self, j):
        s = self.spot
        self.go(("f1", j), self.part.at[j % 2, 1 - s.c], self.sum_at(j), self.ss.at[j], self.sr.at[j], s.sibling)

    def f2(self, j):
        s = self.spot
        own, total = self.part.at[j % 2, s.c], self.sum_at(j)
        slot = j % self.SLOTS
        remote(total, total, self.ss.at[j], self.sr.at[j], s.sibling).wait_recv()

        def add(p):
            def one(z):
                total[z, p] = (total[z, p].astype(F32) + own[z, p].astype(F32)).astype(BF)
            self.each_layer(one)

        add(s.pd)
        for i, (rows, device) in enumerate(((pl.ds(0, self.cut), s.across_y), (pl.ds(self.cut, self.rows - self.cut), s.across_x))):
            self.go(j, total.at[:, s.pd, rows, :], self.dg.at[slot, :, rows, :], self.ds.at[j, i], self.dr.at[j, i], device)
        for p in (s.px, s.py, s.p):
            add(p)

    def f3(self, j):
        s = self.spot
        total, slot = self.sum_at(j), j % self.SLOTS
        for i, (low, size, p) in enumerate(((0, self.cut, s.px), (self.cut, self.rows - self.cut, s.py))):
            rows = pl.ds(low, size)
            came = self.dg.at[slot, :, rows, :]
            remote(came, came, self.ds.at[j, i], self.dr.at[j, i], s.across_y).wait_recv()

            def one(z):
                total[z, p, rows, :] = (total[z, p, rows, :].astype(F32) + self.dg[slot, z, rows, :].astype(F32)).astype(BF)
            self.each_layer(one)
        for i, (p, device) in enumerate(((s.px, s.across_x), (s.py, s.across_y))):
            self.go(j, total.at[:, p], self.pl.at[slot, i], self.ps.at[j, i], self.pr.at[j, i], device)

    def f4(self, j):
        s = self.spot
        total, slot = self.sum_at(j), j % self.SLOTS
        for i in range(2):
            came = self.pl.at[slot, i]
            remote(came, came, self.ps.at[j, i], self.pr.at[j, i], s.across_x).wait_recv()
        for k in [*range(1, s.layers), 0]:
            z = s.layer(k)
            total[z, s.p] = (total[z, s.p].astype(F32) + self.pl[slot, 0, z].astype(F32) + self.pl[slot, 1, z].astype(F32)).astype(BF)
            if k:
                self.go(j, total.at[z, s.p], self.zb.at[slot, k], self.zs.at[j, k], self.zr.at[j, k], s.in_layer(z))

    def f5(self, j):
        s = self.spot
        slot = j % self.SLOTS
        total = self.sums[j % (STAGES - 1), s.z, s.p].astype(F32)
        for k in range(1, s.layers):
            came = self.zb.at[slot, k]
            remote(came, came, self.zs.at[j, k], self.zr.at[j, k], s.across_x).wait_recv()
            total = total + self.zb[slot, k].astype(F32)
        self.sent(j)
        self.sent(("fin", j - self.SLOTS))
        self.fin[slot] = total
        mine, other = (pl.ds(pl.multiple_of(self.half * c, 8), self.half) for c in (s.c, 1 - s.c))
        self.res[2 * j + s.c] = self.fin[slot, mine, :]
        self.go(("fin", j), self.fin.at[slot, other, :], self.res.at[2 * j + s.c], self.fs.at[j], self.fr.at[j], s.sibling)

    def f6(self, j):
        s = self.spot
        came = self.res.at[2 * j + 1 - s.c]
        remote(came, came, self.fs.at[j], self.fr.at[j], s.sibling).wait_recv()

    def advance(self, t):
        for back, step in ((5, self.f6), (4, self.f5), (3, self.f4), (2, self.f3), (1, self.f2), (0, self.f1)):
            if 0 <= t - back < STAGES:
                step(t - back)


class Everyone(Posted):
    @staticmethod
    def scratch(count):
        D = pltpu.SemaphoreType.DMA
        return [D((count,)), D((count,))]

    def __init__(self, spot, board, refs):
        self.spot, self.board = spot, board
        self.send_sem, self.recv_sem = refs

    def post(self, source):
        s = self.spot
        def one(k, other, device):
            remote(source(other), self.board.at[s.me], self.send_sem.at[k], self.recv_sem.at[k], device).start()
        s.others(one)

    def collect(self, own):
        s = self.spot
        def one(k, other, device):
            came = self.board.at[lax.rem(s.me + s.count - k, s.count)]
            remote(came, came, self.send_sem.at[k], self.recv_sem.at[k], device).wait()
        s.others(one)
        self.board[s.me] = own


def place(kind, count):
    return [pl.BlockSpec(memory_space=kind)] * count


def load(src, dst, sem):
    copy = pltpu.make_async_copy(src, dst, sem)
    copy.start()
    return copy


def unit_matrix(values):
    return values.reshape(-1, COL)


def window_tile(per, owner):
    return lax.div(per * owner, 128)


def forward_kernel(layers, *refs):
    joined = layers > 0
    refs = list(refs)
    take = lambda n: [refs.pop(0) for _ in range(n)]
    x, dy, seg, start, rope = take(5)
    owned = take(5) if joined else take(2)
    block_out, turned, qkv_out, att_out, r1_out, dg_out, e2_out, stats_out, bsum_out = take(9)
    weights_out, vec_out = take(2) if joined else (None, None)
    full, xv, dyv, h1, tt, qkv, att, mix, r1, dg, stats, bsum, stage, sem, osem = take(15)
    fetch = [load(x, xv, sem.at[0]), load(dy, dyv, sem.at[1])]
    bsum[...] = jnp.zeros_like(bsum)
    if joined:
        spot = Spot(layers)
        board, canvas, vec, wsem = take(4)
        everyone = Everyone(spot, board, take(2))
        gather = Gather(spot, full, owned[:4], refs)
        window = owned[4]
        weight = lambda u: unit_matrix(full[u])
        spot.meet()
        for j in range(STAGES):
            gather.prepare(j)
        everyone.post(lambda other: window)
        gather.e1(0)
        gather.e1(1)
        everyone.collect(window[...])
        canvas[...] = jnp.zeros_like(canvas)
    else:
        vec = owned[1]
        weight = lambda u: full[u]
        fetch.append(load(owned[0], full, sem.at[2]))
    f = Forward(weight, (xv, dyv, seg, start, vec, rope, h1, tt, qkv, att, mix, r1, dg, stats, bsum))
    blocks = f.tokens // TOK
    if joined:
        share = 4 * f.width // spot.count

        def put(owner, carry):
            canvas[pl.ds(window_tile(share, owner), 2)] += board[owner]
            return carry
        lax.fori_loop(0, spot.count, put, 0)
        tiles = f.width // 128
        for row in range(4):
            for tile in range(tiles):
                vec[row : row + 1, 128 * tile : 128 * (tile + 1)] = canvas[row * tiles + tile]
    fetch[0].wait()
    fetch[1].wait()
    wouts = []

    def stage_done(j):
        if joined:
            gather.e5(j)
            wouts.append(load(full.at[pl.ds(2 * j, 2)], weights_out.at[pl.ds(2 * j, 2)], wsem.at[j]))

    outs = {}

    def work(j):
        if j == 0:
            outs["h1"] = load(tt.at[0], turned.at[0], sem.at[3])
            outs["e2"] = load(mix, e2_out, sem.at[4])
        if j < 3:
            f.project(2 * j)
            f.project(2 * j + 1)
        if j == 1:
            outs.pop("e2").wait()
        if j in (1, 2):
            f.attend(j - 1)
        if j == 2:
            outs["qkv"] = load(qkv, qkv_out, sem.at[5])
            outs["att"] = load(att, att_out, sem.at[6])
            f.mix_turned(1)
            outs["o"] = load(tt.at[1], turned.at[1], sem.at[7])
        if j == 3:
            outs.pop("h1").wait()
            f.residual(0)
            outs["h2"] = load(tt.at[0], turned.at[2], sem.at[3])
            outs["r1"] = load(r1, r1_out, sem.at[8])
        if j == 4:
            outs.pop("o").wait()
            f.hidden(1)
            outs["a"] = load(tt.at[1], turned.at[3], sem.at[7])
            outs["dg"] = load(dg, dg_out, sem.at[9])
        if j == 5:
            f.result(block_out, osem, stage)

    if joined:
        f.norms(mix, 0, 1)
        gather.e2(0)
        f.norms(mix, 1, 2)
        gather.e1(2)
        gather.e2(1)
        f.norms(mix, 2, blocks)
        gather.e3(0)
        for t in range(1, STAGES + 1):
            if t + 2 < STAGES:
                gather.e1(t + 2)
            if t + 1 < STAGES:
                gather.e2(t + 1)
            if t < STAGES:
                gather.e3(t)
            gather.e4(t - 1)
            stage_done(t - 1)
            work(t - 1)
    else:
        f.norms(mix, 0, blocks)
        fetch[2].wait()
        for j in range(STAGES):
            work(j)
    ends = [load(stats, stats_out, sem.at[10]), load(bsum, bsum_out, sem.at[11])]
    if joined:
        ends.append(load(vec, vec_out, sem.at[2]))
    for copy in [*ends, *outs.values(), *wouts]:
        copy.wait()
    if joined:
        gather.all_sent()


def forward(layers, rows, x, dy, seg, start, rope, owned):
    tokens, width = x.shape
    S = jax.ShapeDtypeStruct
    V = pltpu.VMEM
    D = pltpu.SemaphoreType.DMA
    joined = layers > 0
    shape = (UNITS, layers, 4, rows, COL) if joined else (UNITS, width, COL)
    outs = [S((tokens, width), F32), S((4, width, tokens), BF), S((6, tokens, COL), BF), S((2, tokens, 4 * SPAN), BF),
            S((tokens, width), F32), S((tokens, width), BF), S((tokens, width), BF), S((tokens, 128), F32), S((8, width), F32)]
    scratch = [V(shape, BF), V((tokens, width), BF), V((tokens, width), BF), V((tokens, width), BF), V((2, width, tokens), BF),
               V((6, tokens, COL), BF), V((2, tokens, 4 * SPAN), BF), V((tokens, width), BF), V((tokens, width), F32),
               V((tokens, width), BF), V((tokens, 128), F32), V((8, width), F32), V((2, TOK, width), F32), D((12,)), D((2,))]
    if joined:
        outs += [S(shape, BF), S((8, width), F32)]
        count = 8 * layers
        scratch += [V((count, 2, 1, 128), F32), V((4 * width // 128 + 8, 1, 128), F32), V((8, width), F32), D((STAGES,))]
        scratch += Everyone.scratch(count) + Gather.scratch(layers, rows)
    return pl.pallas_call(
        functools.partial(forward_kernel, layers),
        out_shape=outs,
        in_specs=place(pl.ANY, 2) + place(pltpu.VMEM, 3) + (place(pl.ANY, 4) if joined else place(pl.ANY, 1)) + place(pltpu.VMEM, 1),
        out_specs=place(pl.ANY, len(outs)),
        scratch_shapes=scratch,
        compiler_params=pltpu.CompilerParams(vmem_limit_bytes=VMEM_LIMIT, **(dict(collective_id=0, has_side_effects=True) if joined else {})),
        name="layer_forward",
    )(x, dy, seg, start, rope, *owned)


def backward_kernel(layers, *refs):
    joined = layers > 0
    refs = list(refs)
    take = lambda n: [refs.pop(0) for _ in range(n)]
    x, dy, start, rope, vec, turned, qkv_in, att_in, r1_in, dg_in, e2_in, stats_in, bsum_in, gw = take(14)
    dx_out = take(1)[0]
    grad_out, small_out, norm_out = take(3) if joined else (*take(2), None)
    wbuf, part, lt, ea, eb, qkv, att, stats, bsum, rblk, bblk, sem, ssem, osem, psem = take(15)

    def weights(j, slot, s):
        return load(gw.at[pl.ds(2 * j, 2)], wbuf.at[slot], s)

    e = load(e2_in, ea, sem.at[1])
    l0 = load(turned.at[3], lt.at[0], sem.at[2])
    w5 = weights(5, 0, sem.at[0])
    d = load(dg_in, eb, sem.at[3])
    s = load(stats_in, stats, sem.at[4])
    bs = load(bsum_in, bsum, sem.at[5])
    l1 = load(turned.at[2], lt.at[1], sem.at[7])
    w4 = weights(4, 1, sem.at[6])
    w3 = weights(3, 2, sem.at[8])
    qk = load(qkv_in, qkv, sem.at[9])
    at = load(att_in.at[0], att, sem.at[10])
    if joined:
        spot = Spot(layers)
        board, norms, sheet, note = take(4)
        small_talk = Everyone(spot, board, take(2))
        norm_talk = Everyone(spot, norms, take(2))
        scatter = Scatter(spot, part, refs)
        spot.meet()
    b = Backward((wbuf, part, lt, ea, eb, qkv, att, vec, rope, stats, bsum, start, rblk, bblk))
    blocks = b.tokens // TOK

    def spill(r):
        return pltpu.make_async_copy(part.at[r % 2], grad_out.at[pl.ds(2 * r, 2)], psem.at[r % 2])

    def grad_stage(r, left, rights):
        if r >= 2:
            if joined:
                scatter.sent(("f1", r - 2))
            else:
                spill(r - 2).wait()
        for half in range(2):
            b.weight_grad(r % 2, half, left, rights[half])
        if joined:
            scatter.advance(r)
        else:
            spill(r).start()

    halves = lambda ref: [lambda: ref[:, :COL], lambda: ref[:, COL:]]
    units = lambda u: [lambda: qkv[u], lambda: qkv[u + 1]]
    for cp in (e, l0):
        cp.wait()
    grad_stage(0, 0, halves(ea))
    l2 = load(turned.at[1], lt.at[0], sem.at[2])
    for cp in (w5, d, s, bs):
        cp.wait()
    b.hidden(0)
    w0 = weights(0, 0, sem.at[0])
    l1.wait()
    grad_stage(1, 1, halves(eb))
    l3 = load(turned.at[0], lt.at[1], sem.at[7])
    w4.wait()
    b.second_norm(1, [(r1_in, rblk, ssem.at[0]), (dy, bblk, ssem.at[1])])
    w1 = weights(1, 1, sem.at[6])
    l2.wait()
    grad_stage(2, 0, halves(ea))
    w3.wait()
    b.mixed(2)
    w2 = weights(2, 2, sem.at[8])
    qk.wait()
    at.wait()
    b.attend(0)
    at = load(att_in.at[1], att, sem.at[10])
    l3.wait()
    grad_stage(3, 1, units(0))
    at.wait()
    b.attend(1)
    grad_stage(4, 1, units(2))
    grad_stage(5, 1, units(4))
    for cp in (w0, w1, w2):
        cp.wait()
    loads = [(x, bblk, ssem.at[1])]
    if joined:
        for i in range(blocks):
            b.first_norm(loads, dx_out, osem, rblk, i, i + 1)
            scatter.advance(STAGES + i)
    else:
        b.first_norm(loads, dx_out, osem, rblk, 0, blocks)
    if not joined:
        fin = load(bsum, small_out, sem.at[5])
        for r in range(STAGES - 2, STAGES):
            spill(r).wait()
        fin.wait()
        return
    tiles = b.width // 128
    for row, source in enumerate((3, 2, 1, 0)):
        for tile in range(tiles):
            sheet[row * tiles + tile] = bsum[source : source + 1, 128 * tile : 128 * (tile + 1)]
    share = 4 * b.width // spot.count
    own = lambda owner: sheet.at[pl.ds(window_tile(share, owner), 2)]
    small_talk.post(own)
    for t in range(STAGES + blocks, STAGES + 6):
        scatter.advance(t)
    small_talk.collect(sheet[pl.ds(window_tile(share, spot.me), 2)])
    fin = load(scatter.res, grad_out, sem.at[9])

    def add(owner, carry):
        return carry + board[owner]
    total = lax.fori_loop(0, spot.count, add, jnp.zeros((2, 1, 128), F32))
    first = lax.rem(share * spot.me, 128)
    spots = lax.broadcasted_iota(jnp.int32, (2, 1, 128), 0) * 128 + lax.broadcasted_iota(jnp.int32, (2, 1, 128), 2)
    mine = jnp.where((spots >= first) & (spots < first + share), total, 0.0)
    small_out[...] = mine

    def square(unit, carry):
        values = scatter.res[unit]
        return carry + jnp.sum(values * values, 0, keepdims=True)
    squares = lax.fori_loop(0, UNITS, square, jnp.zeros((1, COL), F32))
    value = jnp.sum(squares) + jnp.sum(mine * mine)
    note[...] = jnp.full((8, 128), value, F32)
    norm_talk.post(lambda other: note)
    norm_talk.collect(note[...])
    whole = lax.fori_loop(0, spot.count, lambda owner, carry: carry + norms[owner], jnp.zeros((8, 128), F32))
    norm_out[...] = jnp.sqrt(whole)
    fin.wait()
    scatter.all_sent()


def backward(layers, rows, *args):
    tokens, width = args[0].shape
    S = jax.ShapeDtypeStruct
    V = pltpu.VMEM
    D = pltpu.SemaphoreType.DMA
    joined = layers > 0
    grid = (layers, 4, rows) if joined else (width,)
    outs = [S((tokens, width), F32)]
    scratch = [V((3, 2) + grid + (COL,), BF), V((2, 2) + grid + (COL,), BF), V((2, width, tokens), BF), V((tokens, width), BF), V((tokens, width), BF),
               V((6, tokens, COL), BF), V((tokens, 4 * SPAN), BF), V((tokens, 128), F32), V((8, width), F32),
               V((2, TOK, width), F32), V((2, TOK, width), BF), D((11,)), D((2, 2)), D((2,)), D((2,))]
    specs = place(pl.ANY, 3)
    if joined:
        count = 8 * layers
        outs += [S((UNITS, rows // 2, COL), F32), S((2, 1, 128), F32), S((8, 128), F32)]
        specs = place(pl.ANY, 2) + place(pltpu.VMEM, 2)
        scratch += [V((count, 2, 1, 128), F32), V((count, 8, 128), F32), V((4 * width // 128 + 8, 1, 128), F32), V((8, 128), F32)]
        scratch += Everyone.scratch(count) + Everyone.scratch(count) + Scatter.scratch(layers, rows)
    else:
        outs += [S((UNITS, width, COL), BF), S((8, width), F32)]
    return pl.pallas_call(
        functools.partial(backward_kernel, layers),
        out_shape=outs,
        in_specs=place(pl.ANY, 2) + place(pltpu.VMEM, 3) + place(pl.ANY, 9),
        out_specs=specs,
        scratch_shapes=scratch,
        compiler_params=pltpu.CompilerParams(vmem_limit_bytes=VMEM_LIMIT, **(dict(collective_id=1, has_side_effects=True) if joined else {})),
        name="layer_backward",
    )(*args)


def adam_update(master, gradient, first, second, clip_scale, weight_decay, step_rate):
    gradient = gradient * clip_scale
    first_new = beta_first * first + (1.0 - beta_first) * gradient
    second_new = beta_second * second + (1.0 - beta_second) * gradient * gradient
    fix_first = 1.0 - beta_first**STEP
    fix_second = 1.0 - beta_second**STEP
    update_step = (
        first_new / fix_first / (jnp.sqrt(second_new / fix_second) + eps_adam)
        + weight_decay * master
    )
    master_new = master - step_rate * update_step
    return (master_new, first_new, second_new)


def unit_columns(full_in, full_out, full_up, full_down):
    parts = [full_in[:, 2 * COL * (u % 3) + COL * (u // 3) :][:, :COL] for u in range(6)]
    for full in (full_out, full_up, full_down):
        parts += [full[:, :COL], full[:, COL:]]
    return jnp.stack(parts)


def by_matrix(units):
    join = lambda *at: jnp.concatenate([units[i] for i in at], 1)
    return join(6, 9, 7, 10, 8, 11), join(4, 5), join(2, 3), join(0, 1)


def shards(
    inputs,
    segments,
    starts,
    out_grad,
    proj_in,
    proj_out,
    up_proj,
    down_proj,
    gains_biases,
    first_in,
    first_out,
    first_up,
    first_down,
    first_small,
    second_in,
    second_out,
    second_up,
    second_down,
    second_small,
):
    axes = ("wide", "narrow")
    wide, narrow = lax.axis_size("wide"), lax.axis_size("narrow")
    tokens, width = inputs.shape
    share = gains_biases.shape[0]
    me = lax.axis_index("wide") * narrow + lax.axis_index("narrow")
    rows = width // wide
    joined = narrow == 2 and wide % 4 == 0 and rows % 16 == 0 and share == 160
    layers = wide // 4 if joined else 0
    seg = segments.reshape(tokens // GROUP, GROUP).astype(F32)
    start = starts.reshape(tokens // TOK, TOK).astype(F32)
    rope = jnp.asarray(rope_tables())
    small_low = lax.reduce_precision(gains_biases, 8, 7)
    if joined:
        shift = lax.rem(share * me, 128)
        window = lax.dynamic_update_slice(jnp.zeros((256,), F32), small_low, (shift,)).reshape(2, 1, 128)
        *kept, weights, vec = forward(layers, rows, inputs, out_grad, seg, start, rope, (proj_in, proj_out, up_proj, down_proj, window))
    else:
        gathered = [lax.all_gather(m.astype(BF), axes, axis=0, tiled=True) for m in (proj_in, proj_out, up_proj, down_proj)]
        weights = unit_columns(*gathered)
        vec = lax.all_gather(small_low, axes, axis=0, tiled=True).reshape(4, width)
        vec = jnp.pad(vec, ((0, 4), (0, 0)))
        kept = forward(layers, rows, inputs, out_grad, seg, start, rope, (weights, vec))
    block_out, turned, qkv, att, r1, slope, e2, stats, sums = kept
    made = backward(layers, rows, inputs, out_grad, start, rope, vec, turned, qkv, att, r1, slope, e2, stats, sums, weights)
    input_grad = made[0]
    if joined:
        shard_in, shard_out, shard_up, shard_down = by_matrix(made[1])
        shard_small = lax.dynamic_slice(made[2].reshape(256), (shift,), (share,))
        grad_norm = made[3][0, 0]
    else:
        full_grads = [m.astype(F32) for m in by_matrix(made[1])]
        scatter = lambda m: lax.psum_scatter(m, axes, scatter_dimension=0, tiled=True)
        shard_in, shard_out, shard_up, shard_down = (scatter(m) for m in full_grads)
        shard_small = scatter(jnp.concatenate([made[2][3], made[2][2], made[2][1], made[2][0]]))
        squares = sum(jnp.sum(m * m) for m in (shard_in, shard_out, shard_up, shard_down, shard_small))
        grad_norm = jnp.sqrt(lax.psum(squares, axes))
    clip_scale = jnp.minimum(1.0, clip_limit / (grad_norm + 1e-06))
    news = [
        adam_update(proj_in, shard_in, first_in, second_in, clip_scale, decay_rate, learn_rate),
        adam_update(proj_out, shard_out, first_out, second_out, clip_scale, decay_rate, learn_rate),
        adam_update(up_proj, shard_up, first_up, second_up, clip_scale, decay_rate, learn_rate),
        adam_update(down_proj, shard_down, first_down, second_down, clip_scale, decay_rate, learn_rate),
        adam_update(gains_biases, shard_small, first_small, second_small, clip_scale, 0.0, small_rate),
    ]
    return (
        block_out,
        input_grad,
        grad_norm,
        *(new[0] for new in news),
        *(new[1] for new in news),
        *(new[2] for new in news),
        *(new[0].astype(BF) for new in news),
    )


def solution(mesh):
    split, flat = P(("wide", "narrow"), None), P(("wide", "narrow"))
    state = (split, split, split, split, flat)
    return jax.shard_map(
        shards,
        mesh=mesh,
        in_specs=(split,) * 4 + state * 3,
        out_specs=(split, split, P()) + state * 4,
        check_vma=False,
    )
```

```python
import functools
import math

import jax
import jax.numpy as jnp
import numpy as np
from jax import lax
from jax.experimental import pallas as pl
from jax.experimental.pallas import tpu as pltpu
from jax.sharding import PartitionSpec as P

HEADS = 16
HEAD_DIM = 80
STEP = 5
PATCHES = 16

eps_norm = 1e-05
eps_stat = 1e-05
rope_base = 10000.0
clip_limit = 256.0
learn_rate = 0.03
small_rate = 0.4
decay_rate = 0.1
beta_first = 0.9
beta_second = 0.999
eps_adam = 1e-08

BF = jnp.bfloat16
F32 = jnp.float32
MESH = pl.DeviceIdType.MESH

COL = 640
UNITS = 12
STAGES = 6
SPAN = 256
GROUP = 128
TOK = 256
WIDE_TOK = 512
VMEM_LIMIT = 64 << 20


def lanes(ref_cols):
    return lax.broadcasted_iota(jnp.int32, (1, ref_cols), 1)


def nn(left_in, right_in):
    return lax.dot_general(
        left_in, right_in, (((1,), (0,)), ((), ())), preferred_element_type=F32
    )


def nt(left_in, right_in):
    return lax.dot_general(
        left_in, right_in, (((1,), (1,)), ((), ())), preferred_element_type=F32
    )


def unit_cols(side):
    return pl.ds(pl.multiple_of(COL * side, 128), COL)


def rope_tables():
    half = HEAD_DIM // 2
    inverse = np.float32(rope_base) ** (-np.arange(half, dtype=np.float32) * np.float32(2.0) / np.float32(HEAD_DIM))
    angles = np.arange(PATCHES, dtype=np.float32)[:, None] * inverse.astype(np.float32)[None, :]
    cosine, sine = np.cos(angles), np.sin(angles)
    zero = np.zeros_like(sine)
    heads = COL // HEAD_DIM
    full = [
        np.tile(np.concatenate(pair, 1), (1, heads))
        for pair in ((cosine, cosine), (-sine, zero), (zero, sine))
    ]
    return np.stack(full).astype(np.float32)


def rotate(values_in, table, sign):
    rows = values_in.shape[0]
    ahead = pltpu.roll(values_in, COL - HEAD_DIM // 2, 1)
    behind = pltpu.roll(values_in, HEAD_DIM // 2, 1)
    cube = (rows // PATCHES, PATCHES, COL)
    turn = ahead.reshape(cube) * table[1] + behind.reshape(cube) * table[2]
    straight = values_in.reshape(cube) * table[0]
    return (straight + sign * turn).reshape(rows, COL)


def eye(size):
    row = lax.broadcasted_iota(jnp.int32, (size, size), 0)
    col = lax.broadcasted_iota(jnp.int32, (size, size), 1)
    return row == col


def to_column(row_in, same):
    return jnp.sum(jnp.where(same, row_in, 0.0), 1, keepdims=True)


def to_row(column_in, same):
    return jnp.sum(jnp.where(same, column_in, 0.0), 0, keepdims=True)


def per_token(table):
    rows = table.shape[0]
    size = rows * PATCHES
    wide = jnp.broadcast_to(table.astype(F32)[:, None, :], (rows, PATCHES, PATCHES)).reshape(size, PATCHES)
    patch = lax.rem(lax.broadcasted_iota(jnp.int32, (size, PATCHES), 0), PATCHES)
    hit = lax.broadcasted_iota(jnp.int32, (size, PATCHES), 1) == patch
    return jnp.sum(jnp.where(hit, wide, 0.0), 1, keepdims=True)


def context_mask(start_table):
    start_col = per_token(start_table).astype(jnp.int32)
    size = start_col.shape[0]
    row = lax.broadcasted_iota(jnp.int32, (size, size), 0)
    col = lax.broadcasted_iota(jnp.int32, (size, size), 1)
    return col == lax.div(row, PATCHES) * PATCHES + start_col


def pair_masks(pair):
    lane = lanes(SPAN)
    low = 160 * pair - 128 * (160 * pair // 128)
    return (
        (lane >= low) & (lane < low + HEAD_DIM),
        (lane >= low + HEAD_DIM) & (lane < low + 2 * HEAD_DIM),
    )


def both_heads(window, masks):
    zero = jnp.zeros_like(window)
    return jnp.concatenate([jnp.where(masks[0], window, zero), jnp.where(masks[1], window, zero)], 0)


def turn_pair(pair_in):
    return jnp.concatenate([pair_in[:, :GROUP].T, pair_in[:, GROUP:].T], 1)


def attention_bias(seg_table):
    row = lax.broadcasted_iota(jnp.int32, (GROUP, GROUP), 0)
    col = lax.broadcasted_iota(jnp.int32, (GROUP, GROUP), 1)
    seg_col = per_token(seg_table)
    seg_row = to_row(seg_col, row == col)
    allowed = (lax.div(row, PATCHES) == lax.div(col, PATCHES)) & (row <= col) & (seg_col == seg_row)
    bias = jnp.where(allowed, 0.0, -1e30)
    return jnp.concatenate([bias, bias], 1)


def head_window(qkv, unit, rows, pair):
    low = COL * (unit % 2) + 128 * (160 * pair // 128)
    return qkv[unit // 2, rows, low : low + SPAN]


def spread_windows(parts):
    tiles = []
    for tile in range(5):
        total = None
        for pair in (tile - 1, tile):
            if 0 <= pair < 4:
                piece = parts[pair][:, 128 * (tile - pair) : 128 * (tile - pair) + 128]
                total = piece if total is None else total + piece
        tiles.append(total)
    return jnp.concatenate(tiles, 1)


class Forward:
    def __init__(self, weight, refs):
        self.weight = weight
        (self.xv, self.dyv, self.seg, self.start, self.vec, self.rope, self.h1, self.tt, self.qkv, self.att,
         self.mix, self.r1, self.dg, self.stats, self.bsum) = refs
        self.tokens = self.xv.shape[0]
        self.width = self.xv.shape[1]

    def blocks(self, body, low=0, high=None):
        def step(i, carry):
            body(pl.multiple_of(i * TOK, TOK), i)
            return carry
        lax.fori_loop(low, self.tokens // TOK if high is None else high, step, 0)

    def norms(self, low, high):
        width = self.width
        gain = self.vec[0:1, :]

        def body(at, i):
            rows = pl.ds(at, TOK)
            same = eye(TOK)
            x = self.xv[rows, :].astype(F32)
            mean = jnp.sum(x, 1, keepdims=True) * (1.0 / width)
            off = x - mean
            spread = jnp.sqrt(jnp.sum(off * off, 1, keepdims=True) * (1.0 / width) + eps_stat)
            mask = context_mask(self.start[pl.ds(i * (TOK // PATCHES), TOK // PATCHES), :])
            mu = jnp.sum(jnp.where(mask, to_row(mean, same), 0.0), 1, keepdims=True)
            sigma = jnp.sum(jnp.where(mask, to_row(spread, same), 0.0), 1, keepdims=True)
            z = (x - mu) / sigma
            scale = lax.rsqrt(jnp.sum(z * z, 1, keepdims=True) * (1.0 / width) + eps_norm)
            h1 = (z * scale * gain).astype(BF)
            self.h1[rows, :] = h1
            self.tt[0, :, rows] = h1.T
            dy = self.dyv[rows, :].astype(F32)
            low = (dy * sigma).astype(BF)
            self.dyv[rows, :] = low
            self.bsum[0:1, :] += jnp.sum(low.astype(F32), 0, keepdims=True)
            self.stats[rows, 0:1] = mu
            self.stats[rows, 1:2] = sigma
            self.stats[rows, 2:3] = mean
            self.stats[rows, 3:4] = spread
            self.stats[rows, 4:5] = scale
            self.stats[rows, 6:7] = jnp.sum(dy, 1, keepdims=True)

        self.blocks(body, low, high)

    def project(self, stage):
        def step(i, carry):
            rows = pl.ds(pl.multiple_of(i * WIDE_TOK, WIDE_TOK), WIDE_TOK)
            made = nn(self.h1[rows, :], self.weight(stage))
            for side in range(2):
                cols = slice(COL * side, COL * (side + 1))
                part = made[:, cols]
                if (2 * stage + side) % 3 < 2:
                    part = rotate(part, self.rope, 1.0)
                self.qkv[stage, rows, cols] = part.astype(BF)
            return carry

        lax.fori_loop(0, self.tokens // WIDE_TOK, step, 0)

    def attend(self, half, low=0, high=None):
        scale = 1.0 / math.sqrt(HEAD_DIM)

        def step(g, carry):
            rows = pl.ds(pl.multiple_of(g * GROUP, GROUP), GROUP)
            bias = attention_bias(self.seg[pl.ds(g * (GROUP // PATCHES), GROUP // PATCHES), :])
            look = lambda kind, pair: head_window(self.qkv, 3 * half + kind, rows, pair)
            scores = [
                nt(look(1, pair), both_heads(look(0, pair), pair_masks(pair)))
                for pair in range(4)
            ]
            probs = []
            for pair in range(4):
                own = scores[pair] * scale + bias
                expo = jnp.exp(own - jnp.max(own, 0, keepdims=True))
                prob = (expo * (1.0 / jnp.sum(expo, 0, keepdims=True))).astype(BF)
                self.att[half, rows, SPAN * pair : SPAN * (pair + 1)] = prob
                probs.append(prob)
            parts = [
                nn(turn_pair(probs[pair]), both_heads(look(2, pair), pair_masks(pair)))
                for pair in range(4)
            ]
            self.mix[rows, COL * half : COL * (half + 1)] = spread_windows(parts).astype(BF)
            return carry

        lax.fori_loop(low, self.tokens // GROUP if high is None else high, step, 0)

    def mix_turned(self, slot):
        def body(at, i):
            rows = pl.ds(at, TOK)
            self.tt[slot, :, rows] = self.mix[rows, :].T

        self.blocks(body)

    def residual(self, slot):
        width = self.width
        gain = self.vec[1:2, :]

        def body(at, i):
            rows = pl.ds(at, TOK)
            mix = self.mix[rows, :]
            made = nn(mix, self.weight(3))
            z = (self.xv[rows, :].astype(F32) - self.stats[rows, 0:1]) / self.stats[rows, 1:2]
            r1 = z + made
            scale = lax.rsqrt(jnp.sum(r1 * r1, 1, keepdims=True) * (1.0 / width) + eps_norm)
            self.stats[rows, 5:6] = scale
            self.r1[rows, :] = r1
            h2 = (r1 * scale * gain).astype(BF)
            self.h1[rows, :] = h2
            self.tt[slot, :, rows] = h2.T

        self.blocks(body)

    def hidden(self, slot):
        bias = self.vec[2:3, :]
        c0 = math.sqrt(2.0 / math.pi)

        def body(at, i):
            rows = pl.ds(at, TOK)
            made = nn(self.h1[rows, :], self.weight(4))
            for half in range(2):
                cols = slice(COL * half, COL * (half + 1))
                u = made[:, cols] + bias[:, cols]
                square = u * u
                bend = jnp.tanh(c0 * (u + 0.044715 * u * square))
                act = (0.5 * u * (1.0 + bend)).astype(BF)
                slope = 0.5 * (1.0 + bend) + (0.5 * c0) * u * (1.0 - bend * bend) * (1.0 + (3 * 0.044715) * square)
                self.dg[rows, cols] = slope.astype(BF)
                self.mix[rows, cols] = act
                self.tt[slot, cols, rows] = act.T

        self.blocks(body)

    def chunk(self, i):
        per = self.tokens // TOK
        return self.qkv.at[lax.div(i, per), pl.ds(pl.multiple_of(TOK * lax.rem(i, per), TOK), TOK), :]

    def down_grad(self, left):
        def step(i, carry):
            rows = pl.ds(pl.multiple_of(i * TOK, TOK), TOK)
            self.chunk(i)[...] = nn(self.tt[left, rows, :], self.dyv[...]).astype(BF)
            return carry
        lax.fori_loop(0, self.width // TOK, step, 0)


class Backward:
    def __init__(self, refs):
        (self.wbuf, self.part, self.lt, self.ea, self.eb, self.qkv, self.att, self.vec, self.rope,
         self.stats, self.bsum, self.start, self.rblk, self.bblk) = refs
        self.tokens, self.width = self.ea.shape

    def blocks(self, body, low=0, high=None):
        def step(i, carry):
            body(pl.multiple_of(i * TOK, TOK), i)
            return carry
        lax.fori_loop(low, self.tokens // TOK if high is None else high, step, 0)

    def weight(self, slot):
        return self.wbuf[slot].reshape(self.width, self.width)

    def weight_grad(self, slot, left, right):
        part = self.part.at[slot]
        if len(part.shape) == 4:
            tall = 2 * part.shape[1] * part.shape[2]
            def step(i, carry):
                rows = pl.ds(pl.multiple_of(i * tall, 16), tall)
                for low in range(0, self.width, 512):
                    cols = slice(low, min(low + 512, self.width))
                    made = nn(self.lt[left, rows, :], right(cols))
                    part[pl.ds(2 * i, 2), :, :, cols] = made.astype(BF).reshape((2,) + part.shape[1:3] + (made.shape[1],))
                return carry
        else:
            tall = TOK
            def step(i, carry):
                rows = pl.ds(pl.multiple_of(i * tall, tall), tall)
                part[rows, :] = nn(self.lt[left, rows, :], right(slice(None))).astype(BF)
                return carry
        lax.fori_loop(0, self.width // tall, step, 0)

    def hidden(self, slot):
        def body(at, i):
            rows = pl.ds(at, TOK)
            low = (nt(self.ea[rows, :], self.weight(slot)) * self.eb[rows, :].astype(F32)).astype(BF)
            self.eb[rows, :] = low
            self.bsum[1:2, :] += jnp.sum(low.astype(F32), 0, keepdims=True)

        self.blocks(body)

    def stream(self, body, loads, low=0, high=None):
        count = self.tokens // TOK
        high = count if high is None else high

        def copies(i):
            slot = lax.rem(i, 2)
            rows = pl.ds(pl.multiple_of(i * TOK, TOK), TOK)
            return [pltpu.make_async_copy(src.at[rows, :], buf.at[slot], sem.at[slot]) for src, buf, sem in loads]

        if low == 0:
            for cp in copies(0):
                cp.start()

        def inner(at, i):
            @pl.when(i + 1 < count)
            def _():
                for cp in copies(i + 1):
                    cp.start()
            for cp in copies(i):
                cp.wait()
            body(at, i, lax.rem(i, 2))

        self.blocks(inner, low, high)

    def result(self, slot, loads, out, out_sem, low, high):
        bias = self.vec[3:4, :]
        count = self.tokens // TOK

        def copy(i):
            turn = lax.rem(i, 2)
            return pltpu.make_async_copy(self.rblk.at[turn], out.at[pl.ds(pl.multiple_of(i * TOK, TOK), TOK), :], out_sem.at[turn])

        def fetch(i):
            turn = lax.rem(i, 2)
            rows = pl.ds(pl.multiple_of(i * TOK, TOK), TOK)
            return [pltpu.make_async_copy(src.at[rows, :], buf.at[turn], sem.at[turn]) for src, buf, sem in loads]

        if low == 0:
            for cp in fetch(0):
                cp.start()

        def body(at, i):
            rows = pl.ds(at, TOK)
            turn = lax.rem(i, 2)

            @pl.when(i >= 1)
            def _():
                copy(i - 1).wait()

            @pl.when(i + 1 < count)
            def _():
                for cp in fetch(i + 1):
                    cp.start()

            act = self.eb[rows, :]
            made = nn(act, self.weight(slot))
            for cp in fetch(i):
                cp.wait()
            r2 = self.rblk[turn] + (made + bias)
            self.rblk[turn] = r2 * self.stats[rows, 1:2] + self.stats[rows, 0:1]
            copy(i).start()
            self.stats[rows, 7:8] = jnp.sum(self.bblk[turn].astype(F32) * r2, 1, keepdims=True)

        self.blocks(body, low, high)
        if high == count:
            copy(count - 1).wait()

    def second_norm(self, slot, loads, hold, low, high):
        width = self.width
        gain = self.vec[1:2, :]

        def body(at, i, turn):
            hold[...] = nt(self.eb[pl.ds(at, TOK), :], self.weight(slot))

            def step(c, carry):
                inside = pl.multiple_of(c * GROUP, GROUP)
                rows, local = pl.ds(pl.multiple_of(at + inside, GROUP), GROUP), pl.ds(inside, GROUP)
                dh2 = hold[local, :]
                scale = self.stats[rows, 5:6]
                n2 = self.rblk[turn, local, :] * scale
                self.bsum[2:3, :] += jnp.sum(dh2 * n2, 0, keepdims=True)
                dn = dh2 * gain
                inner = jnp.sum(dn * n2, 1, keepdims=True) * (1.0 / width)
                dr1 = self.bblk[turn, local, :].astype(F32) * self.stats[rows, 1:2] + scale * (dn - n2 * inner)
                self.ea[rows, :] = dr1.astype(BF)
                return carry
            lax.fori_loop(0, TOK // GROUP, step, 0)

        self.stream(body, loads, low, high)

    def mixed(self, slot):
        def body(at, i):
            rows = pl.ds(at, TOK)
            self.eb[rows, :] = nt(self.ea[rows, :], self.weight(slot)).astype(BF)

        self.blocks(body)

    def attend(self, half, low=0, high=None):
        scale = 1.0 / math.sqrt(HEAD_DIM)

        def step(g, carry):
            rows = pl.ds(pl.multiple_of(g * GROUP, GROUP), GROUP)
            starts = [128 * (160 * pair // 128) for pair in range(4)]
            look = lambda kind, pair: head_window(self.qkv, 3 * half + kind, rows, pair)
            masks = [pair_masks(pair) for pair in range(4)]
            dmix = [both_heads(self.eb[rows, pl.ds(COL * half + starts[i], SPAN)], masks[i]) for i in range(4)]
            probs = [self.att[rows, SPAN * i : SPAN * (i + 1)] for i in range(4)]
            das = [nt(look(2, i), dmix[i]) for i in range(4)]
            dss = []
            for i in range(4):
                p32 = probs[i].astype(F32)
                weighed = p32 * das[i]
                dss.append((weighed - p32 * jnp.sum(weighed, 0, keepdims=True)).astype(BF))
            dvs = [nn(probs[i], dmix[i]) for i in range(4)]
            dks = [nn(dss[i], both_heads(look(0, i), masks[i])) for i in range(4)]
            dqs = [nn(turn_pair(dss[i]), both_heads(look(1, i), masks[i])) for i in range(4)]
            dq = rotate(spread_windows(dqs) * scale, self.rope, -1.0)
            dk = rotate(spread_windows(dks) * scale, self.rope, -1.0)
            for kind, made in enumerate((dq, dk, spread_windows(dvs))):
                unit = 3 * half + kind
                self.qkv[unit // 2, rows, COL * (unit % 2) : COL * (unit % 2 + 1)] = made.astype(BF)
            return carry

        lax.fori_loop(low, self.tokens // GROUP if high is None else high, step, 0)

    def first_norm(self, slots, loads, out, out_sem, turns, low, high):
        width = self.width
        gain = self.vec[0:1, :]
        count = self.tokens // TOK

        def copy(i):
            slot = lax.rem(i, 2)
            return pltpu.make_async_copy(turns.at[slot], out.at[pl.ds(pl.multiple_of(i * TOK, TOK), TOK), :], out_sem.at[slot])

        def piece(at, inside, turn):
            rows = pl.ds(pl.multiple_of(at + inside, GROUP), GROUP)
            local = pl.ds(inside, GROUP)
            same = eye(GROUP)
            dh1 = turns[turn, local, :]
            mu, sigma = self.stats[rows, 0:1], self.stats[rows, 1:2]
            mean, spread = self.stats[rows, 2:3], self.stats[rows, 3:4]
            scale = self.stats[rows, 4:5]
            inv = 1.0 / sigma
            x = self.bblk[turn, local, :].astype(F32)
            z = (x - mu) * inv
            n1 = z * scale
            self.bsum[3:4, :] += jnp.sum(dh1 * n1, 0, keepdims=True)
            dn = dh1 * gain
            inner = jnp.sum(dn * n1, 1, keepdims=True) * (1.0 / width)
            dz = scale * (dn - n1 * inner) + self.ea[rows, :].astype(F32)
            dmu = self.stats[rows, 6:7] - jnp.sum(dz, 1, keepdims=True) * inv
            dsigma = self.stats[rows, 7:8] - jnp.sum(dz * z, 1, keepdims=True) * inv
            per = GROUP // PATCHES
            mask = context_mask(self.start[pl.ds(pl.multiple_of(lax.div(at + inside, PATCHES), per), per), :])
            dmean = to_column(jnp.sum(jnp.where(mask, dmu, 0.0), 0, keepdims=True), same)
            dspread = to_column(jnp.sum(jnp.where(mask, dsigma, 0.0), 0, keepdims=True), same)
            turns[turn, local, :] = dz * inv + (dmean * (1.0 / width) + (x - mean) * (dspread * (1.0 / width) / spread))

        def body(at, i, turn):
            rows = pl.ds(at, TOK)
            dh1 = nt(self.qkv[0, rows, :], self.weight(slots[0]))
            for stage in (1, 2):
                dh1 += nt(self.qkv[stage, rows, :], self.weight(slots[stage]))

            @pl.when(i >= 2)
            def _():
                copy(i - 2).wait()

            turns[turn] = dh1

            def step(c, carry):
                piece(at, pl.multiple_of(c * GROUP, GROUP), turn)
                return carry
            lax.fori_loop(0, TOK // GROUP, step, 0)
            copy(i).start()

        self.stream(body, loads, low, high)
        if high == count:
            for i in range(max(count - 2, 0), count):
                copy(i).wait()


class Spot:
    def __init__(self, layers):
        self.layers = layers
        wide, self.c = lax.axis_index("wide"), lax.axis_index("narrow")
        self.z, self.p = lax.div(wide, 4), lax.rem(wide, 4)
        self.px = self.p + 1 - 2 * lax.rem(self.p, 2)
        self.py = lax.rem(self.p + 2, 4)
        self.pd = 3 - self.p
        self.me = 2 * wide + self.c
        self.count = 8 * layers
        self.sibling = self.device(self.z, self.p, 1 - self.c)
        self.across_x = self.device(self.z, self.px, self.c)
        self.across_y = self.device(self.z, self.py, self.c)
        self.pa = jnp.where(self.c == 0, self.px, self.py)
        self.pb = jnp.where(self.c == 0, self.py, self.px)
        self.across_a = self.device(self.z, self.pa, self.c)
        self.across_b = self.device(self.z, self.pb, self.c)

    def device(self, z, p, c):
        return (z * 4 + p, c)

    def layer(self, k):
        return lax.rem(self.z + k, self.layers)

    def in_layer(self, z):
        return self.device(z, self.p, self.c)

    def others(self, body):
        def step(k, carry):
            other = lax.rem(self.me + k, self.count)
            body(k, other, (lax.div(other, 2), lax.rem(other, 2)))
            return carry
        lax.fori_loop(1, self.count, step, 0)

    def meet(self):
        door = pltpu.get_barrier_semaphore()
        self.others(lambda k, other, device: pl.semaphore_signal(door, 1, device_id=device, device_id_type=MESH))
        pl.semaphore_wait(door, self.count - 1)


def remote(src, dst, send, recv, device):
    return pltpu.make_async_remote_copy(src, dst, send, recv, device_id=device, device_id_type=MESH)


class Posted:
    def __init__(self):
        self.groups = {}

    def go(self, key, *args):
        copy = remote(*args)
        copy.start()
        self.groups.setdefault(key, []).append(copy)

    def sent(self, key):
        for copy in self.groups.pop(key, []):
            copy.wait_send()

    def all_sent(self):
        for key in list(self.groups):
            self.sent(key)


class Gather(Posted):
    @staticmethod
    def scratch(layers, rows):
        D = pltpu.SemaphoreType.DMA
        n = STAGES
        return [pltpu.VMEM((n, rows, COL), F32), D((n,)), D((n,)), D((n,)), D((n, layers)), D((n, layers)),
                D((n, layers, 2)), D((n, layers, 2)), D((n, 2)), D((n, 2)), D((n, 4)), D((n, 4))]

    def __init__(self, spot, full, owned, refs):
        super().__init__()
        self.spot, self.full, self.owned = spot, full, owned
        (self.desk, self.local, self.es, self.er, self.zs, self.zr, self.ps, self.pr, self.ds, self.dr, self.ss, self.sr) = refs
        self.rows = self.desk.shape[1]
        self.half = self.rows // 2
        self.cut = self.rows // 32 * 16 + (16 if self.rows % 32 else 0)

    def line(self, j, p, side=None):
        return self.full.at[j, :, p, :, unit_cols(self.spot.c if side is None else side)]

    def block(self, j, z, p):
        return self.full.at[j, z, p, :, unit_cols(self.spot.c)]

    def shard(self, j, unit):
        if j < 3:
            column = 2 * COL * lax.rem(unit, 3) + COL * lax.div(unit, 3)
            return self.owned[0].at[:, pl.ds(pl.multiple_of(column, 128), COL)]
        return self.owned[j - 2].at[:, pl.ds(pl.multiple_of(COL * lax.rem(unit, 2), 128), COL)]

    def desk_rows(self, j, core):
        return self.desk.at[j, pl.ds(pl.multiple_of(self.half * core, 8), self.half), :]

    def prepare(self, j):
        c = self.spot.c
        place_at = self.desk_rows(j, c)
        pltpu.make_async_copy(self.shard(j, 2 * j + c), place_at, self.local.at[j]).start()
        self.go(j, self.shard(j, 2 * j + 1 - c), place_at, self.es.at[j], self.er.at[j], self.spot.sibling)

    def across(self, j, k):
        s = self.spot
        block = self.block(j, s.layer(s.layers - k), s.p)
        self.go(j, block, block, self.ps.at[j, k, 0], self.pr.at[j, k, 0], s.across_x)
        self.go(j, block, block, self.ps.at[j, k, 1], self.pr.at[j, k, 1], s.across_y)

    def e1(self, j):
        s = self.spot
        mine, other = self.desk_rows(j, s.c), self.desk_rows(j, 1 - s.c)
        pltpu.make_async_copy(mine, mine, self.local.at[j]).wait()
        remote(other, other, self.es.at[j], self.er.at[j], s.sibling).wait_recv()
        self.block(j, s.z, s.p)[...] = self.desk[j].astype(BF)
        self.across(j, 0)

    def e0(self, j):
        s = self.spot
        block = self.block(j, s.z, s.p)
        for k in range(1, s.layers):
            self.go(j, block, block, self.zs.at[j, k], self.zr.at[j, k], s.in_layer(s.layer(k)))

    def e2(self, j):
        s = self.spot
        for k in range(1, s.layers):
            z = s.layer(s.layers - k)
            block = self.block(j, z, s.p)
            remote(block, block, self.zs.at[j, k], self.zr.at[j, k], s.in_layer(z)).wait_recv()
            self.across(j, k)
        self.to_sibling(j, 0, s.p)

    def to_sibling(self, j, i, p):
        line = self.line(j, p)
        self.go(j, line, line, self.ss.at[j, i], self.sr.at[j, i], self.spot.sibling)

    def corner(self, j, p, top):
        rows = pl.ds(0, self.cut) if top else pl.ds(self.cut, self.rows - self.cut)
        return self.full.at[j, :, p, rows, unit_cols(self.spot.c)]

    def e3(self, j):
        s = self.spot
        for k in range(s.layers):
            z = s.layer(s.layers - k)
            for i, p in ((0, s.px), (1, s.py)):
                block = self.block(j, z, p)
                remote(block, block, self.ps.at[j, k, i], self.pr.at[j, k, i], s.across_x).wait_recv()
        top, rest = self.corner(j, s.pa, True), self.corner(j, s.pb, False)
        self.go(j, top, top, self.ds.at[j, 0], self.dr.at[j, 0], s.across_b)
        self.go(j, rest, rest, self.ds.at[j, 1], self.dr.at[j, 1], s.across_a)
        self.to_sibling(j, 1, s.px)
        self.to_sibling(j, 2, s.py)

    def e4(self, j):
        s = self.spot
        top, rest = self.corner(j, s.pd, True), self.corner(j, s.pd, False)
        remote(top, top, self.ds.at[j, 0], self.dr.at[j, 0], s.across_y).wait_recv()
        remote(rest, rest, self.ds.at[j, 1], self.dr.at[j, 1], s.across_x).wait_recv()
        self.to_sibling(j, 3, s.pd)

    def e5(self, j):
        s = self.spot
        for i, p in enumerate((s.p, s.px, s.py, s.pd)):
            line = self.line(j, p, 1 - s.c)
            remote(line, line, self.ss.at[j, i], self.sr.at[j, i], s.sibling).wait_recv()


class Scatter(Posted):
    SLOTS = 3

    @staticmethod
    def scratch(layers, rows):
        D, V = pltpu.SemaphoreType.DMA, pltpu.VMEM
        n, m = STAGES, Scatter.SLOTS
        return [V((n - 1, layers, 4, rows, COL), BF), V((m, layers, rows, COL), BF), V((m, 2, layers, rows, COL), BF),
                V((m, layers, rows, COL), BF), V((m, rows, COL), F32), V((UNITS, rows // 2, COL), F32),
                D((n,)), D((n,)), D((n, 2)), D((n, 2)), D((n, 2)), D((n, 2)), D((n, layers)), D((n, layers)), D((n,)), D((n,))]

    def __init__(self, spot, part, refs):
        super().__init__()
        self.spot, self.part = spot, part
        (self.sums, self.dg, self.pl, self.zb, self.fin, self.res,
         self.ss, self.sr, self.ds, self.dr, self.ps, self.pr, self.zs, self.zr, self.fs, self.fr) = refs
        self.rows = self.dg.shape[2]
        self.half = self.rows // 2
        self.cut = self.rows // 32 * 16 + (16 if self.rows % 32 else 0)

    def sum_at(self, j):
        return self.sums.at[j % (STAGES - 1)]

    def each_layer(self, body):
        def step(z, carry):
            body(z)
            return carry
        lax.fori_loop(0, self.spot.layers, step, 0)

    def f1(self, j):
        s = self.spot
        self.go(("f1", j), self.part.at[j % 2, :, :, :, unit_cols(1 - s.c)], self.sum_at(j), self.ss.at[j], self.sr.at[j], s.sibling)

    def corners(self, j):
        s = self.spot
        total, slot = self.sum_at(j), j % self.SLOTS
        for i, (rows, device) in enumerate(((pl.ds(0, self.cut), s.across_b), (pl.ds(self.cut, self.rows - self.cut), s.across_a))):
            self.go(j, total.at[:, s.pd, rows, :], self.dg.at[slot, :, rows, :], self.ds.at[j, i], self.dr.at[j, i], device)

    def f2(self, j):
        s = self.spot
        own, total = self.part.at[j % 2], self.sum_at(j)
        remote(total, total, self.ss.at[j], self.sr.at[j], s.sibling).wait_recv()

        def add(p):
            def one(z):
                total[z, p] = total[z, p] + own[z, p, :, unit_cols(s.c)]
            self.each_layer(one)

        add(s.pd)
        self.corners(j)
        for p in (s.px, s.py, s.p):
            add(p)

    def f3(self, j):
        s = self.spot
        total, slot = self.sum_at(j), j % self.SLOTS
        for i, (low, size, p) in enumerate(((0, self.cut, s.pa), (self.cut, self.rows - self.cut, s.pb))):
            rows = pl.ds(low, size)
            came = self.dg.at[slot, :, rows, :]
            remote(came, came, self.ds.at[j, i], self.dr.at[j, i], s.across_y).wait_recv()

            def one(z):
                total[z, p, rows, :] = total[z, p, rows, :] + self.dg[slot, z, rows, :]
            self.each_layer(one)
        for i, (p, device) in enumerate(((s.px, s.across_x), (s.py, s.across_y))):
            self.go(j, total.at[:, p], self.pl.at[slot, i], self.ps.at[j, i], self.pr.at[j, i], device)

    def f4(self, j):
        s = self.spot
        total, slot = self.sum_at(j), j % self.SLOTS
        for i in range(2):
            came = self.pl.at[slot, i]
            remote(came, came, self.ps.at[j, i], self.pr.at[j, i], s.across_x).wait_recv()
        for k in [*range(1, s.layers), 0]:
            z = s.layer(k)
            total[z, s.p] = (total[z, s.p].astype(F32) + self.pl[slot, 0, z].astype(F32) + self.pl[slot, 1, z].astype(F32)).astype(BF)
            if k:
                self.go(j, total.at[z, s.p], self.zb.at[slot, k], self.zs.at[j, k], self.zr.at[j, k], s.in_layer(z))

    def f5(self, j):
        s = self.spot
        slot = j % self.SLOTS
        total = self.sums[j % (STAGES - 1), s.z, s.p].astype(F32)
        for k in range(1, s.layers):
            came = self.zb.at[slot, k]
            remote(came, came, self.zs.at[j, k], self.zr.at[j, k], s.across_x).wait_recv()
            total = total + self.zb[slot, k].astype(F32)
        self.sent(j)
        self.sent(("fin", j - self.SLOTS))
        self.fin[slot] = total
        mine, other = (pl.ds(pl.multiple_of(self.half * c, 8), self.half) for c in (s.c, 1 - s.c))
        self.res[2 * j + s.c] = self.fin[slot, mine, :]
        self.go(("fin", j), self.fin.at[slot, other, :], self.res.at[2 * j + s.c], self.fs.at[j], self.fr.at[j], s.sibling)

    def f6(self, j):
        s = self.spot
        came = self.res.at[2 * j + 1 - s.c]
        remote(came, came, self.fs.at[j], self.fr.at[j], s.sibling).wait_recv()


class Everyone(Posted):
    @staticmethod
    def scratch(count):
        D = pltpu.SemaphoreType.DMA
        return [D((count,)), D((count,))]

    def __init__(self, spot, board, refs):
        self.spot, self.board = spot, board
        self.send_sem, self.recv_sem = refs

    def post(self, source):
        s = self.spot
        def one(k, other, device):
            remote(source(other), self.board.at[s.me], self.send_sem.at[k], self.recv_sem.at[k], device).start()
        s.others(one)

    def collect(self, own):
        s = self.spot
        def one(k, other, device):
            came = self.board.at[lax.rem(s.me + s.count - k, s.count)]
            remote(came, came, self.send_sem.at[k], self.recv_sem.at[k], device).wait()
        s.others(one)
        self.board[s.me] = own


FORWARD_ORDER = (
    "e10", "e00", "e11", "e01", "e12", "e13", "e14", "e15", "v", "n0", "n1", "e20", "e02", "n2", "e21", "e30", "n3", "e22", "e03",
    "e31", "e40", "e32", "e23", "e04", "e41", "e50", "e05", "p0", "e51", "p1", "e24", "e42", "a0", "e33", "a1", "a2", "e52", "a3",
    "p2", "e34", "a4", "e25", "e43", "a5", "a6", "a7", "e53", "m", "e44", "r", "e54", "h", "e35", "g", "X", "e45", "Y", "e55",
)
BACKWARD_ORDER = (
    "h", "g1", "f30", "s", "f21", "g2", "f40", "f31", "m", "a0", "a1", "a2", "f22", "a3", "g3", "f32", "f50", "a4", "a5", "a6",
    "f41", "a7", "f23", "r0", "g4", "r1", "f33", "f42", "f51", "f24", "g5", "f52", "r2", "f43", "r3", "f34", "f25", "n03", "f53",
    "f44", "f35", "n34", "f45", "f54",
)


def place(kind, count):
    return [pl.BlockSpec(memory_space=kind)] * count


def load(src, dst, sem):
    copy = pltpu.make_async_copy(src, dst, sem)
    copy.start()
    return copy


def window_tile(per, owner):
    return lax.div(per * owner, 128)


def forward_kernel(layers, *refs):
    joined = layers > 0
    refs = list(refs)
    take = lambda n: [refs.pop(0) for _ in range(n)]
    x, dy, seg, start, rope = take(5)
    owned = take(5) if joined else take(2)
    turned, qkv_out, att_out, r1_out, dg_out, e2_out, act_out, stats_out, bsum_out, down_out = take(10)
    weights_out, vec_out = take(2) if joined else (None, None)
    full, xv, dyv, h1, tt, qkv, att, mix, r1, dg, stats, bsum, sem, dsem = take(14)
    fetch = [load(x, xv, sem.at[0]), load(dy, dyv, sem.at[1])]
    bsum[...] = jnp.zeros_like(bsum)
    if joined:
        spot = Spot(layers)
        board, canvas, vec, wsem, came, csend, crecv = take(7)
        everyone = Everyone(spot, board, take(2))
        gather = Gather(spot, full, owned[:4], refs)
        window = owned[4]
        weight = lambda j: full[j].reshape(h1.shape[1], h1.shape[1])
        spot.meet()
        for j in range(STAGES):
            gather.prepare(j)
        everyone.post(lambda other: window)
        canvas[...] = jnp.zeros_like(canvas)
    else:
        vec = owned[1]
        weight = lambda j: full[j]
        fetch.append(load(owned[0], full, sem.at[2]))
    f = Forward(weight, (xv, dyv, seg, start, vec, rope, h1, tt, qkv, att, mix, r1, dg, stats, bsum))
    blocks = f.tokens // TOK
    groups = f.tokens // GROUP
    outs = {}

    def vectors():
        everyone.collect(window[...])
        share = 4 * f.width // spot.count

        def put(owner, carry):
            canvas[pl.ds(window_tile(share, owner), 2)] += board[owner]
            return carry
        lax.fori_loop(0, spot.count, put, 0)
        tiles = f.width // 128
        for row in range(4):
            for tile in range(tiles):
                vec[row : row + 1, 128 * tile : 128 * (tile + 1)] = canvas[row * tiles + tile]

    def norm(i):
        if i == 0:
            fetch[0].wait()
            fetch[1].wait()
        f.norms(i * blocks // 4, (i + 1) * blocks // 4)
        if i == 3:
            outs["h1"] = load(tt.at[0], turned.at[0], sem.at[3])
            outs["e2"] = load(dyv, e2_out, sem.at[4])

    def attend(i):
        f.attend(i // 4, i % 4 * groups // 4, (i % 4 + 1) * groups // 4)

    def turn_mix():
        outs["qkv"] = load(qkv, qkv_out, sem.at[5])
        outs["att"] = load(att, att_out, sem.at[6])
        f.mix_turned(1)
        outs["o"] = load(tt.at[1], turned.at[1], sem.at[7])

    def residual():
        outs.pop("h1").wait()
        f.residual(0)
        outs["h2"] = load(tt.at[0], turned.at[2], sem.at[3])
        outs["r1"] = load(r1, r1_out, sem.at[8])

    def hidden():
        outs.pop("o").wait()
        f.hidden(1)
        outs["dg"] = load(dg, dg_out, sem.at[9])
        outs["act"] = load(mix, act_out, sem.at[7])

    def down_grad():
        outs.pop("qkv").wait()
        f.down_grad(1)

    down_chunks = f.width // TOK

    def exchange(i):
        return remote(f.chunk(i).at[:, unit_cols(1 - spot.c)], came.at[i], csend.at[i], crecv.at[i], spot.sibling)

    def give():
        for i in range(down_chunks):
            exchange(i).start()

    def receive():
        for i in range(down_chunks):
            exchange(i).wait()
            came[i] = came[i] + f.chunk(i)[:, unit_cols(spot.c)]
            outs["d", i] = load(came.at[i], down_out.at[i], dsem.at[i])

    steps = {"v": vectors, "n": norm, "p": f.project, "a": attend, "m": turn_mix, "r": residual, "h": hidden, "g": down_grad,
             "X": give, "Y": receive}
    if joined:
        for name in FORWARD_ORDER:
            if name in steps:
                steps[name]()
            elif name[0] == "e":
                j = int(name[2])
                getattr(gather, name[:2])(j)
                if name[1] == "5":
                    outs["w", j] = load(full.at[j], weights_out.at[j], wsem.at[j])
            else:
                steps[name[0]](int(name[1]))
    else:
        for i in range(4):
            norm(i)
        fetch[2].wait()
        for j in range(3):
            f.project(j)
        for i in range(8):
            attend(i)
        for name in "mrhg":
            steps[name]()
        for i in range(down_chunks):
            outs["d", i] = load(f.chunk(i), down_out.at[i], dsem.at[i])
    outs["stats"] = load(stats, stats_out, sem.at[10])
    outs["bsum"] = load(bsum, bsum_out, sem.at[11])
    if joined:
        outs["vec"] = load(vec, vec_out, sem.at[2])
    for copy in outs.values():
        copy.wait()
    if joined:
        gather.all_sent()


def forward(layers, rows, x, dy, seg, start, rope, owned):
    tokens, width = x.shape
    S = jax.ShapeDtypeStruct
    V = pltpu.VMEM
    D = pltpu.SemaphoreType.DMA
    joined = layers > 0
    shape = (STAGES, layers, 4, rows, width) if joined else (STAGES, width, width)
    chunks = width // TOK
    outs = [S((3, width, tokens), BF), S((3, tokens, width), BF), S((2, tokens, 4 * SPAN), BF),
            S((tokens, width), F32), S((tokens, width), BF), S((tokens, width), BF), S((tokens, width), BF), S((tokens, 128), F32), S((8, width), F32),
            S((chunks, TOK, COL if joined else width), BF)]
    scratch = [V(shape, BF), V((tokens, width), BF), V((tokens, width), BF), V((tokens, width), BF), V((2, width, tokens), BF),
               V((3, tokens, width), BF), V((2, tokens, 4 * SPAN), BF), V((tokens, width), BF), V((tokens, width), F32),
               V((tokens, width), BF), V((tokens, 128), F32), V((8, width), F32), D((12,)), D((chunks,))]
    if joined:
        outs += [S(shape, BF), S((8, width), F32)]
        count = 8 * layers
        scratch += [V((count, 2, 1, 128), F32), V((4 * width // 128 + 8, 1, 128), F32), V((8, width), F32), D((STAGES,)),
                    V((chunks, TOK, COL), BF), D((chunks,)), D((chunks,))]
        scratch += Everyone.scratch(count) + Gather.scratch(layers, rows)
    return pl.pallas_call(
        functools.partial(forward_kernel, layers),
        out_shape=outs,
        in_specs=place(pl.ANY, 2) + place(pltpu.VMEM, 3) + (place(pl.ANY, 4) if joined else place(pl.ANY, 1)) + place(pltpu.VMEM, 1),
        out_specs=place(pl.ANY, len(outs)),
        scratch_shapes=scratch,
        compiler_params=pltpu.CompilerParams(vmem_limit_bytes=VMEM_LIMIT, **(dict(collective_id=0, has_side_effects=True) if joined else {})),
        name="layer_forward",
    )(x, dy, seg, start, rope, *owned)


def backward_kernel(layers, *refs):
    joined = layers > 0
    refs = list(refs)
    take = lambda n: [refs.pop(0) for _ in range(n)]
    x, dy, start, rope, vec, turned, qkv_in, att_in, r1_in, dg_in, e2_in, act_in, stats_in, bsum_in, down_in, gw = take(16)
    out, dx_out, grad_out, small_out = take(4)
    norm_out = take(1)[0] if joined else None
    wbuf, part, lt, ea, eb, qkv, att, stats, bsum, rblk, bblk, hold, sem, ssem, osem, psem = take(16)

    def weights(j, slot, s):
        return load(gw.at[j], wbuf.at[slot], s)

    if joined:
        spot = Spot(layers)
        board, norms, sheet, note = take(4)
        small_talk = Everyone(spot, board, take(2))
        norm_talk = Everyone(spot, norms, take(2))
        scatter = Scatter(spot, part, refs)
        down = load(down_in, scatter.sum_at(0), psem.at[0])
    e = load(e2_in, ea, sem.at[1])
    w5 = weights(5, 0, sem.at[0])
    d = load(dg_in, eb, sem.at[3])
    bs = load(bsum_in, bsum, sem.at[5])
    s = load(stats_in, stats, sem.at[4])
    l2 = load(turned.at[2], lt.at[0], sem.at[2])
    w4 = weights(4, 1, sem.at[6])
    l1 = load(turned.at[1], lt.at[1], sem.at[7])
    w3 = weights(3, 2, sem.at[8])
    qk = load(qkv_in, qkv, sem.at[9])
    at = load(att_in.at[0], att, sem.at[10])
    b = Backward((wbuf, part, lt, ea, eb, qkv, att, vec, rope, stats, bsum, start, rblk, bblk))
    blocks = b.tokens // TOK
    groups = b.tokens // GROUP
    if joined:
        spot.meet()
        down.wait()
        scatter.corners(0)

    def spill(r):
        return pltpu.make_async_copy(part.at[r % 2], grad_out.at[r - 1], psem.at[r % 2])

    def grad(r):
        if r >= 3:
            if joined:
                scatter.sent(("f1", r - 2))
            else:
                spill(r - 2).wait()
        left, right = {1: (0, lambda cols: eb[:, cols]), 2: (1, lambda cols: ea[:, cols])}.get(r, (0, lambda cols: qkv[r - 3, :, cols]))
        for copy in waits.pop(r, []):
            copy.wait()
        b.weight_grad(r % 2, left, right)
        if joined:
            scatter.f1(r)
        else:
            spill(r).start()
        if r == 1:
            waits[3] = [load(turned.at[0], lt.at[0], sem.at[2])]

    waits = {1: [l2], 2: [l1], "w": []}
    loads = [(r1_in, rblk, ssem.at[0]), (dy, bblk, ssem.at[1])]

    def hidden():
        for copy in (w5, d, e, bs):
            copy.wait()
        b.hidden(0)

    def second_norm():
        w4.wait()
        s.wait()
        b.second_norm(1, loads, hold, 0, blocks)
        waits["w"].append(weights(0, 1, sem.at[6]))

    def mixed():
        w3.wait()
        b.mixed(2)
        waits["w"].append(weights(1, 2, sem.at[8]))
        qk.wait()

    def attend(i):
        if i == 0:
            at.wait()
        if i == 4:
            waits["a"].wait()
        b.attend(i // 4, i % 4 * groups // 4, (i % 4 + 1) * groups // 4)
        if i == 3:
            waits["a"] = load(att_in.at[1], att, sem.at[10])
        if i == 7:
            waits["act"] = load(act_in, eb, sem.at[3])

    def result(i):
        if i == 0:
            waits["act"].wait()
        b.result(0, loads, out, osem, i * blocks // 4, (i + 1) * blocks // 4)
        if i == 3:
            waits["w"].append(weights(2, 0, sem.at[0]))

    def first_norm(low, high):
        if low == 0:
            for copy in waits["w"]:
                copy.wait()
        b.first_norm((1, 2, 0), [(x, bblk, ssem.at[1])], dx_out, osem, rblk, low * blocks // 4, high * blocks // 4)

    for name in BACKWARD_ORDER:
        if name[0] == "f":
            if joined:
                getattr(scatter, name[:2])(int(name[2]))
        elif name[0] in "gar":
            {"g": grad, "a": attend, "r": result}[name[0]](int(name[1]))
        elif name[0] == "n":
            first_norm(int(name[1]), int(name[2]))
        else:
            {"h": hidden, "s": second_norm, "m": mixed}[name]()
    if not joined:
        fin = load(bsum, small_out, sem.at[5])
        for r in range(STAGES - 2, STAGES):
            spill(r).wait()
        fin.wait()
        return
    tiles = b.width // 128
    for row, source in enumerate((3, 2, 1, 0)):
        for tile in range(tiles):
            sheet[row * tiles + tile] = bsum[source : source + 1, 128 * tile : 128 * (tile + 1)]
    share = 4 * b.width // spot.count
    own = lambda owner: sheet.at[pl.ds(window_tile(share, owner), 2)]
    small_talk.post(own)
    small_talk.collect(sheet[pl.ds(window_tile(share, spot.me), 2)])

    def add(owner, carry):
        return carry + board[owner]
    total = lax.fori_loop(0, spot.count, add, jnp.zeros((2, 1, 128), F32))
    first = lax.rem(share * spot.me, 128)
    spots = lax.broadcasted_iota(jnp.int32, (2, 1, 128), 0) * 128 + lax.broadcasted_iota(jnp.int32, (2, 1, 128), 2)
    mine = jnp.where((spots >= first) & (spots < first + share), total, 0.0)
    small_out[...] = mine
    scatter.f5(STAGES - 1)
    for j in range(STAGES):
        scatter.f6(j)
    fin = load(scatter.res, grad_out, sem.at[9])

    def square(unit, carry):
        values = scatter.res[unit]
        return carry + jnp.sum(values * values, 0, keepdims=True)
    squares = lax.fori_loop(0, UNITS, square, jnp.zeros((1, COL), F32))
    value = jnp.sum(squares) + jnp.sum(mine * mine)
    note[...] = jnp.full((8, 128), value, F32)
    norm_talk.post(lambda other: note)
    norm_talk.collect(note[...])
    whole = lax.fori_loop(0, spot.count, lambda owner, carry: carry + norms[owner], jnp.zeros((8, 128), F32))
    norm_out[...] = jnp.sqrt(whole)
    fin.wait()
    scatter.all_sent()


def backward(layers, rows, *args):
    tokens, width = args[0].shape
    S = jax.ShapeDtypeStruct
    V = pltpu.VMEM
    D = pltpu.SemaphoreType.DMA
    joined = layers > 0
    grid = (layers, 4, rows, width) if joined else (width, width)
    outs = [S((tokens, width), F32), S((tokens, width), F32)]
    scratch = [V((3,) + grid, BF), V((2,) + grid, BF), V((2, width, tokens), BF), V((tokens, width), BF), V((tokens, width), BF),
               V((3, tokens, width), BF), V((tokens, 4 * SPAN), BF), V((tokens, 128), F32), V((8, width), F32),
               V((2, TOK, width), F32), V((2, TOK, width), BF), V((TOK, width), F32), D((11,)), D((2, 2)), D((2,)), D((2,))]
    specs = place(pl.ANY, 4)
    if joined:
        count = 8 * layers
        outs += [S((UNITS, rows // 2, COL), F32), S((2, 1, 128), F32), S((8, 128), F32)]
        specs = place(pl.ANY, 3) + place(pltpu.VMEM, 2)
        scratch += [V((count, 2, 1, 128), F32), V((count, 8, 128), F32), V((4 * width // 128 + 8, 1, 128), F32), V((8, 128), F32)]
        scratch += Everyone.scratch(count) + Everyone.scratch(count) + Scatter.scratch(layers, rows)
    else:
        outs += [S((STAGES - 1, width, width), BF), S((8, width), F32)]
    return pl.pallas_call(
        functools.partial(backward_kernel, layers),
        out_shape=outs,
        in_specs=place(pl.ANY, 2) + place(pltpu.VMEM, 3) + place(pl.ANY, 11),
        out_specs=specs,
        scratch_shapes=scratch,
        compiler_params=pltpu.CompilerParams(vmem_limit_bytes=VMEM_LIMIT, **(dict(collective_id=1, has_side_effects=True) if joined else {})),
        name="layer_backward",
    )(*args)


def adam_update(master, gradient, first, second, clip_scale, weight_decay, step_rate):
    gradient = gradient * clip_scale
    first_new = beta_first * first + (1.0 - beta_first) * gradient
    second_new = beta_second * second + (1.0 - beta_second) * gradient * gradient
    fix_first = 1.0 - beta_first**STEP
    fix_second = 1.0 - beta_second**STEP
    update_step = (
        first_new / fix_first / (jnp.sqrt(second_new / fix_second) + eps_adam)
        + weight_decay * master
    )
    master_new = master - step_rate * update_step
    return (master_new, first_new, second_new)


def adam_kernel(*refs):
    refs = list(refs)
    take = lambda n: [refs.pop(0) for _ in range(n)]
    sources, results, held, made = take(14), take(16), take(14), take(16)
    in_sem, out_sem = refs
    copies = [load(src, dst, in_sem.at[i]) for i, (src, dst) in enumerate(zip(sources, held))]
    for copy in copies[:2]:
        copy.wait()
    grads, norm = held[:2]
    clip_scale = jnp.minimum(1.0, clip_limit / (norm[0:1, 0:1] + 1e-06))
    outs = []
    for i in range(4):
        mine = [2 + i, 6 + i, 10 + i]
        for at in mine:
            copies[at].wait()
        for at, unit in enumerate(COLUMNS[i]):
            cols = slice(COL * at, COL * (at + 1))
            new = adam_update(*(held[m][:, cols] for m in mine[:1]), grads[unit], *(held[m][:, cols] for m in mine[1:]), clip_scale, decay_rate, learn_rate)
            for kind, value in enumerate((*new, new[0].astype(BF))):
                made[4 * kind + i][:, cols] = value
        outs += [load(made[4 * kind + i], results[4 * kind + i], out_sem.at[4 * kind + i]) for kind in range(4)]
    for copy in outs:
        copy.wait()


def adam_matrices(grads, norm, masters, firsts, seconds):
    shapes = [jax.ShapeDtypeStruct(m.shape, F32) for m in masters] * 3 + [jax.ShapeDtypeStruct(m.shape, BF) for m in masters]
    ins = (grads, norm, *masters, *firsts, *seconds)
    room = lambda arrays: [pltpu.VMEM(a.shape, a.dtype) for a in arrays]
    made = pl.pallas_call(
        adam_kernel,
        out_shape=shapes,
        in_specs=place(pl.ANY, 14),
        out_specs=place(pl.ANY, 16),
        scratch_shapes=[*room(ins), *room(shapes), pltpu.SemaphoreType.DMA((14,)), pltpu.SemaphoreType.DMA((16,))],
        compiler_params=pltpu.CompilerParams(vmem_limit_bytes=VMEM_LIMIT),
        name="adam",
    )(*ins)
    return [made[4 * i : 4 * i + 4] for i in range(4)]


def stage_columns(full_in, full_out, full_up, full_down):
    parts = [full_in[:, 2 * COL * (u % 3) + COL * (u // 3) :][:, :COL] for u in range(6)]
    pairs = [jnp.concatenate(parts[2 * i : 2 * i + 2], 1) for i in range(3)]
    return jnp.stack([*pairs, full_out, full_up, full_down])


COLUMNS = ((6, 9, 7, 10, 8, 11), (4, 5), (2, 3), (0, 1))


def by_matrix(units):
    return [jnp.concatenate([units[i] for i in at], 1) for at in COLUMNS]


def turned_down(kept, joined, layers, rows):
    down = kept[-1].reshape(layers, 4, rows, COL) if joined else kept[-1]
    return (*kept[:-1], down)


def shards(
    inputs,
    segments,
    starts,
    out_grad,
    proj_in,
    proj_out,
    up_proj,
    down_proj,
    gains_biases,
    first_in,
    first_out,
    first_up,
    first_down,
    first_small,
    second_in,
    second_out,
    second_up,
    second_down,
    second_small,
):
    axes = ("wide", "narrow")
    wide, narrow = lax.axis_size("wide"), lax.axis_size("narrow")
    tokens, width = inputs.shape
    share = gains_biases.shape[0]
    me = lax.axis_index("wide") * narrow + lax.axis_index("narrow")
    rows = width // wide
    joined = narrow == 2 and wide % 4 == 0 and rows % 16 == 0 and share == 160
    layers = wide // 4 if joined else 0
    rope = jnp.asarray(rope_tables())
    small_low = lax.reduce_precision(gains_biases, 8, 7)
    if joined:
        shift = lax.rem(share * me, 128)
        window = lax.dynamic_update_slice(jnp.zeros((256,), F32), small_low, (shift,)).reshape(2, 1, 128)
        *kept, weights, vec = forward(layers, rows, inputs, out_grad, segments, starts, rope, (proj_in, proj_out, up_proj, down_proj, window))
    else:
        gathered = [lax.all_gather(m.astype(BF), axes, axis=0, tiled=True) for m in (proj_in, proj_out, up_proj, down_proj)]
        weights = stage_columns(*gathered)
        vec = lax.all_gather(small_low, axes, axis=0, tiled=True).reshape(4, width)
        vec = jnp.pad(vec, ((0, 4), (0, 0)))
        kept = forward(layers, rows, inputs, out_grad, segments, starts, rope, (weights, vec))
    made = backward(layers, rows, inputs, out_grad, starts, rope, vec, *turned_down(kept, joined, layers, rows), weights)
    block_out, input_grad = made[:2]
    mats, firsts, seconds = (proj_in, proj_out, up_proj, down_proj), (first_in, first_out, first_up, first_down), (second_in, second_out, second_up, second_down)
    if joined:
        norm = made[4]
        shard_small = lax.dynamic_slice(made[3].reshape(256), (shift,), (share,))
        grad_norm = norm[0, 0]
        clip_scale = jnp.minimum(1.0, clip_limit / (grad_norm + 1e-06))
        mat_news = adam_matrices(made[2], norm, mats, firsts, seconds)
    else:
        stages = jnp.concatenate([kept[-1].reshape(1, width, width), made[2]], 0).astype(F32)
        full_grads = by_matrix([stages[i // 2][:, COL * (i % 2) :][:, :COL] for i in range(UNITS)])
        scatter = lambda m: lax.psum_scatter(m, axes, scatter_dimension=0, tiled=True)
        grads = [scatter(m) for m in full_grads]
        shard_small = scatter(jnp.concatenate([made[3][3], made[3][2], made[3][1], made[3][0]]))
        squares = sum(jnp.sum(m * m) for m in (*grads, shard_small))
        grad_norm = jnp.sqrt(lax.psum(squares, axes))
        clip_scale = jnp.minimum(1.0, clip_limit / (grad_norm + 1e-06))
        each = [adam_update(*four, clip_scale, decay_rate, learn_rate) for four in zip(mats, grads, firsts, seconds)]
        mat_news = [[new[i] for new in each] for i in range(3)]
        mat_news.append([m.astype(BF) for m in mat_news[0]])
    small_new = adam_update(gains_biases, shard_small, first_small, second_small, clip_scale, 0.0, small_rate)
    small_news = (*small_new, small_new[0].astype(BF))
    return (
        block_out,
        input_grad,
        grad_norm,
        *(part for mat, small in zip(mat_news, small_news) for part in (*mat, small)),
    )


def solution(mesh):
    split, flat = P(("wide", "narrow"), None), P(("wide", "narrow"))
    state = (split, split, split, split, flat)
    return jax.shard_map(
        shards,
        mesh=mesh,
        in_specs=(split,) * 4 + state * 3,
        out_specs=(split, split, P()) + state * 4,
        check_vma=False,
    )
```

```python
import functools
import math

import jax
import jax.numpy as jnp
import numpy as np
from jax import lax
from jax.experimental import pallas as pl
from jax.experimental.pallas import tpu as pltpu
from jax.sharding import PartitionSpec as P

HEADS = 16
HEAD_DIM = 80
STEP = 5
PATCHES = 16

eps_norm = 1e-05
eps_stat = 1e-05
rope_base = 10000.0
clip_limit = 256.0
learn_rate = 0.03
small_rate = 0.4
decay_rate = 0.1
beta_first = 0.9
beta_second = 0.999
eps_adam = 1e-08

BF = jnp.bfloat16
F32 = jnp.float32
MESH = pl.DeviceIdType.MESH

COL = 640
UNITS = 12
STAGES = 6
SPAN = 256
GROUP = 128
TOK = 256
WIDE_TOK = 512
VMEM_LIMIT = 64 << 20


def lanes(ref_cols):
    return lax.broadcasted_iota(jnp.int32, (1, ref_cols), 1)


def nn(left_in, right_in):
    return lax.dot_general(
        left_in, right_in, (((1,), (0,)), ((), ())), preferred_element_type=F32
    )


def nt(left_in, right_in):
    return lax.dot_general(
        left_in, right_in, (((1,), (1,)), ((), ())), preferred_element_type=F32
    )


def unit_cols(side):
    return pl.ds(pl.multiple_of(COL * side, 128), COL)


def rope_tables():
    half = HEAD_DIM // 2
    inverse = np.float32(rope_base) ** (-np.arange(half, dtype=np.float32) * np.float32(2.0) / np.float32(HEAD_DIM))
    angles = np.arange(PATCHES, dtype=np.float32)[:, None] * inverse.astype(np.float32)[None, :]
    cosine, sine = np.cos(angles), np.sin(angles)
    zero = np.zeros_like(sine)
    heads = COL // HEAD_DIM
    full = [
        np.tile(np.concatenate(pair, 1), (1, heads))
        for pair in ((cosine, cosine), (-sine, zero), (zero, sine))
    ]
    return np.stack(full).astype(np.float32)


def rotate(values_in, table, sign):
    rows = values_in.shape[0]
    ahead = pltpu.roll(values_in, COL - HEAD_DIM // 2, 1)
    behind = pltpu.roll(values_in, HEAD_DIM // 2, 1)
    cube = (rows // PATCHES, PATCHES, COL)
    turn = ahead.reshape(cube) * table[1] + behind.reshape(cube) * table[2]
    straight = values_in.reshape(cube) * table[0]
    return (straight + sign * turn).reshape(rows, COL)


def eye(size):
    row = lax.broadcasted_iota(jnp.int32, (size, size), 0)
    col = lax.broadcasted_iota(jnp.int32, (size, size), 1)
    return row == col


def to_column(row_in, same):
    return jnp.sum(jnp.where(same, row_in, 0.0), 1, keepdims=True)


def to_row(column_in, same):
    return jnp.sum(jnp.where(same, column_in, 0.0), 0, keepdims=True)


def per_token(table):
    rows = table.shape[0]
    size = rows * PATCHES
    wide = jnp.broadcast_to(table.astype(F32)[:, None, :], (rows, PATCHES, PATCHES)).reshape(size, PATCHES)
    patch = lax.rem(lax.broadcasted_iota(jnp.int32, (size, PATCHES), 0), PATCHES)
    hit = lax.broadcasted_iota(jnp.int32, (size, PATCHES), 1) == patch
    return jnp.sum(jnp.where(hit, wide, 0.0), 1, keepdims=True)


def turn_table(table):
    rows = table.shape[1]
    same = jnp.where(eye(rows), 1.0, 0.0).astype(BF)
    return nt(same, table[...].astype(F32).astype(BF))


def context_mask(start_table):
    start_col = per_token(start_table).astype(jnp.int32)
    size = start_col.shape[0]
    row = lax.broadcasted_iota(jnp.int32, (size, size), 0)
    col = lax.broadcasted_iota(jnp.int32, (size, size), 1)
    return col == lax.div(row, PATCHES) * PATCHES + start_col


def pair_masks(pair):
    lane = lanes(SPAN)
    low = 160 * pair - 128 * (160 * pair // 128)
    return (
        (lane >= low) & (lane < low + HEAD_DIM),
        (lane >= low + HEAD_DIM) & (lane < low + 2 * HEAD_DIM),
    )


def both_heads(window, masks):
    zero = jnp.zeros_like(window)
    return jnp.concatenate([jnp.where(masks[0], window, zero), jnp.where(masks[1], window, zero)], 0)


def turn_pair(pair_in):
    return jnp.concatenate([pair_in[:, :GROUP].T, pair_in[:, GROUP:].T], 1)


def attention_bias(seg_table):
    row = lax.broadcasted_iota(jnp.int32, (GROUP, GROUP), 0)
    col = lax.broadcasted_iota(jnp.int32, (GROUP, GROUP), 1)
    seg_col = per_token(seg_table)
    seg_row = to_row(seg_col, row == col)
    allowed = (lax.div(row, PATCHES) == lax.div(col, PATCHES)) & (row <= col) & (seg_col == seg_row)
    bias = jnp.where(allowed, 0.0, -1e30)
    return jnp.concatenate([bias, bias], 1)


def head_window(qkv, unit, rows, pair):
    low = COL * (unit % 2) + 128 * (160 * pair // 128)
    return qkv[unit // 2, rows, low : low + SPAN]


def spread_windows(parts):
    tiles = []
    for tile in range(5):
        total = None
        for pair in (tile - 1, tile):
            if 0 <= pair < 4:
                piece = parts[pair][:, 128 * (tile - pair) : 128 * (tile - pair) + 128]
                total = piece if total is None else total + piece
        tiles.append(total)
    return jnp.concatenate(tiles, 1)


class Forward:
    def __init__(self, weight, refs):
        self.weight = weight
        (self.xv, self.dyv, self.seg, self.start, self.vec, self.rope, self.h1, self.tt, self.qkv, self.att,
         self.mix, self.r1, self.dg, self.stats, self.bsum) = refs
        self.tokens = self.xv.shape[0]
        self.width = self.xv.shape[1]

    def blocks(self, body, low=0, high=None):
        def step(i, carry):
            body(pl.multiple_of(i * TOK, TOK), i)
            return carry
        lax.fori_loop(low, self.tokens // TOK if high is None else high, step, 0)

    def norms(self, low, high):
        width = self.width
        gain = self.vec[0:1, :]

        def body(at, i):
            rows = pl.ds(at, TOK)
            same = eye(TOK)
            x = self.xv[rows, :].astype(F32)
            mean = jnp.sum(x, 1, keepdims=True) * (1.0 / width)
            off = x - mean
            spread = jnp.sqrt(jnp.sum(off * off, 1, keepdims=True) * (1.0 / width) + eps_stat)
            mask = context_mask(self.start[pl.ds(i * (TOK // PATCHES), TOK // PATCHES), :])
            mu = jnp.sum(jnp.where(mask, to_row(mean, same), 0.0), 1, keepdims=True)
            sigma = jnp.sum(jnp.where(mask, to_row(spread, same), 0.0), 1, keepdims=True)
            z = (x - mu) / sigma
            scale = lax.rsqrt(jnp.sum(z * z, 1, keepdims=True) * (1.0 / width) + eps_norm)
            h1 = (z * scale * gain).astype(BF)
            self.h1[rows, :] = h1
            self.tt[0, :, rows] = h1.T
            dy = self.dyv[rows, :].astype(F32)
            low = (dy * sigma).astype(BF)
            self.dyv[rows, :] = low
            self.bsum[0:1, :] += jnp.sum(low.astype(F32), 0, keepdims=True)
            self.stats[rows, 0:1] = mu
            self.stats[rows, 1:2] = sigma
            self.stats[rows, 2:3] = mean
            self.stats[rows, 3:4] = spread
            self.stats[rows, 4:5] = scale
            self.stats[rows, 6:7] = jnp.sum(dy, 1, keepdims=True)

        self.blocks(body, low, high)

    def project(self, stage):
        def step(i, carry):
            rows = pl.ds(pl.multiple_of(i * WIDE_TOK, WIDE_TOK), WIDE_TOK)
            made = nn(self.h1[rows, :], self.weight(stage))
            for side in range(2):
                cols = slice(COL * side, COL * (side + 1))
                part = made[:, cols]
                if (2 * stage + side) % 3 < 2:
                    part = rotate(part, self.rope, 1.0)
                self.qkv[stage, rows, cols] = part.astype(BF)
            return carry

        lax.fori_loop(0, self.tokens // WIDE_TOK, step, 0)

    def attend(self, half, low=0, high=None):
        scale = 1.0 / math.sqrt(HEAD_DIM)

        def step(g, carry):
            rows = pl.ds(pl.multiple_of(g * GROUP, GROUP), GROUP)
            bias = attention_bias(self.seg[pl.ds(g * (GROUP // PATCHES), GROUP // PATCHES), :])
            look = lambda kind, pair: head_window(self.qkv, 3 * half + kind, rows, pair)
            scores = [
                nt(look(1, pair), both_heads(look(0, pair), pair_masks(pair)))
                for pair in range(4)
            ]
            probs = []
            for pair in range(4):
                own = scores[pair] * scale + bias
                expo = jnp.exp(own - jnp.max(own, 0, keepdims=True))
                prob = (expo * (1.0 / jnp.sum(expo, 0, keepdims=True))).astype(BF)
                self.att[half, rows, SPAN * pair : SPAN * (pair + 1)] = prob
                probs.append(prob)
            parts = [
                nn(turn_pair(probs[pair]), both_heads(look(2, pair), pair_masks(pair)))
                for pair in range(4)
            ]
            self.mix[rows, COL * half : COL * (half + 1)] = spread_windows(parts).astype(BF)
            return carry

        lax.fori_loop(low, self.tokens // GROUP if high is None else high, step, 0)

    def mix_turned(self, slot):
        def body(at, i):
            rows = pl.ds(at, TOK)
            self.tt[slot, :, rows] = self.mix[rows, :].T

        self.blocks(body)

    def residual(self, slot):
        width = self.width
        gain = self.vec[1:2, :]

        def body(at, i):
            rows = pl.ds(at, TOK)
            mix = self.mix[rows, :]
            made = nn(mix, self.weight(3))
            z = (self.xv[rows, :].astype(F32) - self.stats[rows, 0:1]) / self.stats[rows, 1:2]
            r1 = z + made
            scale = lax.rsqrt(jnp.sum(r1 * r1, 1, keepdims=True) * (1.0 / width) + eps_norm)
            self.stats[rows, 5:6] = scale
            self.r1[rows, :] = r1
            h2 = (r1 * scale * gain).astype(BF)
            self.h1[rows, :] = h2
            self.tt[slot, :, rows] = h2.T

        self.blocks(body)

    def hidden(self, slot):
        bias = self.vec[2:3, :]
        c0 = math.sqrt(2.0 / math.pi)

        def body(at, i):
            rows = pl.ds(at, TOK)
            made = nn(self.h1[rows, :], self.weight(4))
            for half in range(2):
                cols = slice(COL * half, COL * (half + 1))
                u = made[:, cols] + bias[:, cols]
                square = u * u
                bend = jnp.tanh(c0 * (u + 0.044715 * u * square))
                act = (0.5 * u * (1.0 + bend)).astype(BF)
                slope = 0.5 * (1.0 + bend) + (0.5 * c0) * u * (1.0 - bend * bend) * (1.0 + (3 * 0.044715) * square)
                self.dg[rows, cols] = slope.astype(BF)
                self.mix[rows, cols] = act
                self.tt[slot, cols, rows] = act.T

        self.blocks(body)

    def chunk(self, i):
        per = self.tokens // TOK
        return self.qkv.at[lax.div(i, per), pl.ds(pl.multiple_of(TOK * lax.rem(i, per), TOK), TOK), :]

    def down_grad(self, left):
        def step(i, carry):
            rows = pl.ds(pl.multiple_of(i * TOK, TOK), TOK)
            self.chunk(i)[...] = nn(self.tt[left, rows, :], self.dyv[...]).astype(BF)
            return carry
        lax.fori_loop(0, self.width // TOK, step, 0)


class Backward:
    def __init__(self, refs):
        (self.wbuf, self.part, self.lt, self.ea, self.eb, self.qkv, self.att, self.vec, self.rope,
         self.stats, self.bsum, self.start, self.rblk, self.bblk) = refs
        self.tokens, self.width = self.ea.shape

    def blocks(self, body, low=0, high=None):
        def step(i, carry):
            body(pl.multiple_of(i * TOK, TOK), i)
            return carry
        lax.fori_loop(low, self.tokens // TOK if high is None else high, step, 0)

    def weight(self, slot):
        return self.wbuf[slot].reshape(self.width, self.width)

    def weight_grad(self, slot, left, right):
        part = self.part.at[slot]
        if len(part.shape) == 4:
            tall = 2 * part.shape[1] * part.shape[2]
            def step(i, carry):
                rows = pl.ds(pl.multiple_of(i * tall, 16), tall)
                for low in range(0, self.width, 512):
                    cols = slice(low, min(low + 512, self.width))
                    made = nn(self.lt[left, rows, :], right(cols))
                    part[pl.ds(2 * i, 2), :, :, cols] = made.astype(BF).reshape((2,) + part.shape[1:3] + (made.shape[1],))
                return carry
        else:
            tall = TOK
            def step(i, carry):
                rows = pl.ds(pl.multiple_of(i * tall, tall), tall)
                part[rows, :] = nn(self.lt[left, rows, :], right(slice(None))).astype(BF)
                return carry
        lax.fori_loop(0, self.width // tall, step, 0)

    def hidden(self, slot):
        def body(at, i):
            rows = pl.ds(at, TOK)
            low = (nt(self.ea[rows, :], self.weight(slot)) * self.eb[rows, :].astype(F32)).astype(BF)
            self.eb[rows, :] = low
            self.bsum[1:2, :] += jnp.sum(low.astype(F32), 0, keepdims=True)

        self.blocks(body)

    def stream(self, body, loads, low=0, high=None):
        count = self.tokens // TOK
        high = count if high is None else high

        def copies(i):
            slot = lax.rem(i, 2)
            rows = pl.ds(pl.multiple_of(i * TOK, TOK), TOK)
            return [pltpu.make_async_copy(src.at[rows, :], buf.at[slot], sem.at[slot]) for src, buf, sem in loads]

        if low == 0:
            for cp in copies(0):
                cp.start()

        def inner(at, i):
            @pl.when(i + 1 < count)
            def _():
                for cp in copies(i + 1):
                    cp.start()
            for cp in copies(i):
                cp.wait()
            body(at, i, lax.rem(i, 2))

        self.blocks(inner, low, high)

    def result(self, slot, loads, out, out_sem, low, high):
        bias = self.vec[3:4, :]
        count = self.tokens // TOK

        def copy(i):
            turn = lax.rem(i, 2)
            return pltpu.make_async_copy(self.rblk.at[turn], out.at[pl.ds(pl.multiple_of(i * TOK, TOK), TOK), :], out_sem.at[turn])

        def fetch(i):
            turn = lax.rem(i, 2)
            rows = pl.ds(pl.multiple_of(i * TOK, TOK), TOK)
            return [pltpu.make_async_copy(src.at[rows, :], buf.at[turn], sem.at[turn]) for src, buf, sem in loads]

        if low == 0:
            for cp in fetch(0):
                cp.start()

        def body(at, i):
            rows = pl.ds(at, TOK)
            turn = lax.rem(i, 2)

            @pl.when(i >= 1)
            def _():
                copy(i - 1).wait()

            @pl.when(i + 1 < count)
            def _():
                for cp in fetch(i + 1):
                    cp.start()

            act = self.eb[rows, :]
            made = nn(act, self.weight(slot))
            for cp in fetch(i):
                cp.wait()
            r2 = self.rblk[turn] + (made + bias)
            self.rblk[turn] = r2 * self.stats[rows, 1:2] + self.stats[rows, 0:1]
            copy(i).start()
            self.stats[rows, 7:8] = jnp.sum(self.bblk[turn].astype(F32) * r2, 1, keepdims=True)

        self.blocks(body, low, high)
        if high == count:
            copy(count - 1).wait()

    def second_norm(self, slot, loads, hold, low, high):
        width = self.width
        gain = self.vec[1:2, :]

        def body(at, i, turn):
            hold[...] = nt(self.eb[pl.ds(at, TOK), :], self.weight(slot))

            def step(c, carry):
                inside = pl.multiple_of(c * GROUP, GROUP)
                rows, local = pl.ds(pl.multiple_of(at + inside, GROUP), GROUP), pl.ds(inside, GROUP)
                dh2 = hold[local, :]
                scale = self.stats[rows, 5:6]
                n2 = self.rblk[turn, local, :] * scale
                self.bsum[2:3, :] += jnp.sum(dh2 * n2, 0, keepdims=True)
                dn = dh2 * gain
                inner = jnp.sum(dn * n2, 1, keepdims=True) * (1.0 / width)
                dr1 = self.bblk[turn, local, :].astype(F32) * self.stats[rows, 1:2] + scale * (dn - n2 * inner)
                self.ea[rows, :] = dr1.astype(BF)
                return carry
            lax.fori_loop(0, TOK // GROUP, step, 0)

        self.stream(body, loads, low, high)

    def mixed(self, slot):
        def body(at, i):
            rows = pl.ds(at, TOK)
            self.eb[rows, :] = nt(self.ea[rows, :], self.weight(slot)).astype(BF)

        self.blocks(body)

    def attend(self, half, low=0, high=None):
        scale = 1.0 / math.sqrt(HEAD_DIM)

        def step(g, carry):
            rows = pl.ds(pl.multiple_of(g * GROUP, GROUP), GROUP)
            starts = [128 * (160 * pair // 128) for pair in range(4)]
            look = lambda kind, pair: head_window(self.qkv, 3 * half + kind, rows, pair)
            masks = [pair_masks(pair) for pair in range(4)]
            dmix = [both_heads(self.eb[rows, pl.ds(COL * half + starts[i], SPAN)], masks[i]) for i in range(4)]
            probs = [self.att[rows, SPAN * i : SPAN * (i + 1)] for i in range(4)]
            das = [nt(look(2, i), dmix[i]) for i in range(4)]
            dss = []
            for i in range(4):
                p32 = probs[i].astype(F32)
                weighed = p32 * das[i]
                dss.append((weighed - p32 * jnp.sum(weighed, 0, keepdims=True)).astype(BF))
            dvs = [nn(probs[i], dmix[i]) for i in range(4)]
            dks = [nn(dss[i], both_heads(look(0, i), masks[i])) for i in range(4)]
            dqs = [nn(turn_pair(dss[i]), both_heads(look(1, i), masks[i])) for i in range(4)]
            dq = rotate(spread_windows(dqs) * scale, self.rope, -1.0)
            dk = rotate(spread_windows(dks) * scale, self.rope, -1.0)
            for kind, made in enumerate((dq, dk, spread_windows(dvs))):
                unit = 3 * half + kind
                self.qkv[unit // 2, rows, COL * (unit % 2) : COL * (unit % 2 + 1)] = made.astype(BF)
            return carry

        lax.fori_loop(low, self.tokens // GROUP if high is None else high, step, 0)

    def first_norm(self, slots, loads, out, out_sem, turns, low, high):
        width = self.width
        gain = self.vec[0:1, :]
        count = self.tokens // TOK

        def copy(i):
            slot = lax.rem(i, 2)
            return pltpu.make_async_copy(turns.at[slot], out.at[pl.ds(pl.multiple_of(i * TOK, TOK), TOK), :], out_sem.at[slot])

        def piece(at, inside, turn):
            rows = pl.ds(pl.multiple_of(at + inside, GROUP), GROUP)
            local = pl.ds(inside, GROUP)
            same = eye(GROUP)
            dh1 = turns[turn, local, :]
            mu, sigma = self.stats[rows, 0:1], self.stats[rows, 1:2]
            mean, spread = self.stats[rows, 2:3], self.stats[rows, 3:4]
            scale = self.stats[rows, 4:5]
            inv = 1.0 / sigma
            x = self.bblk[turn, local, :].astype(F32)
            z = (x - mu) * inv
            n1 = z * scale
            self.bsum[3:4, :] += jnp.sum(dh1 * n1, 0, keepdims=True)
            dn = dh1 * gain
            inner = jnp.sum(dn * n1, 1, keepdims=True) * (1.0 / width)
            dz = scale * (dn - n1 * inner) + self.ea[rows, :].astype(F32)
            dmu = self.stats[rows, 6:7] - jnp.sum(dz, 1, keepdims=True) * inv
            dsigma = self.stats[rows, 7:8] - jnp.sum(dz * z, 1, keepdims=True) * inv
            per = GROUP // PATCHES
            mask = context_mask(self.start[pl.ds(pl.multiple_of(lax.div(at + inside, PATCHES), per), per), :])
            dmean = to_column(jnp.sum(jnp.where(mask, dmu, 0.0), 0, keepdims=True), same)
            dspread = to_column(jnp.sum(jnp.where(mask, dsigma, 0.0), 0, keepdims=True), same)
            turns[turn, local, :] = dz * inv + (dmean * (1.0 / width) + (x - mean) * (dspread * (1.0 / width) / spread))

        def body(at, i, turn):
            rows = pl.ds(at, TOK)
            dh1 = nt(self.qkv[0, rows, :], self.weight(slots[0]))
            for stage in (1, 2):
                dh1 += nt(self.qkv[stage, rows, :], self.weight(slots[stage]))

            @pl.when(i >= 2)
            def _():
                copy(i - 2).wait()

            turns[turn] = dh1

            def step(c, carry):
                piece(at, pl.multiple_of(c * GROUP, GROUP), turn)
                return carry
            lax.fori_loop(0, TOK // GROUP, step, 0)
            copy(i).start()

        self.stream(body, loads, low, high)
        if high == count:
            for i in range(max(count - 2, 0), count):
                copy(i).wait()


class Spot:
    def __init__(self, layers):
        self.layers = layers
        wide, self.c = lax.axis_index("wide"), lax.axis_index("narrow")
        self.z, self.p = lax.div(wide, 4), lax.rem(wide, 4)
        self.px = self.p + 1 - 2 * lax.rem(self.p, 2)
        self.py = lax.rem(self.p + 2, 4)
        self.pd = 3 - self.p
        self.me = 2 * wide + self.c
        self.count = 8 * layers
        self.sibling = self.device(self.z, self.p, 1 - self.c)
        self.across_x = self.device(self.z, self.px, self.c)
        self.across_y = self.device(self.z, self.py, self.c)
        self.pa = jnp.where(self.c == 0, self.px, self.py)
        self.pb = jnp.where(self.c == 0, self.py, self.px)
        self.across_a = self.device(self.z, self.pa, self.c)
        self.across_b = self.device(self.z, self.pb, self.c)

    def device(self, z, p, c):
        return (z * 4 + p, c)

    def layer(self, k):
        return lax.rem(self.z + k, self.layers)

    def in_layer(self, z):
        return self.device(z, self.p, self.c)

    def others(self, body):
        def step(k, carry):
            other = lax.rem(self.me + k, self.count)
            body(k, other, (lax.div(other, 2), lax.rem(other, 2)))
            return carry
        lax.fori_loop(1, self.count, step, 0)

    def meet(self):
        door = pltpu.get_barrier_semaphore()
        self.others(lambda k, other, device: pl.semaphore_signal(door, 1, device_id=device, device_id_type=MESH))
        pl.semaphore_wait(door, self.count - 1)


def remote(src, dst, send, recv, device):
    return pltpu.make_async_remote_copy(src, dst, send, recv, device_id=device, device_id_type=MESH)


class Posted:
    def __init__(self):
        self.groups = {}

    def go(self, key, *args):
        copy = remote(*args)
        copy.start()
        self.groups.setdefault(key, []).append(copy)

    def sent(self, key):
        for copy in self.groups.pop(key, []):
            copy.wait_send()

    def all_sent(self):
        for key in list(self.groups):
            self.sent(key)


class Gather(Posted):
    @staticmethod
    def scratch(layers, rows):
        D = pltpu.SemaphoreType.DMA
        n = STAGES
        return [pltpu.VMEM((n, rows, COL), F32), D((n,)), D((n,)), D((n,)), D((n, layers)), D((n, layers)),
                D((n, layers, 2)), D((n, layers, 2)), D((n, 2)), D((n, 2)), D((n, 4)), D((n, 4))]

    def __init__(self, spot, full, owned, refs):
        super().__init__()
        self.spot, self.full, self.owned = spot, full, owned
        (self.desk, self.local, self.es, self.er, self.zs, self.zr, self.ps, self.pr, self.ds, self.dr, self.ss, self.sr) = refs
        self.rows = self.desk.shape[1]
        self.half = self.rows // 2
        self.cut = self.rows // 32 * 16 + (16 if self.rows % 32 else 0)

    def line(self, j, p, side=None):
        return self.full.at[j, :, p, :, unit_cols(self.spot.c if side is None else side)]

    def block(self, j, z, p):
        return self.full.at[j, z, p, :, unit_cols(self.spot.c)]

    def shard(self, j, unit):
        if j < 3:
            column = 2 * COL * lax.rem(unit, 3) + COL * lax.div(unit, 3)
            return self.owned[0].at[:, pl.ds(pl.multiple_of(column, 128), COL)]
        return self.owned[j - 2].at[:, pl.ds(pl.multiple_of(COL * lax.rem(unit, 2), 128), COL)]

    def desk_rows(self, j, core):
        return self.desk.at[j, pl.ds(pl.multiple_of(self.half * core, 8), self.half), :]

    def prepare(self, j):
        c = self.spot.c
        place_at = self.desk_rows(j, c)
        pltpu.make_async_copy(self.shard(j, 2 * j + c), place_at, self.local.at[j]).start()
        self.go(j, self.shard(j, 2 * j + 1 - c), place_at, self.es.at[j], self.er.at[j], self.spot.sibling)

    def across(self, j, k):
        s = self.spot
        block = self.block(j, s.layer(s.layers - k), s.p)
        self.go(j, block, block, self.ps.at[j, k, 0], self.pr.at[j, k, 0], s.across_x)
        self.go(j, block, block, self.ps.at[j, k, 1], self.pr.at[j, k, 1], s.across_y)

    def e1(self, j):
        s = self.spot
        mine, other = self.desk_rows(j, s.c), self.desk_rows(j, 1 - s.c)
        pltpu.make_async_copy(mine, mine, self.local.at[j]).wait()
        remote(other, other, self.es.at[j], self.er.at[j], s.sibling).wait_recv()
        self.block(j, s.z, s.p)[...] = self.desk[j].astype(BF)
        self.across(j, 0)

    def e0(self, j):
        s = self.spot
        block = self.block(j, s.z, s.p)
        for k in range(1, s.layers):
            self.go(j, block, block, self.zs.at[j, k], self.zr.at[j, k], s.in_layer(s.layer(k)))

    def e2(self, j):
        s = self.spot
        for k in range(1, s.layers):
            z = s.layer(s.layers - k)
            block = self.block(j, z, s.p)
            remote(block, block, self.zs.at[j, k], self.zr.at[j, k], s.in_layer(z)).wait_recv()
            self.across(j, k)
        self.to_sibling(j, 0, s.p)

    def to_sibling(self, j, i, p):
        line = self.line(j, p)
        self.go(j, line, line, self.ss.at[j, i], self.sr.at[j, i], self.spot.sibling)

    def corner(self, j, p, top):
        rows = pl.ds(0, self.cut) if top else pl.ds(self.cut, self.rows - self.cut)
        return self.full.at[j, :, p, rows, unit_cols(self.spot.c)]

    def e3(self, j):
        s = self.spot
        for k in range(s.layers):
            z = s.layer(s.layers - k)
            for i, p in ((0, s.px), (1, s.py)):
                block = self.block(j, z, p)
                remote(block, block, self.ps.at[j, k, i], self.pr.at[j, k, i], s.across_x).wait_recv()
        top, rest = self.corner(j, s.pa, True), self.corner(j, s.pb, False)
        self.go(j, top, top, self.ds.at[j, 0], self.dr.at[j, 0], s.across_b)
        self.go(j, rest, rest, self.ds.at[j, 1], self.dr.at[j, 1], s.across_a)
        self.to_sibling(j, 1, s.px)
        self.to_sibling(j, 2, s.py)

    def e4(self, j):
        s = self.spot
        top, rest = self.corner(j, s.pd, True), self.corner(j, s.pd, False)
        remote(top, top, self.ds.at[j, 0], self.dr.at[j, 0], s.across_y).wait_recv()
        remote(rest, rest, self.ds.at[j, 1], self.dr.at[j, 1], s.across_x).wait_recv()
        self.to_sibling(j, 3, s.pd)

    def e5(self, j):
        s = self.spot
        for i, p in enumerate((s.p, s.px, s.py, s.pd)):
            line = self.line(j, p, 1 - s.c)
            remote(line, line, self.ss.at[j, i], self.sr.at[j, i], s.sibling).wait_recv()


class Scatter(Posted):
    SLOTS = 3

    @staticmethod
    def scratch(layers, rows):
        D, V = pltpu.SemaphoreType.DMA, pltpu.VMEM
        n, m = STAGES, Scatter.SLOTS
        return [V((n - 1, layers, 4, rows, COL), BF), V((m, layers, rows, COL), BF), V((m, 2, layers, rows, COL), BF),
                V((m, layers, rows, COL), BF), V((m, rows, COL), F32), V((UNITS, rows // 2, COL), F32),
                D((n,)), D((n,)), D((n, 2, layers)), D((n, 2, layers)), D((n, 2, layers)), D((n, 2, layers)), D((n, layers)), D((n, layers)), D((n,)), D((n,))]

    def __init__(self, spot, part, refs):
        super().__init__()
        self.spot, self.part = spot, part
        (self.sums, self.dg, self.pl, self.zb, self.fin, self.res,
         self.ss, self.sr, self.ds, self.dr, self.ps, self.pr, self.zs, self.zr, self.fs, self.fr) = refs
        self.rows = self.dg.shape[2]
        self.half = self.rows // 2
        self.cut = self.rows // 32 * 16 + (16 if self.rows % 32 else 0)

    def sum_at(self, j):
        return self.sums.at[j % (STAGES - 1)]

    def each_layer(self, body):
        def step(z, carry):
            body(z)
            return carry
        lax.fori_loop(0, self.spot.layers, step, 0)

    def f1(self, j):
        s = self.spot
        self.go(("f1", j), self.part.at[j % 2, :, :, :, unit_cols(1 - s.c)], self.sum_at(j), self.ss.at[j], self.sr.at[j], s.sibling)

    def order(self):
        return [*range(1, self.spot.layers), 0]

    def corners(self, j):
        s = self.spot
        total, slot = self.sum_at(j), j % self.SLOTS
        for k in self.order():
            z = s.layer(k)
            for i, (rows, device) in enumerate(((pl.ds(0, self.cut), s.across_b), (pl.ds(self.cut, self.rows - self.cut), s.across_a))):
                self.go(j, total.at[z, s.pd, rows, :], self.dg.at[slot, z, rows, :], self.ds.at[j, i, k], self.dr.at[j, i, k], device)

    def f2(self, j):
        s = self.spot
        own, total = self.part.at[j % 2], self.sum_at(j)
        remote(total, total, self.ss.at[j], self.sr.at[j], s.sibling).wait_recv()

        def add(p):
            def one(z):
                total[z, p] = total[z, p] + own[z, p, :, unit_cols(s.c)]
            self.each_layer(one)

        add(s.pd)
        self.corners(j)
        for p in (s.px, s.py, s.p):
            add(p)

    def f3(self, j):
        s = self.spot
        total, slot = self.sum_at(j), j % self.SLOTS
        for k in self.order():
            z = s.layer(k)
            for i, (low, size, p) in enumerate(((0, self.cut, s.pa), (self.cut, self.rows - self.cut, s.pb))):
                rows = pl.ds(low, size)
                came = self.dg.at[slot, z, rows, :]
                remote(came, came, self.ds.at[j, i, k], self.dr.at[j, i, k], s.across_y).wait_recv()
                total[z, p, rows, :] = total[z, p, rows, :] + came[...]
            for i, (p, device) in enumerate(((s.px, s.across_x), (s.py, s.across_y))):
                self.go(j, total.at[z, p], self.pl.at[slot, i, z], self.ps.at[j, i, k], self.pr.at[j, i, k], device)

    def f4(self, j):
        s = self.spot
        total, slot = self.sum_at(j), j % self.SLOTS
        for k in self.order():
            z = s.layer(k)
            for i in range(2):
                came = self.pl.at[slot, i, z]
                remote(came, came, self.ps.at[j, i, k], self.pr.at[j, i, k], s.across_x).wait_recv()
            total[z, s.p] = (total[z, s.p].astype(F32) + self.pl[slot, 0, z].astype(F32) + self.pl[slot, 1, z].astype(F32)).astype(BF)
            if k:
                self.go(j, total.at[z, s.p], self.zb.at[slot, k], self.zs.at[j, k], self.zr.at[j, k], s.in_layer(z))

    def f5(self, j):
        s = self.spot
        slot = j % self.SLOTS
        total = self.sums[j % (STAGES - 1), s.z, s.p].astype(F32)
        for k in range(1, s.layers):
            came = self.zb.at[slot, k]
            remote(came, came, self.zs.at[j, k], self.zr.at[j, k], s.across_x).wait_recv()
            total = total + self.zb[slot, k].astype(F32)
        self.sent(j)
        self.sent(("fin", j - self.SLOTS))
        self.fin[slot] = total
        mine, other = (pl.ds(pl.multiple_of(self.half * c, 8), self.half) for c in (s.c, 1 - s.c))
        self.res[2 * j + s.c] = self.fin[slot, mine, :]
        self.go(("fin", j), self.fin.at[slot, other, :], self.res.at[2 * j + s.c], self.fs.at[j], self.fr.at[j], s.sibling)

    def f6(self, j):
        s = self.spot
        came = self.res.at[2 * j + 1 - s.c]
        remote(came, came, self.fs.at[j], self.fr.at[j], s.sibling).wait_recv()


class Everyone(Posted):
    @staticmethod
    def scratch(count):
        D = pltpu.SemaphoreType.DMA
        return [D((count,)), D((count,))]

    def __init__(self, spot, board, refs):
        self.spot, self.board = spot, board
        self.send_sem, self.recv_sem = refs

    def post(self, source):
        s = self.spot
        def one(k, other, device):
            remote(source(other), self.board.at[s.me], self.send_sem.at[k], self.recv_sem.at[k], device).start()
        s.others(one)

    def collect(self, own):
        s = self.spot
        def one(k, other, device):
            came = self.board.at[lax.rem(s.me + s.count - k, s.count)]
            remote(came, came, self.send_sem.at[k], self.recv_sem.at[k], device).wait()
        s.others(one)
        self.board[s.me] = own


FORWARD_ORDER = (
    "e10", "e00", "e11", "e01", "e12", "e13", "e14", "e15", "v", "n0", "n1", "e20", "e02", "n2", "e21", "e30", "n3", "e22", "e03",
    "e31", "e40", "e32", "e23", "e04", "e41", "e50", "e05", "p0", "e51", "p1", "e24", "e42", "a0", "e33", "a1", "a2", "e52", "a3",
    "p2", "e34", "a4", "e25", "e43", "a5", "a6", "a7", "e53", "m", "e44", "r", "e54", "h", "e35", "g", "X", "e45", "Y", "e55",
)
BACKWARD_ORDER = (
    "h", "g1", "f30", "s", "f21", "g2", "f40", "f31", "m", "a0", "a1", "a2", "f22", "a3", "g3", "f32", "f50", "a4", "a5", "a6",
    "f41", "a7", "f23", "r0", "g4", "r1", "f33", "f42", "f51", "f24", "g5", "f52", "r2", "f43", "r3", "f34", "f25", "n03", "f53",
    "f44", "f35", "n34", "f45", "f54",
)


def place(kind, count):
    return [pl.BlockSpec(memory_space=kind)] * count


def load(src, dst, sem):
    copy = pltpu.make_async_copy(src, dst, sem)
    copy.start()
    return copy


def window_tile(per, owner):
    return lax.div(per * owner, 128)


def forward_kernel(layers, *refs):
    joined = layers > 0
    refs = list(refs)
    take = lambda n: [refs.pop(0) for _ in range(n)]
    x, dy, seg_in, start_in, rope = take(5)
    owned = take(5) if joined else take(2)
    turned, qkv_out, att_out, r1_out, dg_out, e2_out, act_out, stats_out, bsum_out, down_out = take(10)
    weights_out, vec_out = take(2) if joined else (None, None)
    full, xv, dyv, h1, tt, qkv, att, mix, r1, dg, stats, bsum, seg, start, sem, dsem = take(16)
    fetch = [load(x, xv, sem.at[0]), load(dy, dyv, sem.at[1])]
    bsum[...] = jnp.zeros_like(bsum)
    seg[...] = turn_table(seg_in)
    start[...] = turn_table(start_in)
    if joined:
        spot = Spot(layers)
        board, canvas, vec, wsem, came, csend, crecv = take(7)
        everyone = Everyone(spot, board, take(2))
        gather = Gather(spot, full, owned[:4], refs)
        window = owned[4]
        weight = lambda j: full[j].reshape(h1.shape[1], h1.shape[1])
        spot.meet()
        for j in range(STAGES):
            gather.prepare(j)
        everyone.post(lambda other: window)
        canvas[...] = jnp.zeros_like(canvas)
    else:
        vec = owned[1]
        weight = lambda j: full[j]
        fetch.append(load(owned[0], full, sem.at[2]))
    f = Forward(weight, (xv, dyv, seg, start, vec, rope, h1, tt, qkv, att, mix, r1, dg, stats, bsum))
    blocks = f.tokens // TOK
    groups = f.tokens // GROUP
    outs = {}

    def vectors():
        everyone.collect(window[...])
        share = 4 * f.width // spot.count

        def put(owner, carry):
            canvas[pl.ds(window_tile(share, owner), 2)] += board[owner]
            return carry
        lax.fori_loop(0, spot.count, put, 0)
        tiles = f.width // 128
        for row in range(4):
            for tile in range(tiles):
                vec[row : row + 1, 128 * tile : 128 * (tile + 1)] = canvas[row * tiles + tile]

    def norm(i):
        if i == 0:
            fetch[0].wait()
            fetch[1].wait()
        f.norms(i * blocks // 4, (i + 1) * blocks // 4)
        if i == 3:
            outs["h1"] = load(tt.at[0], turned.at[0], sem.at[3])
            outs["e2"] = load(dyv, e2_out, sem.at[4])

    def attend(i):
        f.attend(i // 4, i % 4 * groups // 4, (i % 4 + 1) * groups // 4)

    def turn_mix():
        outs["qkv"] = load(qkv, qkv_out, sem.at[5])
        outs["att"] = load(att, att_out, sem.at[6])
        f.mix_turned(1)
        outs["o"] = load(tt.at[1], turned.at[1], sem.at[7])

    def residual():
        outs.pop("h1").wait()
        f.residual(0)
        outs["h2"] = load(tt.at[0], turned.at[2], sem.at[3])
        outs["r1"] = load(r1, r1_out, sem.at[8])

    def hidden():
        outs.pop("o").wait()
        f.hidden(1)
        outs["dg"] = load(dg, dg_out, sem.at[9])
        outs["act"] = load(mix, act_out, sem.at[7])

    def down_grad():
        outs.pop("qkv").wait()
        f.down_grad(1)

    down_chunks = f.width // TOK

    def exchange(i):
        return remote(f.chunk(i).at[:, unit_cols(1 - spot.c)], came.at[i], csend.at[i], crecv.at[i], spot.sibling)

    def give():
        for i in range(down_chunks):
            exchange(i).start()

    def receive():
        for i in range(down_chunks):
            exchange(i).wait()
            came[i] = came[i] + f.chunk(i)[:, unit_cols(spot.c)]
            outs["d", i] = load(came.at[i], down_out.at[i], dsem.at[i])

    steps = {"v": vectors, "n": norm, "p": f.project, "a": attend, "m": turn_mix, "r": residual, "h": hidden, "g": down_grad,
             "X": give, "Y": receive}
    if joined:
        for name in FORWARD_ORDER:
            if name in steps:
                steps[name]()
            elif name[0] == "e":
                j = int(name[2])
                getattr(gather, name[:2])(j)
                if name[1] == "5":
                    outs["w", j] = load(full.at[j], weights_out.at[j], wsem.at[j])
            else:
                steps[name[0]](int(name[1]))
    else:
        for i in range(4):
            norm(i)
        fetch[2].wait()
        for j in range(3):
            f.project(j)
        for i in range(8):
            attend(i)
        for name in "mrhg":
            steps[name]()
        for i in range(down_chunks):
            outs["d", i] = load(f.chunk(i), down_out.at[i], dsem.at[i])
    outs["stats"] = load(stats, stats_out, sem.at[10])
    outs["bsum"] = load(bsum, bsum_out, sem.at[11])
    if joined:
        outs["vec"] = load(vec, vec_out, sem.at[2])
    for copy in outs.values():
        copy.wait()
    if joined:
        gather.all_sent()


def forward(layers, rows, x, dy, seg, start, rope, owned):
    tokens, width = x.shape
    S = jax.ShapeDtypeStruct
    V = pltpu.VMEM
    D = pltpu.SemaphoreType.DMA
    joined = layers > 0
    shape = (STAGES, layers, 4, rows, width) if joined else (STAGES, width, width)
    chunks = width // TOK
    outs = [S((3, width, tokens), BF), S((3, tokens, width), BF), S((2, tokens, 4 * SPAN), BF),
            S((tokens, width), F32), S((tokens, width), BF), S((tokens, width), BF), S((tokens, width), BF), S((tokens, 128), F32), S((8, width), F32),
            S((chunks, TOK, COL if joined else width), BF)]
    scratch = [V(shape, BF), V((tokens, width), BF), V((tokens, width), BF), V((tokens, width), BF), V((2, width, tokens), BF),
               V((3, tokens, width), BF), V((2, tokens, 4 * SPAN), BF), V((tokens, width), BF), V((tokens, width), F32),
               V((tokens, width), BF), V((tokens, 128), F32), V((8, width), F32), V((tokens // PATCHES, PATCHES), F32), V((tokens // PATCHES, PATCHES), F32), D((12,)), D((chunks,))]
    if joined:
        outs += [S(shape, BF), S((8, width), F32)]
        count = 8 * layers
        scratch += [V((count, 2, 1, 128), F32), V((4 * width // 128 + 8, 1, 128), F32), V((8, width), F32), D((STAGES,)),
                    V((chunks, TOK, COL), BF), D((chunks,)), D((chunks,))]
        scratch += Everyone.scratch(count) + Gather.scratch(layers, rows)
    return pl.pallas_call(
        functools.partial(forward_kernel, layers),
        out_shape=outs,
        in_specs=place(pl.ANY, 2) + place(pltpu.VMEM, 3) + (place(pl.ANY, 4) if joined else place(pl.ANY, 1)) + place(pltpu.VMEM, 1),
        out_specs=place(pl.ANY, len(outs)),
        scratch_shapes=scratch,
        compiler_params=pltpu.CompilerParams(vmem_limit_bytes=VMEM_LIMIT, **(dict(collective_id=0, has_side_effects=True) if joined else {})),
        name="layer_forward",
    )(x, dy, seg, start, rope, *owned)


def backward_kernel(layers, *refs):
    joined = layers > 0
    refs = list(refs)
    take = lambda n: [refs.pop(0) for _ in range(n)]
    x, dy, start_in, rope, vec, turned, qkv_in, att_in, r1_in, dg_in, e2_in, act_in, stats_in, bsum_in, down_in, gw = take(16)
    out, dx_out, grad_out, small_out = take(4)
    norm_out = take(1)[0] if joined else None
    wbuf, part, lt, ea, eb, qkv, att, stats, bsum, rblk, bblk, hold, start, sem, ssem, osem, psem = take(17)
    start[...] = turn_table(start_in)

    def weights(j, slot, s):
        return load(gw.at[j], wbuf.at[slot], s)

    if joined:
        spot = Spot(layers)
        board, norms, sheet, note = take(4)
        small_talk = Everyone(spot, board, take(2))
        norm_talk = Everyone(spot, norms, take(2))
        scatter = Scatter(spot, part, refs)
        down = load(down_in, scatter.sum_at(0), psem.at[0])
    e = load(e2_in, ea, sem.at[1])
    w5 = weights(5, 0, sem.at[0])
    d = load(dg_in, eb, sem.at[3])
    bs = load(bsum_in, bsum, sem.at[5])
    s = load(stats_in, stats, sem.at[4])
    l2 = load(turned.at[2], lt.at[0], sem.at[2])
    w4 = weights(4, 1, sem.at[6])
    l1 = load(turned.at[1], lt.at[1], sem.at[7])
    w3 = weights(3, 2, sem.at[8])
    qk = load(qkv_in, qkv, sem.at[9])
    at = load(att_in.at[0], att, sem.at[10])
    b = Backward((wbuf, part, lt, ea, eb, qkv, att, vec, rope, stats, bsum, start, rblk, bblk))
    blocks = b.tokens // TOK
    groups = b.tokens // GROUP
    if joined:
        spot.meet()
        down.wait()
        scatter.corners(0)

    def spill(r):
        return pltpu.make_async_copy(part.at[r % 2], grad_out.at[r - 1], psem.at[r % 2])

    def grad(r):
        if r >= 3:
            if joined:
                scatter.sent(("f1", r - 2))
            else:
                spill(r - 2).wait()
        left, right = {1: (0, lambda cols: eb[:, cols]), 2: (1, lambda cols: ea[:, cols])}.get(r, (0, lambda cols: qkv[r - 3, :, cols]))
        for copy in waits.pop(r, []):
            copy.wait()
        b.weight_grad(r % 2, left, right)
        if joined:
            scatter.f1(r)
        else:
            spill(r).start()
        if r == 1:
            waits[3] = [load(turned.at[0], lt.at[0], sem.at[2])]

    waits = {1: [l2], 2: [l1], "w": []}
    loads = [(r1_in, rblk, ssem.at[0]), (dy, bblk, ssem.at[1])]

    def hidden():
        for copy in (w5, d, e, bs):
            copy.wait()
        b.hidden(0)

    def second_norm():
        w4.wait()
        s.wait()
        b.second_norm(1, loads, hold, 0, blocks)
        waits["w"].append(weights(0, 1, sem.at[6]))

    def mixed():
        w3.wait()
        b.mixed(2)
        waits["w"].append(weights(1, 2, sem.at[8]))
        qk.wait()

    def attend(i):
        if i == 0:
            at.wait()
        if i == 4:
            waits["a"].wait()
        b.attend(i // 4, i % 4 * groups // 4, (i % 4 + 1) * groups // 4)
        if i == 3:
            waits["a"] = load(att_in.at[1], att, sem.at[10])
        if i == 7:
            waits["act"] = load(act_in, eb, sem.at[3])

    def result(i):
        if i == 0:
            waits["act"].wait()
        b.result(0, loads, out, osem, i * blocks // 4, (i + 1) * blocks // 4)
        if i == 3:
            waits["w"].append(weights(2, 0, sem.at[0]))

    def first_norm(low, high):
        if low == 0:
            for copy in waits["w"]:
                copy.wait()
        b.first_norm((1, 2, 0), [(x, bblk, ssem.at[1])], dx_out, osem, rblk, low * blocks // 4, high * blocks // 4)

    for name in BACKWARD_ORDER:
        if name[0] == "f":
            if joined:
                getattr(scatter, name[:2])(int(name[2]))
        elif name[0] in "gar":
            {"g": grad, "a": attend, "r": result}[name[0]](int(name[1]))
        elif name[0] == "n":
            first_norm(int(name[1]), int(name[2]))
        else:
            {"h": hidden, "s": second_norm, "m": mixed}[name]()
    if not joined:
        fin = load(bsum, small_out, sem.at[5])
        for r in range(STAGES - 2, STAGES):
            spill(r).wait()
        fin.wait()
        return
    tiles = b.width // 128
    for row, source in enumerate((3, 2, 1, 0)):
        for tile in range(tiles):
            sheet[row * tiles + tile] = bsum[source : source + 1, 128 * tile : 128 * (tile + 1)]
    share = 4 * b.width // spot.count
    own = lambda owner: sheet.at[pl.ds(window_tile(share, owner), 2)]
    small_talk.post(own)
    small_talk.collect(sheet[pl.ds(window_tile(share, spot.me), 2)])

    def add(owner, carry):
        return carry + board[owner]
    total = lax.fori_loop(0, spot.count, add, jnp.zeros((2, 1, 128), F32))
    first = lax.rem(share * spot.me, 128)
    spots = lax.broadcasted_iota(jnp.int32, (2, 1, 128), 0) * 128 + lax.broadcasted_iota(jnp.int32, (2, 1, 128), 2)
    mine = jnp.where((spots >= first) & (spots < first + share), total, 0.0)
    small_out[...] = mine
    scatter.f5(STAGES - 1)
    for j in range(STAGES):
        scatter.f6(j)
    fin = load(scatter.res, grad_out, sem.at[9])

    def square(unit, carry):
        values = scatter.res[unit]
        return carry + jnp.sum(values * values, 0, keepdims=True)
    squares = lax.fori_loop(0, UNITS, square, jnp.zeros((1, COL), F32))
    value = jnp.sum(squares) + jnp.sum(mine * mine)
    note[...] = jnp.full((8, 128), value, F32)
    norm_talk.post(lambda other: note)
    norm_talk.collect(note[...])
    whole = lax.fori_loop(0, spot.count, lambda owner, carry: carry + norms[owner], jnp.zeros((8, 128), F32))
    norm_out[...] = jnp.sqrt(whole)
    fin.wait()
    scatter.all_sent()


def backward(layers, rows, *args):
    tokens, width = args[0].shape
    S = jax.ShapeDtypeStruct
    V = pltpu.VMEM
    D = pltpu.SemaphoreType.DMA
    joined = layers > 0
    grid = (layers, 4, rows, width) if joined else (width, width)
    outs = [S((tokens, width), F32), S((tokens, width), F32)]
    scratch = [V((3,) + grid, BF), V((2,) + grid, BF), V((2, width, tokens), BF), V((tokens, width), BF), V((tokens, width), BF),
               V((3, tokens, width), BF), V((tokens, 4 * SPAN), BF), V((tokens, 128), F32), V((8, width), F32),
               V((2, TOK, width), F32), V((2, TOK, width), BF), V((TOK, width), F32), V((tokens // PATCHES, PATCHES), F32), D((11,)), D((2, 2)), D((2,)), D((2,))]
    specs = place(pl.ANY, 4)
    if joined:
        count = 8 * layers
        outs += [S((UNITS, rows // 2, COL), F32), S((2, 1, 128), F32), S((8, 128), F32)]
        specs = place(pl.ANY, 3) + place(pltpu.VMEM, 2)
        scratch += [V((count, 2, 1, 128), F32), V((count, 8, 128), F32), V((4 * width // 128 + 8, 1, 128), F32), V((8, 128), F32)]
        scratch += Everyone.scratch(count) + Everyone.scratch(count) + Scatter.scratch(layers, rows)
    else:
        outs += [S((STAGES - 1, width, width), BF), S((8, width), F32)]
    return pl.pallas_call(
        functools.partial(backward_kernel, layers),
        out_shape=outs,
        in_specs=place(pl.ANY, 2) + place(pltpu.VMEM, 3) + place(pl.ANY, 11),
        out_specs=specs,
        scratch_shapes=scratch,
        compiler_params=pltpu.CompilerParams(vmem_limit_bytes=VMEM_LIMIT, **(dict(collective_id=1, has_side_effects=True) if joined else {})),
        name="layer_backward",
    )(*args)


def adam_update(master, gradient, first, second, clip_scale, weight_decay, step_rate):
    gradient = gradient * clip_scale
    first_new = beta_first * first + (1.0 - beta_first) * gradient
    second_new = beta_second * second + (1.0 - beta_second) * gradient * gradient
    fix_first = 1.0 - beta_first**STEP
    fix_second = 1.0 - beta_second**STEP
    update_step = (
        first_new / fix_first / (jnp.sqrt(second_new / fix_second) + eps_adam)
        + weight_decay * master
    )
    master_new = master - step_rate * update_step
    return (master_new, first_new, second_new)


def adam_kernel(*refs):
    refs = list(refs)
    take = lambda n: [refs.pop(0) for _ in range(n)]
    sources, large = take(14), take(2)
    results, norm_out, large_out = take(16), take(1)[0], take(2)
    held, made = take(14), take(16)
    carried, in_sem, out_sem, large_sem = refs
    copies = [load(src, dst, in_sem.at[i]) for i, (src, dst) in enumerate(zip(sources, held))]
    outs = []
    piece = large[0].shape[0] // 4
    parts = [(i, at, pl.ds(piece * at, piece)) for i in range(2) for at in range(4)]
    passing = [load(large[i].at[rows, :], carried.at[i, rows, :], large_sem.at[i, at]) for i, at, rows in parts]
    for copy in copies[:2]:
        copy.wait()
    grads, norm = held[:2]
    norm_out[...] = norm[0:1, 0:1]
    clip_scale = jnp.minimum(1.0, clip_limit / (norm[0:1, 0:1] + 1e-06))
    for i in range(4):
        mine = [2 + i, 6 + i, 10 + i]
        for at in mine:
            copies[at].wait()
        for at, unit in enumerate(COLUMNS[i]):
            cols = slice(COL * at, COL * (at + 1))
            new = adam_update(*(held[m][:, cols] for m in mine[:1]), grads[unit], *(held[m][:, cols] for m in mine[1:]), clip_scale, decay_rate, learn_rate)
            for kind, value in enumerate((*new, new[0].astype(BF))):
                made[4 * kind + i][:, cols] = value
        outs += [load(made[4 * kind + i], results[4 * kind + i], out_sem.at[4 * kind + i]) for kind in range(4)]
    for copy, (i, at, rows) in zip(passing, parts):
        copy.wait()
        outs.append(load(carried.at[i, rows, :], large_out[i].at[rows, :], large_sem.at[i, at]))
    for copy in outs:
        copy.wait()


def adam_matrices(grads, norm, masters, firsts, seconds, large):
    shapes = [jax.ShapeDtypeStruct(m.shape, F32) for m in masters] * 3 + [jax.ShapeDtypeStruct(m.shape, BF) for m in masters]
    ins = (grads, norm, *masters, *firsts, *seconds)
    room = lambda arrays: [pltpu.VMEM(a.shape, a.dtype) for a in arrays]
    made = pl.pallas_call(
        adam_kernel,
        out_shape=[*shapes, jax.ShapeDtypeStruct((1, 1), F32), *(jax.ShapeDtypeStruct(m.shape, F32) for m in large)],
        in_specs=place(pl.ANY, 16),
        out_specs=place(pl.ANY, 16) + place(pltpu.VMEM, 1) + place(pl.ANY, 2),
        scratch_shapes=[*room(ins), *room(shapes), pltpu.VMEM((2,) + large[0].shape, F32), pltpu.SemaphoreType.DMA((14,)), pltpu.SemaphoreType.DMA((16,)), pltpu.SemaphoreType.DMA((2, 4))],
        compiler_params=pltpu.CompilerParams(vmem_limit_bytes=VMEM_LIMIT),
        name="adam",
    )(*ins, *large)
    return [made[4 * i : 4 * i + 4] for i in range(4)], made[16], made[17:]


def stage_columns(full_in, full_out, full_up, full_down):
    parts = [full_in[:, 2 * COL * (u % 3) + COL * (u // 3) :][:, :COL] for u in range(6)]
    pairs = [jnp.concatenate(parts[2 * i : 2 * i + 2], 1) for i in range(3)]
    return jnp.stack([*pairs, full_out, full_up, full_down])


COLUMNS = ((6, 9, 7, 10, 8, 11), (4, 5), (2, 3), (0, 1))


def by_matrix(units):
    return [jnp.concatenate([units[i] for i in at], 1) for at in COLUMNS]


def turned_down(kept, joined, layers, rows):
    down = kept[-1].reshape(layers, 4, rows, COL) if joined else kept[-1]
    return (*kept[:-1], down)


def shards(
    inputs,
    segments,
    starts,
    out_grad,
    proj_in,
    proj_out,
    up_proj,
    down_proj,
    gains_biases,
    first_in,
    first_out,
    first_up,
    first_down,
    first_small,
    second_in,
    second_out,
    second_up,
    second_down,
    second_small,
):
    axes = ("wide", "narrow")
    wide, narrow = lax.axis_size("wide"), lax.axis_size("narrow")
    tokens, width = inputs.shape
    share = gains_biases.shape[0]
    me = lax.axis_index("wide") * narrow + lax.axis_index("narrow")
    rows = width // wide
    joined = narrow == 2 and wide % 4 == 0 and rows % 16 == 0 and share == 160
    layers = wide // 4 if joined else 0
    rope = jnp.asarray(rope_tables())
    small_low = lax.reduce_precision(gains_biases, 8, 7)
    if joined:
        shift = lax.rem(share * me, 128)
        window = lax.dynamic_slice(jnp.pad(small_low, (96, 96)), (96 - shift,), (256,)).reshape(2, 1, 128)
        *kept, weights, vec = forward(layers, rows, inputs, out_grad, segments.T, starts.T, rope, (proj_in, proj_out, up_proj, down_proj, window))
    else:
        gathered = [lax.all_gather(m.astype(BF), axes, axis=0, tiled=True) for m in (proj_in, proj_out, up_proj, down_proj)]
        weights = stage_columns(*gathered)
        vec = lax.all_gather(small_low, axes, axis=0, tiled=True).reshape(4, width)
        vec = jnp.pad(vec, ((0, 4), (0, 0)))
        kept = forward(layers, rows, inputs, out_grad, segments.T, starts.T, rope, (weights, vec))
    made = backward(layers, rows, inputs, out_grad, starts.T, rope, vec, *turned_down(kept, joined, layers, rows), weights)
    block_out, input_grad = made[:2]
    mats, firsts, seconds = (proj_in, proj_out, up_proj, down_proj), (first_in, first_out, first_up, first_down), (second_in, second_out, second_up, second_down)
    if joined:
        shard_small = lax.dynamic_slice(made[3].reshape(256), (shift,), (share,))
        mat_news, grad_norm, (block_out, input_grad) = adam_matrices(made[2], made[4], mats, firsts, seconds, made[:2])
        grad_norm = grad_norm.reshape(())
        clip_scale = jnp.minimum(1.0, clip_limit / (grad_norm + 1e-06))
    else:
        stages = jnp.concatenate([kept[-1].reshape(1, width, width), made[2]], 0).astype(F32)
        full_grads = by_matrix([stages[i // 2][:, COL * (i % 2) :][:, :COL] for i in range(UNITS)])
        scatter = lambda m: lax.psum_scatter(m, axes, scatter_dimension=0, tiled=True)
        grads = [scatter(m) for m in full_grads]
        shard_small = scatter(jnp.concatenate([made[3][3], made[3][2], made[3][1], made[3][0]]))
        squares = sum(jnp.sum(m * m) for m in (*grads, shard_small))
        grad_norm = jnp.sqrt(lax.psum(squares, axes))
        clip_scale = jnp.minimum(1.0, clip_limit / (grad_norm + 1e-06))
        each = [adam_update(*four, clip_scale, decay_rate, learn_rate) for four in zip(mats, grads, firsts, seconds)]
        mat_news = [[new[i] for new in each] for i in range(3)]
        mat_news.append([m.astype(BF) for m in mat_news[0]])
    small_new = adam_update(gains_biases, shard_small, first_small, second_small, clip_scale, 0.0, small_rate)
    small_news = (*small_new, small_new[0].astype(BF))
    return (
        block_out,
        input_grad,
        grad_norm,
        *(part for mat, small in zip(mat_news, small_news) for part in (*mat, small)),
    )


def solution(mesh):
    split, flat = P(("wide", "narrow"), None), P(("wide", "narrow"))
    state = (split, split, split, split, flat)
    return jax.shard_map(
        shards,
        mesh=mesh,
        in_specs=(split,) * 4 + state * 3,
        out_specs=(split, split, P()) + state * 4,
        check_vma=False,
    )
```

```python
import functools
import math

import jax
import jax.numpy as jnp
import numpy as np
from jax import lax
from jax.experimental import pallas as pl
from jax.experimental.pallas import tpu as pltpu
from jax.sharding import PartitionSpec as P

HEADS = 16
HEAD_DIM = 80
STEP = 5
PATCHES = 16

eps_norm = 1e-05
eps_stat = 1e-05
rope_base = 10000.0
clip_limit = 256.0
learn_rate = 0.03
small_rate = 0.4
decay_rate = 0.1
beta_first = 0.9
beta_second = 0.999
eps_adam = 1e-08

BF = jnp.bfloat16
F32 = jnp.float32
MESH = pl.DeviceIdType.MESH

COL = 640
UNITS = 12
STAGES = 6
SPAN = 256
GROUP = 128
TOK = 256
WIDE_TOK = 512
VMEM_LIMIT = 64 << 20


def lanes(ref_cols):
    return lax.broadcasted_iota(jnp.int32, (1, ref_cols), 1)


def nn(left_in, right_in):
    return lax.dot_general(
        left_in, right_in, (((1,), (0,)), ((), ())), preferred_element_type=F32
    )


def nt(left_in, right_in):
    return lax.dot_general(
        left_in, right_in, (((1,), (1,)), ((), ())), preferred_element_type=F32
    )


def unit_cols(side):
    return pl.ds(pl.multiple_of(COL * side, 128), COL)


def rope_tables():
    half = HEAD_DIM // 2
    inverse = np.float32(rope_base) ** (-np.arange(half, dtype=np.float32) * np.float32(2.0) / np.float32(HEAD_DIM))
    angles = np.arange(PATCHES, dtype=np.float32)[:, None] * inverse.astype(np.float32)[None, :]
    cosine, sine = np.cos(angles), np.sin(angles)
    zero = np.zeros_like(sine)
    heads = COL // HEAD_DIM
    full = [
        np.tile(np.concatenate(pair, 1), (1, heads))
        for pair in ((cosine, cosine), (-sine, zero), (zero, sine))
    ]
    return np.stack(full).astype(np.float32)


def rotate(values_in, table, sign):
    rows = values_in.shape[0]
    ahead = pltpu.roll(values_in, COL - HEAD_DIM // 2, 1)
    behind = pltpu.roll(values_in, HEAD_DIM // 2, 1)
    cube = (rows // PATCHES, PATCHES, COL)
    turn = ahead.reshape(cube) * table[1] + behind.reshape(cube) * table[2]
    straight = values_in.reshape(cube) * table[0]
    return (straight + sign * turn).reshape(rows, COL)


def eye(size):
    row = lax.broadcasted_iota(jnp.int32, (size, size), 0)
    col = lax.broadcasted_iota(jnp.int32, (size, size), 1)
    return row == col


def to_column(row_in, same):
    return jnp.sum(jnp.where(same, row_in, 0.0), 1, keepdims=True)


def to_row(column_in, same):
    return jnp.sum(jnp.where(same, column_in, 0.0), 0, keepdims=True)


def per_token(table):
    rows = table.shape[0]
    size = rows * PATCHES
    wide = jnp.broadcast_to(table.astype(F32)[:, None, :], (rows, PATCHES, PATCHES)).reshape(size, PATCHES)
    patch = lax.rem(lax.broadcasted_iota(jnp.int32, (size, PATCHES), 0), PATCHES)
    hit = lax.broadcasted_iota(jnp.int32, (size, PATCHES), 1) == patch
    return jnp.sum(jnp.where(hit, wide, 0.0), 1, keepdims=True)


def turn_table(table):
    rows = table.shape[1]
    same = jnp.where(eye(rows), 1.0, 0.0).astype(BF)
    return nt(same, table[...].astype(F32).astype(BF))


def context_mask(start_table):
    start_col = per_token(start_table).astype(jnp.int32)
    size = start_col.shape[0]
    row = lax.broadcasted_iota(jnp.int32, (size, size), 0)
    col = lax.broadcasted_iota(jnp.int32, (size, size), 1)
    return col == lax.div(row, PATCHES) * PATCHES + start_col


def pair_masks(pair):
    lane = lanes(SPAN)
    low = 160 * pair - 128 * (160 * pair // 128)
    return (
        (lane >= low) & (lane < low + HEAD_DIM),
        (lane >= low + HEAD_DIM) & (lane < low + 2 * HEAD_DIM),
    )


def both_heads(window, masks):
    zero = jnp.zeros_like(window)
    return jnp.concatenate([jnp.where(masks[0], window, zero), jnp.where(masks[1], window, zero)], 0)


def turn_pair(pair_in):
    return jnp.concatenate([pair_in[:, :GROUP].T, pair_in[:, GROUP:].T], 1)


def attention_bias(seg_table):
    row = lax.broadcasted_iota(jnp.int32, (GROUP, GROUP), 0)
    col = lax.broadcasted_iota(jnp.int32, (GROUP, GROUP), 1)
    seg_col = per_token(seg_table)
    seg_row = to_row(seg_col, row == col)
    allowed = (lax.div(row, PATCHES) == lax.div(col, PATCHES)) & (row <= col) & (seg_col == seg_row)
    bias = jnp.where(allowed, 0.0, -1e30)
    return jnp.concatenate([bias, bias], 1)


def head_window(qkv, unit, rows, pair):
    low = COL * (unit % 2) + 128 * (160 * pair // 128)
    return qkv[unit // 2, rows, low : low + SPAN]


def spread_windows(parts):
    tiles = []
    for tile in range(5):
        total = None
        for pair in (tile - 1, tile):
            if 0 <= pair < 4:
                piece = parts[pair][:, 128 * (tile - pair) : 128 * (tile - pair) + 128]
                total = piece if total is None else total + piece
        tiles.append(total)
    return jnp.concatenate(tiles, 1)


class Forward:
    def __init__(self, weight, refs):
        self.weight = weight
        (self.xv, self.dyv, self.seg, self.start, self.vec, self.rope, self.h1, self.tt, self.qkv, self.att,
         self.mix, self.r1, self.dg, self.stats, self.bsum) = refs
        self.tokens = self.xv.shape[0]
        self.width = self.xv.shape[1]

    def blocks(self, body, low=0, high=None):
        def step(i, carry):
            body(pl.multiple_of(i * TOK, TOK), i)
            return carry
        lax.fori_loop(low, self.tokens // TOK if high is None else high, step, 0)

    def norms(self, low, high):
        width = self.width
        gain = self.vec[0:1, :]

        def body(at, i):
            rows = pl.ds(at, TOK)
            same = eye(TOK)
            x = self.xv[rows, :].astype(F32)
            mean = jnp.sum(x, 1, keepdims=True) * (1.0 / width)
            off = x - mean
            spread = jnp.sqrt(jnp.sum(off * off, 1, keepdims=True) * (1.0 / width) + eps_stat)
            mask = context_mask(self.start[pl.ds(i * (TOK // PATCHES), TOK // PATCHES), :])
            mu = jnp.sum(jnp.where(mask, to_row(mean, same), 0.0), 1, keepdims=True)
            sigma = jnp.sum(jnp.where(mask, to_row(spread, same), 0.0), 1, keepdims=True)
            z = (x - mu) / sigma
            scale = lax.rsqrt(jnp.sum(z * z, 1, keepdims=True) * (1.0 / width) + eps_norm)
            h1 = (z * scale * gain).astype(BF)
            self.h1[rows, :] = h1
            self.tt[0, :, rows] = h1.T
            dy = self.dyv[rows, :].astype(F32)
            low = (dy * sigma).astype(BF)
            self.dyv[rows, :] = low
            self.bsum[0:1, :] += jnp.sum(low.astype(F32), 0, keepdims=True)
            self.stats[rows, 0:1] = mu
            self.stats[rows, 1:2] = sigma
            self.stats[rows, 2:3] = mean
            self.stats[rows, 3:4] = spread
            self.stats[rows, 4:5] = scale
            self.stats[rows, 6:7] = jnp.sum(dy, 1, keepdims=True)

        self.blocks(body, low, high)

    def project(self, stage):
        def step(i, carry):
            rows = pl.ds(pl.multiple_of(i * WIDE_TOK, WIDE_TOK), WIDE_TOK)
            made = nn(self.h1[rows, :], self.weight(stage))
            for side in range(2):
                cols = slice(COL * side, COL * (side + 1))
                part = made[:, cols]
                if (2 * stage + side) % 3 < 2:
                    part = rotate(part, self.rope, 1.0)
                self.qkv[stage, rows, cols] = part.astype(BF)
            return carry

        lax.fori_loop(0, self.tokens // WIDE_TOK, step, 0)

    def attend(self, half, low=0, high=None):
        scale = 1.0 / math.sqrt(HEAD_DIM)

        def step(g, carry):
            rows = pl.ds(pl.multiple_of(g * GROUP, GROUP), GROUP)
            bias = attention_bias(self.seg[pl.ds(g * (GROUP // PATCHES), GROUP // PATCHES), :])
            look = lambda kind, pair: head_window(self.qkv, 3 * half + kind, rows, pair)
            scores = [
                nt(look(1, pair), both_heads(look(0, pair), pair_masks(pair)))
                for pair in range(4)
            ]
            probs = []
            for pair in range(4):
                own = scores[pair] * scale + bias
                expo = jnp.exp(own - jnp.max(own, 0, keepdims=True))
                prob = (expo * (1.0 / jnp.sum(expo, 0, keepdims=True))).astype(BF)
                self.att[half, rows, SPAN * pair : SPAN * (pair + 1)] = prob
                probs.append(prob)
            parts = [
                nn(turn_pair(probs[pair]), both_heads(look(2, pair), pair_masks(pair)))
                for pair in range(4)
            ]
            self.mix[rows, COL * half : COL * (half + 1)] = spread_windows(parts).astype(BF)
            return carry

        lax.fori_loop(low, self.tokens // GROUP if high is None else high, step, 0)

    def mix_turned(self, slot):
        def body(at, i):
            rows = pl.ds(at, TOK)
            self.tt[slot, :, rows] = self.mix[rows, :].T

        self.blocks(body)

    def residual(self, slot):
        width = self.width
        gain = self.vec[1:2, :]

        def body(at, i):
            rows = pl.ds(at, TOK)
            mix = self.mix[rows, :]
            made = nn(mix, self.weight(3))
            z = (self.xv[rows, :].astype(F32) - self.stats[rows, 0:1]) / self.stats[rows, 1:2]
            r1 = z + made
            scale = lax.rsqrt(jnp.sum(r1 * r1, 1, keepdims=True) * (1.0 / width) + eps_norm)
            self.stats[rows, 5:6] = scale
            self.r1[rows, :] = r1
            h2 = (r1 * scale * gain).astype(BF)
            self.h1[rows, :] = h2
            self.tt[slot, :, rows] = h2.T

        self.blocks(body)

    def hidden(self, slot):
        bias = self.vec[2:3, :]
        c0 = math.sqrt(2.0 / math.pi)

        def body(at, i):
            rows = pl.ds(at, TOK)
            made = nn(self.h1[rows, :], self.weight(4))
            for half in range(2):
                cols = slice(COL * half, COL * (half + 1))
                u = made[:, cols] + bias[:, cols]
                square = u * u
                bend = jnp.tanh(c0 * (u + 0.044715 * u * square))
                act = (0.5 * u * (1.0 + bend)).astype(BF)
                slope = 0.5 * (1.0 + bend) + (0.5 * c0) * u * (1.0 - bend * bend) * (1.0 + (3 * 0.044715) * square)
                self.dg[rows, cols] = slope.astype(BF)
                self.mix[rows, cols] = act
                self.tt[slot, cols, rows] = act.T

        self.blocks(body)

    def chunk(self, i):
        per = self.tokens // TOK
        return self.qkv.at[lax.div(i, per), pl.ds(pl.multiple_of(TOK * lax.rem(i, per), TOK), TOK), :]

    def down_grad(self, left, after=lambda i: None):
        def step(i, carry):
            rows = pl.ds(pl.multiple_of(i * TOK, TOK), TOK)
            self.chunk(i)[...] = nn(self.tt[left, rows, :], self.dyv[...]).astype(BF)
            after(i)
            return carry
        lax.fori_loop(0, self.width // TOK, step, 0)


class Backward:
    def __init__(self, refs):
        (self.wbuf, self.part, self.lt, self.ea, self.eb, self.qkv, self.att, self.vec, self.rope,
         self.stats, self.bsum, self.start, self.rblk, self.bblk) = refs
        self.tokens, self.width = self.ea.shape

    def blocks(self, body, low=0, high=None):
        def step(i, carry):
            body(pl.multiple_of(i * TOK, TOK), i)
            return carry
        lax.fori_loop(low, self.tokens // TOK if high is None else high, step, 0)

    def weight(self, slot):
        return self.wbuf[slot].reshape(self.width, self.width)

    def weight_grad(self, slot, left, right, after=lambda i: None):
        part = self.part.at[slot]
        if len(part.shape) == 4:
            tall = 2 * part.shape[1] * part.shape[2]
            for i in range(self.width // tall):
                rows = pl.ds(i * tall, tall)
                for low in range(0, self.width, 512):
                    cols = slice(low, min(low + 512, self.width))
                    made = nn(self.lt[left, rows, :], right(cols))
                    part[pl.ds(2 * i, 2), :, :, cols] = made.astype(BF).reshape((2,) + part.shape[1:3] + (made.shape[1],))
                after(i)
            return
        tall = TOK

        def step(i, carry):
            rows = pl.ds(pl.multiple_of(i * tall, tall), tall)
            part[rows, :] = nn(self.lt[left, rows, :], right(slice(None))).astype(BF)
            return carry
        lax.fori_loop(0, self.width // tall, step, 0)

    def hidden(self, slot):
        def body(at, i):
            rows = pl.ds(at, TOK)
            low = (nt(self.ea[rows, :], self.weight(slot)) * self.eb[rows, :].astype(F32)).astype(BF)
            self.eb[rows, :] = low
            self.bsum[1:2, :] += jnp.sum(low.astype(F32), 0, keepdims=True)

        self.blocks(body)

    def stream(self, body, loads, low=0, high=None):
        count = self.tokens // TOK
        high = count if high is None else high

        def copies(i):
            slot = lax.rem(i, 2)
            rows = pl.ds(pl.multiple_of(i * TOK, TOK), TOK)
            return [pltpu.make_async_copy(src.at[rows, :], buf.at[slot], sem.at[slot]) for src, buf, sem in loads]

        if low == 0:
            for cp in copies(0):
                cp.start()

        def inner(at, i):
            @pl.when(i + 1 < count)
            def _():
                for cp in copies(i + 1):
                    cp.start()
            for cp in copies(i):
                cp.wait()
            body(at, i, lax.rem(i, 2))

        self.blocks(inner, low, high)

    def result(self, slot, loads, out, out_sem, low, high):
        bias = self.vec[3:4, :]
        count = self.tokens // TOK

        def copy(i):
            turn = lax.rem(i, 2)
            return pltpu.make_async_copy(self.rblk.at[turn], out.at[pl.ds(pl.multiple_of(i * TOK, TOK), TOK), :], out_sem.at[turn])

        def fetch(i):
            turn = lax.rem(i, 2)
            rows = pl.ds(pl.multiple_of(i * TOK, TOK), TOK)
            return [pltpu.make_async_copy(src.at[rows, :], buf.at[turn], sem.at[turn]) for src, buf, sem in loads]

        if low == 0:
            for cp in fetch(0):
                cp.start()

        def body(at, i):
            rows = pl.ds(at, TOK)
            turn = lax.rem(i, 2)

            @pl.when(i >= 1)
            def _():
                copy(i - 1).wait()

            @pl.when(i + 1 < count)
            def _():
                for cp in fetch(i + 1):
                    cp.start()

            act = self.eb[rows, :]
            made = nn(act, self.weight(slot))
            for cp in fetch(i):
                cp.wait()
            r2 = self.rblk[turn] + (made + bias)
            self.rblk[turn] = r2 * self.stats[rows, 1:2] + self.stats[rows, 0:1]
            copy(i).start()
            self.stats[rows, 7:8] = jnp.sum(self.bblk[turn].astype(F32) * r2, 1, keepdims=True)

        self.blocks(body, low, high)
        if high == count:
            copy(count - 1).wait()

    def second_norm(self, slot, loads, hold, low, high):
        width = self.width
        gain = self.vec[1:2, :]

        def body(at, i, turn):
            hold[...] = nt(self.eb[pl.ds(at, TOK), :], self.weight(slot))

            def step(c, carry):
                inside = pl.multiple_of(c * GROUP, GROUP)
                rows, local = pl.ds(pl.multiple_of(at + inside, GROUP), GROUP), pl.ds(inside, GROUP)
                dh2 = hold[local, :]
                scale = self.stats[rows, 5:6]
                n2 = self.rblk[turn, local, :] * scale
                self.bsum[2:3, :] += jnp.sum(dh2 * n2, 0, keepdims=True)
                dn = dh2 * gain
                inner = jnp.sum(dn * n2, 1, keepdims=True) * (1.0 / width)
                dr1 = self.bblk[turn, local, :].astype(F32) * self.stats[rows, 1:2] + scale * (dn - n2 * inner)
                self.ea[rows, :] = dr1.astype(BF)
                return carry
            lax.fori_loop(0, TOK // GROUP, step, 0)

        self.stream(body, loads, low, high)

    def mixed(self, slot):
        def body(at, i):
            rows = pl.ds(at, TOK)
            self.eb[rows, :] = nt(self.ea[rows, :], self.weight(slot)).astype(BF)

        self.blocks(body)

    def attend(self, half, low=0, high=None):
        scale = 1.0 / math.sqrt(HEAD_DIM)

        def step(g, carry):
            rows = pl.ds(pl.multiple_of(g * GROUP, GROUP), GROUP)
            starts = [128 * (160 * pair // 128) for pair in range(4)]
            look = lambda kind, pair: head_window(self.qkv, 3 * half + kind, rows, pair)
            masks = [pair_masks(pair) for pair in range(4)]
            dmix = [both_heads(self.eb[rows, pl.ds(COL * half + starts[i], SPAN)], masks[i]) for i in range(4)]
            probs = [self.att[rows, SPAN * i : SPAN * (i + 1)] for i in range(4)]
            das = [nt(look(2, i), dmix[i]) for i in range(4)]
            dss = []
            for i in range(4):
                p32 = probs[i].astype(F32)
                weighed = p32 * das[i]
                dss.append((weighed - p32 * jnp.sum(weighed, 0, keepdims=True)).astype(BF))
            dvs = [nn(probs[i], dmix[i]) for i in range(4)]
            dks = [nn(dss[i], both_heads(look(0, i), masks[i])) for i in range(4)]
            dqs = [nn(turn_pair(dss[i]), both_heads(look(1, i), masks[i])) for i in range(4)]
            dq = rotate(spread_windows(dqs) * scale, self.rope, -1.0)
            dk = rotate(spread_windows(dks) * scale, self.rope, -1.0)
            for kind, made in enumerate((dq, dk, spread_windows(dvs))):
                unit = 3 * half + kind
                self.qkv[unit // 2, rows, COL * (unit % 2) : COL * (unit % 2 + 1)] = made.astype(BF)
            return carry

        lax.fori_loop(low, self.tokens // GROUP if high is None else high, step, 0, unroll=True)

    def first_norm(self, slots, loads, out, out_sem, turns, low, high):
        width = self.width
        gain = self.vec[0:1, :]
        count = self.tokens // TOK

        def copy(i):
            slot = lax.rem(i, 2)
            return pltpu.make_async_copy(turns.at[slot], out.at[pl.ds(pl.multiple_of(i * TOK, TOK), TOK), :], out_sem.at[slot])

        def piece(at, inside, turn):
            rows = pl.ds(pl.multiple_of(at + inside, GROUP), GROUP)
            local = pl.ds(inside, GROUP)
            same = eye(GROUP)
            dh1 = turns[turn, local, :]
            mu, sigma = self.stats[rows, 0:1], self.stats[rows, 1:2]
            mean, spread = self.stats[rows, 2:3], self.stats[rows, 3:4]
            scale = self.stats[rows, 4:5]
            inv = 1.0 / sigma
            x = self.bblk[turn, local, :].astype(F32)
            z = (x - mu) * inv
            n1 = z * scale
            self.bsum[3:4, :] += jnp.sum(dh1 * n1, 0, keepdims=True)
            dn = dh1 * gain
            inner = jnp.sum(dn * n1, 1, keepdims=True) * (1.0 / width)
            dz = scale * (dn - n1 * inner) + self.ea[rows, :].astype(F32)
            dmu = self.stats[rows, 6:7] - jnp.sum(dz, 1, keepdims=True) * inv
            dsigma = self.stats[rows, 7:8] - jnp.sum(dz * z, 1, keepdims=True) * inv
            per = GROUP // PATCHES
            mask = context_mask(self.start[pl.ds(pl.multiple_of(lax.div(at + inside, PATCHES), per), per), :])
            dmean = to_column(jnp.sum(jnp.where(mask, dmu, 0.0), 0, keepdims=True), same)
            dspread = to_column(jnp.sum(jnp.where(mask, dsigma, 0.0), 0, keepdims=True), same)
            turns[turn, local, :] = dz * inv + (dmean * (1.0 / width) + (x - mean) * (dspread * (1.0 / width) / spread))

        def body(at, i, turn):
            rows = pl.ds(at, TOK)
            dh1 = nt(self.qkv[0, rows, :], self.weight(slots[0]))
            for stage in (1, 2):
                dh1 += nt(self.qkv[stage, rows, :], self.weight(slots[stage]))

            @pl.when(i >= 2)
            def _():
                copy(i - 2).wait()

            turns[turn] = dh1

            def step(c, carry):
                piece(at, pl.multiple_of(c * GROUP, GROUP), turn)
                return carry
            lax.fori_loop(0, TOK // GROUP, step, 0)
            copy(i).start()

        self.stream(body, loads, low, high)
        if high == count:
            for i in range(max(count - 2, 0), count):
                copy(i).wait()


class Spot:
    def __init__(self, layers):
        self.layers = layers
        wide, self.c = lax.axis_index("wide"), lax.axis_index("narrow")
        self.z, self.p = lax.div(wide, 4), lax.rem(wide, 4)
        self.px = self.p + 1 - 2 * lax.rem(self.p, 2)
        self.py = lax.rem(self.p + 2, 4)
        self.pd = 3 - self.p
        self.me = 2 * wide + self.c
        self.count = 8 * layers
        self.sibling = self.device(self.z, self.p, 1 - self.c)
        self.across_x = self.device(self.z, self.px, self.c)
        self.across_y = self.device(self.z, self.py, self.c)
        self.pa = jnp.where(self.c == 0, self.px, self.py)
        self.pb = jnp.where(self.c == 0, self.py, self.px)
        self.across_a = self.device(self.z, self.pa, self.c)
        self.across_b = self.device(self.z, self.pb, self.c)

    def device(self, z, p, c):
        return (z * 4 + p, c)

    def layer(self, k):
        return lax.rem(self.z + k, self.layers)

    def in_layer(self, z):
        return self.device(z, self.p, self.c)

    def others(self, body):
        def step(k, carry):
            other = lax.rem(self.me + k, self.count)
            body(k, other, (lax.div(other, 2), lax.rem(other, 2)))
            return carry
        lax.fori_loop(1, self.count, step, 0)

    def meet(self):
        door = pltpu.get_barrier_semaphore()
        self.others(lambda k, other, device: pl.semaphore_signal(door, 1, device_id=device, device_id_type=MESH))
        pl.semaphore_wait(door, self.count - 1)


def remote(src, dst, send, recv, device):
    return pltpu.make_async_remote_copy(src, dst, send, recv, device_id=device, device_id_type=MESH)


class Posted:
    def __init__(self):
        self.groups = {}

    def go(self, key, *args):
        copy = remote(*args)
        copy.start()
        self.groups.setdefault(key, []).append(copy)

    def sent(self, key):
        for copy in self.groups.pop(key, []):
            copy.wait_send()

    def all_sent(self):
        for key in list(self.groups):
            self.sent(key)


class Gather(Posted):
    @staticmethod
    def scratch(layers, rows):
        D = pltpu.SemaphoreType.DMA
        n = STAGES
        return [pltpu.VMEM((n, rows, COL), F32), D((n,)), D((n,)), D((n,)), D((n, layers)), D((n, layers)),
                D((n, layers, 2)), D((n, layers, 2)), D((n, 2)), D((n, 2)), D((n, 4)), D((n, 4))]

    def __init__(self, spot, full, owned, refs):
        super().__init__()
        self.spot, self.full, self.owned = spot, full, owned
        (self.desk, self.local, self.es, self.er, self.zs, self.zr, self.ps, self.pr, self.ds, self.dr, self.ss, self.sr) = refs
        self.rows = self.desk.shape[1]
        self.half = self.rows // 2
        self.cut = self.rows // 32 * 16 + (16 if self.rows % 32 else 0)

    def line(self, j, p, side=None):
        return self.full.at[j, :, p, :, unit_cols(self.spot.c if side is None else side)]

    def block(self, j, z, p):
        return self.full.at[j, z, p, :, unit_cols(self.spot.c)]

    def shard(self, j, unit):
        if j < 3:
            column = 2 * COL * lax.rem(unit, 3) + COL * lax.div(unit, 3)
            return self.owned[0].at[:, pl.ds(pl.multiple_of(column, 128), COL)]
        return self.owned[j - 2].at[:, pl.ds(pl.multiple_of(COL * lax.rem(unit, 2), 128), COL)]

    def desk_rows(self, j, core):
        return self.desk.at[j, pl.ds(pl.multiple_of(self.half * core, 8), self.half), :]

    def prepare(self, j):
        c = self.spot.c
        place_at = self.desk_rows(j, c)
        pltpu.make_async_copy(self.shard(j, 2 * j + c), place_at, self.local.at[j]).start()
        self.go(j, self.shard(j, 2 * j + 1 - c), place_at, self.es.at[j], self.er.at[j], self.spot.sibling)

    def across(self, j, k):
        s = self.spot
        block = self.block(j, s.layer(s.layers - k), s.p)
        self.go(j, block, block, self.ps.at[j, k, 0], self.pr.at[j, k, 0], s.across_x)
        self.go(j, block, block, self.ps.at[j, k, 1], self.pr.at[j, k, 1], s.across_y)

    def e1(self, j):
        s = self.spot
        mine, other = self.desk_rows(j, s.c), self.desk_rows(j, 1 - s.c)
        pltpu.make_async_copy(mine, mine, self.local.at[j]).wait()
        remote(other, other, self.es.at[j], self.er.at[j], s.sibling).wait_recv()
        self.block(j, s.z, s.p)[...] = self.desk[j].astype(BF)
        self.across(j, 0)

    def e0(self, j):
        s = self.spot
        block = self.block(j, s.z, s.p)
        for k in range(1, s.layers):
            self.go(j, block, block, self.zs.at[j, k], self.zr.at[j, k], s.in_layer(s.layer(k)))

    def e2(self, j):
        s = self.spot
        for k in range(1, s.layers):
            z = s.layer(s.layers - k)
            block = self.block(j, z, s.p)
            remote(block, block, self.zs.at[j, k], self.zr.at[j, k], s.in_layer(z)).wait_recv()
            self.across(j, k)
        self.to_sibling(j, 0, s.p)

    def to_sibling(self, j, i, p):
        line = self.line(j, p)
        self.go(j, line, line, self.ss.at[j, i], self.sr.at[j, i], self.spot.sibling)

    def corner(self, j, p, top):
        rows = pl.ds(0, self.cut) if top else pl.ds(self.cut, self.rows - self.cut)
        return self.full.at[j, :, p, rows, unit_cols(self.spot.c)]

    def e3(self, j):
        s = self.spot
        for k in range(s.layers):
            z = s.layer(s.layers - k)
            for i, p in ((0, s.px), (1, s.py)):
                block = self.block(j, z, p)
                remote(block, block, self.ps.at[j, k, i], self.pr.at[j, k, i], s.across_x).wait_recv()
        top, rest = self.corner(j, s.pa, True), self.corner(j, s.pb, False)
        self.go(j, top, top, self.ds.at[j, 0], self.dr.at[j, 0], s.across_b)
        self.go(j, rest, rest, self.ds.at[j, 1], self.dr.at[j, 1], s.across_a)
        self.to_sibling(j, 1, s.px)
        self.to_sibling(j, 2, s.py)

    def e4(self, j):
        s = self.spot
        top, rest = self.corner(j, s.pd, True), self.corner(j, s.pd, False)
        remote(top, top, self.ds.at[j, 0], self.dr.at[j, 0], s.across_y).wait_recv()
        remote(rest, rest, self.ds.at[j, 1], self.dr.at[j, 1], s.across_x).wait_recv()
        self.to_sibling(j, 3, s.pd)

    def e5(self, j):
        s = self.spot
        for i, p in enumerate((s.p, s.px, s.py, s.pd)):
            line = self.line(j, p, 1 - s.c)
            remote(line, line, self.ss.at[j, i], self.sr.at[j, i], s.sibling).wait_recv()


class Scatter(Posted):
    SLOTS = 3

    @staticmethod
    def scratch(layers, rows):
        D, V = pltpu.SemaphoreType.DMA, pltpu.VMEM
        n, m = STAGES, Scatter.SLOTS
        return [V((n - 1, layers, 4, rows, COL), BF), V((m, layers, rows, COL), BF), V((m, 2, layers, rows, COL), BF),
                V((m, layers, rows, COL), BF), V((m, rows, COL), F32), V((UNITS, rows // 2, COL), F32),
                D((n, layers // 2)), D((n, layers // 2)), D((n, 2, layers)), D((n, 2, layers)), D((n, 2, layers)), D((n, 2, layers)), D((n, layers)), D((n, layers)), D((n,)), D((n,))]

    def __init__(self, spot, part, refs):
        super().__init__()
        self.spot, self.part = spot, part
        (self.sums, self.dg, self.pl, self.zb, self.fin, self.res,
         self.ss, self.sr, self.ds, self.dr, self.ps, self.pr, self.zs, self.zr, self.fs, self.fr) = refs
        self.rows = self.dg.shape[2]
        self.half = self.rows // 2
        self.cut = self.rows // 32 * 16 + (16 if self.rows % 32 else 0)

    def sum_at(self, j):
        return self.sums.at[j % (STAGES - 1)]

    def each_layer(self, body):
        def step(z, carry):
            body(z)
            return carry
        lax.fori_loop(0, self.spot.layers, step, 0)

    def f1(self, j, i):
        s = self.spot
        two = pl.ds(2 * i, 2)
        self.go(("f1", j), self.part.at[j % 2, two, :, :, unit_cols(1 - s.c)], self.sum_at(j).at[two], self.ss.at[j, i], self.sr.at[j, i], s.sibling)

    def order(self):
        return [*range(1, self.spot.layers), 0]

    def corners(self, j):
        s = self.spot
        total, slot = self.sum_at(j), j % self.SLOTS
        for k in self.order():
            z = s.layer(k)
            for i, (rows, device) in enumerate(((pl.ds(0, self.cut), s.across_b), (pl.ds(self.cut, self.rows - self.cut), s.across_a))):
                self.go(j, total.at[z, s.pd, rows, :], self.dg.at[slot, z, rows, :], self.ds.at[j, i, k], self.dr.at[j, i, k], device)

    def f2(self, j):
        s = self.spot
        own, total = self.part.at[j % 2], self.sum_at(j)
        for i in range(s.layers // 2):
            came = total.at[pl.ds(2 * i, 2)]
            remote(came, came, self.ss.at[j, i], self.sr.at[j, i], s.sibling).wait_recv()

        def add(p):
            def one(z):
                total[z, p] = total[z, p] + own[z, p, :, unit_cols(s.c)]
            self.each_layer(one)

        add(s.pd)
        self.corners(j)
        for p in (s.px, s.py, s.p):
            add(p)

    def f3(self, j):
        s = self.spot
        total, slot = self.sum_at(j), j % self.SLOTS
        for k in self.order():
            z = s.layer(k)
            for i, (low, size, p) in enumerate(((0, self.cut, s.pa), (self.cut, self.rows - self.cut, s.pb))):
                rows = pl.ds(low, size)
                came = self.dg.at[slot, z, rows, :]
                remote(came, came, self.ds.at[j, i, k], self.dr.at[j, i, k], s.across_y).wait_recv()
                total[z, p, rows, :] = total[z, p, rows, :] + came[...]
            for i, (p, device) in enumerate(((s.px, s.across_x), (s.py, s.across_y))):
                self.go(j, total.at[z, p], self.pl.at[slot, i, z], self.ps.at[j, i, k], self.pr.at[j, i, k], device)

    def f4(self, j):
        s = self.spot
        total, slot = self.sum_at(j), j % self.SLOTS
        for k in self.order():
            z = s.layer(k)
            for i in range(2):
                came = self.pl.at[slot, i, z]
                remote(came, came, self.ps.at[j, i, k], self.pr.at[j, i, k], s.across_x).wait_recv()
            total[z, s.p] = (total[z, s.p].astype(F32) + self.pl[slot, 0, z].astype(F32) + self.pl[slot, 1, z].astype(F32)).astype(BF)
            if k:
                self.go(j, total.at[z, s.p], self.zb.at[slot, k], self.zs.at[j, k], self.zr.at[j, k], s.in_layer(z))

    def f5(self, j):
        s = self.spot
        slot = j % self.SLOTS
        total = self.sums[j % (STAGES - 1), s.z, s.p].astype(F32)
        for k in range(1, s.layers):
            came = self.zb.at[slot, k]
            remote(came, came, self.zs.at[j, k], self.zr.at[j, k], s.across_x).wait_recv()
            total = total + self.zb[slot, k].astype(F32)
        self.sent(j)
        self.sent(("fin", j - self.SLOTS))
        self.fin[slot] = total
        mine, other = (pl.ds(pl.multiple_of(self.half * c, 8), self.half) for c in (s.c, 1 - s.c))
        self.res[2 * j + s.c] = self.fin[slot, mine, :]
        self.go(("fin", j), self.fin.at[slot, other, :], self.res.at[2 * j + s.c], self.fs.at[j], self.fr.at[j], s.sibling)

    def f6(self, j):
        s = self.spot
        came = self.res.at[2 * j + 1 - s.c]
        remote(came, came, self.fs.at[j], self.fr.at[j], s.sibling).wait_recv()


class Everyone(Posted):
    @staticmethod
    def scratch(count):
        D = pltpu.SemaphoreType.DMA
        return [D((count,)), D((count,))]

    def __init__(self, spot, board, refs):
        self.spot, self.board = spot, board
        self.send_sem, self.recv_sem = refs

    def post(self, source):
        s = self.spot
        def one(k, other, device):
            remote(source(other), self.board.at[s.me], self.send_sem.at[k], self.recv_sem.at[k], device).start()
        s.others(one)

    def collect(self, own):
        s = self.spot
        def one(k, other, device):
            came = self.board.at[lax.rem(s.me + s.count - k, s.count)]
            remote(came, came, self.send_sem.at[k], self.recv_sem.at[k], device).wait()
        s.others(one)
        self.board[s.me] = own


FORWARD_ORDER = (
    "e10", "e00", "e11", "e01", "e12", "e13", "e14", "e15", "v", "n0", "n1", "e20", "e02", "n2", "e21", "e30", "n3", "e22", "e03",
    "e31", "e40", "e32", "e23", "e04", "e41", "e50", "e05", "p0", "e51", "p1", "e24", "e42", "a0", "e33", "a1", "a2", "e52", "a3",
    "p2", "e34", "a4", "e25", "e43", "a5", "a6", "a7", "e53", "m", "e44", "r", "e54", "h", "e35", "g", "e45", "Y", "e55",
)
BACKWARD_ORDER = (
    "h", "f30", "g1", "s", "f21", "f40", "g2", "f31", "m", "f22", "a0", "a1", "a2", "a3", "f41", "g3", "f32", "f50", "a4", "a5",
    "f23", "a6", "a7", "f42", "g4", "f33", "f51", "f24", "g5", "r0", "r1", "f52", "f43", "f34", "f25", "r2", "r3", "f53", "f44", "n01",
    "f35", "n13", "f45", "f54", "n34",
)


def place(kind, count):
    return [pl.BlockSpec(memory_space=kind)] * count


def load(src, dst, sem):
    copy = pltpu.make_async_copy(src, dst, sem)
    copy.start()
    return copy


def window_tile(per, owner):
    return lax.div(per * owner, 128)


def forward_kernel(layers, *refs):
    joined = layers > 0
    refs = list(refs)
    take = lambda n: [refs.pop(0) for _ in range(n)]
    x, dy, seg_in, start_in, rope = take(5)
    owned = take(5) if joined else take(2)
    turned, qkv_out, att_out, r1_out, dg_out, e2_out, act_out, stats_out, bsum_out, down_out = take(10)
    weights_out, vec_out = take(2) if joined else (None, None)
    full, xv, dyv, h1, tt, qkv, att, mix, r1, dg, stats, bsum, seg, start, sem, dsem = take(16)
    fetch = [load(x, xv, sem.at[0]), load(dy, dyv, sem.at[1])]
    bsum[...] = jnp.zeros_like(bsum)
    seg[...] = turn_table(seg_in)
    start[...] = turn_table(start_in)
    if joined:
        spot = Spot(layers)
        board, canvas, vec, wsem, came, csend, crecv = take(7)
        everyone = Everyone(spot, board, take(2))
        gather = Gather(spot, full, owned[:4], refs)
        window = owned[4]
        weight = lambda j: full[j].reshape(h1.shape[1], h1.shape[1])
        spot.meet()
        for j in range(STAGES):
            gather.prepare(j)
        everyone.post(lambda other: window)
        canvas[...] = jnp.zeros_like(canvas)
    else:
        vec = owned[1]
        weight = lambda j: full[j]
        fetch.append(load(owned[0], full, sem.at[2]))
    f = Forward(weight, (xv, dyv, seg, start, vec, rope, h1, tt, qkv, att, mix, r1, dg, stats, bsum))
    blocks = f.tokens // TOK
    groups = f.tokens // GROUP
    outs = {}

    def vectors():
        everyone.collect(window[...])
        share = 4 * f.width // spot.count

        def put(owner, carry):
            canvas[pl.ds(window_tile(share, owner), 2)] += board[owner]
            return carry
        lax.fori_loop(0, spot.count, put, 0)
        tiles = f.width // 128
        for row in range(4):
            for tile in range(tiles):
                vec[row : row + 1, 128 * tile : 128 * (tile + 1)] = canvas[row * tiles + tile]

    def norm(i):
        if i == 0:
            fetch[0].wait()
            fetch[1].wait()
        f.norms(i * blocks // 4, (i + 1) * blocks // 4)
        if i == 3:
            outs["h1"] = load(tt.at[0], turned.at[0], sem.at[3])
            outs["e2"] = load(dyv, e2_out, sem.at[4])

    def attend(i):
        f.attend(i // 4, i % 4 * groups // 4, (i % 4 + 1) * groups // 4)

    def turn_mix():
        outs["qkv"] = load(qkv, qkv_out, sem.at[5])
        outs["att"] = load(att, att_out, sem.at[6])
        f.mix_turned(1)
        outs["o"] = load(tt.at[1], turned.at[1], sem.at[7])

    def residual():
        outs.pop("h1").wait()
        f.residual(0)
        outs["h2"] = load(tt.at[0], turned.at[2], sem.at[3])
        outs["r1"] = load(r1, r1_out, sem.at[8])

    def hidden():
        outs.pop("o").wait()
        f.hidden(1)
        outs["dg"] = load(dg, dg_out, sem.at[9])
        outs["act"] = load(mix, act_out, sem.at[7])

    def down_grad():
        outs.pop("qkv").wait()
        f.down_grad(1, (lambda i: exchange(i).start()) if joined else (lambda i: None))

    down_chunks = f.width // TOK

    def exchange(i):
        return remote(f.chunk(i).at[:, unit_cols(1 - spot.c)], came.at[i], csend.at[i], crecv.at[i], spot.sibling)

    def receive():
        for i in range(down_chunks):
            exchange(i).wait()
            came[i] = came[i] + f.chunk(i)[:, unit_cols(spot.c)]
            outs["d", i] = load(came.at[i], down_out.at[i], dsem.at[i])

    steps = {"v": vectors, "n": norm, "p": f.project, "a": attend, "m": turn_mix, "r": residual, "h": hidden, "g": down_grad,
             "Y": receive}
    if joined:
        for name in FORWARD_ORDER:
            if name in steps:
                steps[name]()
            elif name[0] == "e":
                j = int(name[2])
                getattr(gather, name[:2])(j)
                if name[1] == "5":
                    outs["w", j] = load(full.at[j], weights_out.at[j], wsem.at[j])
            else:
                steps[name[0]](int(name[1]))
    else:
        for i in range(4):
            norm(i)
        fetch[2].wait()
        for j in range(3):
            f.project(j)
        for i in range(8):
            attend(i)
        for name in "mrhg":
            steps[name]()
        for i in range(down_chunks):
            outs["d", i] = load(f.chunk(i), down_out.at[i], dsem.at[i])
    outs["stats"] = load(stats, stats_out, sem.at[10])
    outs["bsum"] = load(bsum, bsum_out, sem.at[11])
    if joined:
        outs["vec"] = load(vec, vec_out, sem.at[2])
    for copy in outs.values():
        copy.wait()
    if joined:
        gather.all_sent()


def forward(layers, rows, x, dy, seg, start, rope, owned):
    tokens, width = x.shape
    S = jax.ShapeDtypeStruct
    V = pltpu.VMEM
    D = pltpu.SemaphoreType.DMA
    joined = layers > 0
    shape = (STAGES, layers, 4, rows, width) if joined else (STAGES, width, width)
    chunks = width // TOK
    outs = [S((3, width, tokens), BF), S((3, tokens, width), BF), S((2, tokens, 4 * SPAN), BF),
            S((tokens, width), F32), S((tokens, width), BF), S((tokens, width), BF), S((tokens, width), BF), S((tokens, 128), F32), S((8, width), F32),
            S((chunks, TOK, COL if joined else width), BF)]
    scratch = [V(shape, BF), V((tokens, width), BF), V((tokens, width), BF), V((tokens, width), BF), V((2, width, tokens), BF),
               V((3, tokens, width), BF), V((2, tokens, 4 * SPAN), BF), V((tokens, width), BF), V((tokens, width), F32),
               V((tokens, width), BF), V((tokens, 128), F32), V((8, width), F32), V((tokens // PATCHES, PATCHES), F32), V((tokens // PATCHES, PATCHES), F32), D((12,)), D((chunks,))]
    if joined:
        outs += [S(shape, BF), S((8, width), F32)]
        count = 8 * layers
        scratch += [V((count, 2, 1, 128), F32), V((4 * width // 128 + 8, 1, 128), F32), V((8, width), F32), D((STAGES,)),
                    V((chunks, TOK, COL), BF), D((chunks,)), D((chunks,))]
        scratch += Everyone.scratch(count) + Gather.scratch(layers, rows)
    return pl.pallas_call(
        functools.partial(forward_kernel, layers),
        out_shape=outs,
        in_specs=place(pl.ANY, 2) + place(pltpu.VMEM, 3) + (place(pl.ANY, 4) if joined else place(pl.ANY, 1)) + place(pltpu.VMEM, 1),
        out_specs=place(pl.ANY, len(outs)),
        scratch_shapes=scratch,
        compiler_params=pltpu.CompilerParams(vmem_limit_bytes=VMEM_LIMIT, **(dict(collective_id=0, has_side_effects=True) if joined else {})),
        name="layer_forward",
    )(x, dy, seg, start, rope, *owned)


def backward_kernel(layers, *refs):
    joined = layers > 0
    refs = list(refs)
    take = lambda n: [refs.pop(0) for _ in range(n)]
    x, dy, start_in, rope, vec, turned, qkv_in, att_in, r1_in, dg_in, e2_in, act_in, stats_in, bsum_in, down_in, gw = take(16)
    out, dx_out, grad_out, small_out = take(4)
    norm_out = take(1)[0] if joined else None
    wbuf, part, lt, ea, eb, qkv, att, stats, bsum, rblk, bblk, hold, start, sem, ssem, osem, psem = take(17)
    start[...] = turn_table(start_in)

    def weights(j, slot, s):
        return load(gw.at[j], wbuf.at[slot], s)

    if joined:
        spot = Spot(layers)
        board, norms, sheet, note = take(4)
        small_talk = Everyone(spot, board, take(2))
        norm_talk = Everyone(spot, norms, take(2))
        scatter = Scatter(spot, part, refs)
        down = load(down_in, scatter.sum_at(0), psem.at[0])
    first = [load(e2_in, ea, sem.at[1]), weights(5, 0, sem.at[0]), load(dg_in, eb, sem.at[3]), load(bsum_in, bsum, sem.at[5])]
    waits = {"w": []}

    def load_more(step):
        if step == 0:
            waits[1] = [load(turned.at[2], lt.at[0], sem.at[2])]
            waits["w4"] = weights(4, 1, sem.at[6])
            waits["stats"] = load(stats_in, stats, sem.at[4])
        if step == 1:
            waits[2] = [load(turned.at[1], lt.at[1], sem.at[7])]
            waits["w3"] = weights(3, 2, sem.at[8])
        if step == 2:
            waits["qkv"] = load(qkv_in, qkv, sem.at[9])
            waits["att"] = load(att_in.at[0], att, sem.at[10])

    b = Backward((wbuf, part, lt, ea, eb, qkv, att, vec, rope, stats, bsum, start, rblk, bblk))
    blocks = b.tokens // TOK
    groups = b.tokens // GROUP
    if joined:
        spot.meet()
        down.wait()
        scatter.corners(0)

    def spill(r):
        return pltpu.make_async_copy(part.at[r % 2], grad_out.at[r - 1], psem.at[r % 2])

    def grad(r):
        if r >= 3:
            if joined:
                scatter.sent(("f1", r - 2))
            else:
                spill(r - 2).wait()
        left, right = {1: (0, lambda cols: eb[:, cols]), 2: (1, lambda cols: ea[:, cols])}.get(r, (0, lambda cols: qkv[r - 3, :, cols]))
        for copy in waits.pop(r, []):
            copy.wait()
        b.weight_grad(r % 2, left, right, (lambda i: scatter.f1(r, i)) if joined else (lambda i: None))
        if not joined:
            spill(r).start()
        if r == 1:
            load_more(2)
            waits[3] = [load(turned.at[0], lt.at[0], sem.at[2])]

    loads = [(r1_in, rblk, ssem.at[0]), (dy, bblk, ssem.at[1])]

    def hidden():
        for copy in first:
            copy.wait()
        load_more(0)
        b.hidden(0)
        load_more(1)

    def second_norm():
        waits["w4"].wait()
        waits["stats"].wait()
        b.second_norm(1, loads, hold, 0, blocks)
        waits["w"].append(weights(0, 1, sem.at[6]))

    def mixed():
        waits["w3"].wait()
        b.mixed(2)
        waits["w"].append(weights(1, 2, sem.at[8]))
        waits["qkv"].wait()

    def attend(i):
        if i == 0:
            waits["att"].wait()
        if i == 4:
            waits["a"].wait()
        b.attend(i // 4, i % 4 * groups // 4, (i % 4 + 1) * groups // 4)
        if i == 3:
            waits["a"] = load(att_in.at[1], att, sem.at[10])
        if i == 7:
            waits["act"] = load(act_in, eb, sem.at[3])

    def result(i):
        if i == 0:
            waits["act"].wait()
        b.result(0, loads, out, osem, i * blocks // 4, (i + 1) * blocks // 4)
        if i == 3:
            waits["w"].append(weights(2, 0, sem.at[0]))

    def first_norm(low, high):
        if low == 0:
            for copy in waits["w"]:
                copy.wait()
        b.first_norm((1, 2, 0), [(x, bblk, ssem.at[1])], dx_out, osem, rblk, low * blocks // 4, high * blocks // 4)

    for name in BACKWARD_ORDER:
        if name[0] == "f":
            if joined:
                getattr(scatter, name[:2])(int(name[2]))
        elif name[0] in "gar":
            {"g": grad, "a": attend, "r": result}[name[0]](int(name[1]))
        elif name[0] == "n":
            first_norm(int(name[1]), int(name[2]))
        else:
            {"h": hidden, "s": second_norm, "m": mixed}[name]()
    if not joined:
        fin = load(bsum, small_out, sem.at[5])
        for r in range(STAGES - 2, STAGES):
            spill(r).wait()
        fin.wait()
        return
    tiles = b.width // 128
    for row, source in enumerate((3, 2, 1, 0)):
        for tile in range(tiles):
            sheet[row * tiles + tile] = bsum[source : source + 1, 128 * tile : 128 * (tile + 1)]
    share = 4 * b.width // spot.count
    own = lambda owner: sheet.at[pl.ds(window_tile(share, owner), 2)]
    small_talk.post(own)
    small_talk.collect(sheet[pl.ds(window_tile(share, spot.me), 2)])

    def add(owner, carry):
        return carry + board[owner]
    total = lax.fori_loop(0, spot.count, add, jnp.zeros((2, 1, 128), F32))
    first = lax.rem(share * spot.me, 128)
    spots = lax.broadcasted_iota(jnp.int32, (2, 1, 128), 0) * 128 + lax.broadcasted_iota(jnp.int32, (2, 1, 128), 2)
    mine = jnp.where((spots >= first) & (spots < first + share), total, 0.0)
    small_out[...] = mine
    scatter.f5(STAGES - 1)
    for j in range(STAGES):
        scatter.f6(j)
    fin = load(scatter.res, grad_out, sem.at[9])

    def square(unit, carry):
        values = scatter.res[unit]
        return carry + jnp.sum(values * values, 0, keepdims=True)
    squares = lax.fori_loop(0, UNITS, square, jnp.zeros((1, COL), F32))
    value = jnp.sum(squares) + jnp.sum(mine * mine)
    note[...] = jnp.full((8, 128), value, F32)
    norm_talk.post(lambda other: note)
    norm_talk.collect(note[...])
    whole = lax.fori_loop(0, spot.count, lambda owner, carry: carry + norms[owner], jnp.zeros((8, 128), F32))
    norm_out[...] = jnp.sqrt(whole)
    fin.wait()
    scatter.all_sent()


def backward(layers, rows, *args):
    tokens, width = args[0].shape
    S = jax.ShapeDtypeStruct
    V = pltpu.VMEM
    D = pltpu.SemaphoreType.DMA
    joined = layers > 0
    grid = (layers, 4, rows, width) if joined else (width, width)
    outs = [S((tokens, width), F32), S((tokens, width), F32)]
    scratch = [V((3,) + grid, BF), V((2,) + grid, BF), V((2, width, tokens), BF), V((tokens, width), BF), V((tokens, width), BF),
               V((3, tokens, width), BF), V((tokens, 4 * SPAN), BF), V((tokens, 128), F32), V((8, width), F32),
               V((2, TOK, width), F32), V((2, TOK, width), BF), V((TOK, width), F32), V((tokens // PATCHES, PATCHES), F32), D((11,)), D((2, 2)), D((2,)), D((2,))]
    specs = place(pl.ANY, 4)
    if joined:
        count = 8 * layers
        outs += [S((UNITS, rows // 2, COL), F32), S((2, 1, 128), F32), S((8, 128), F32)]
        specs = place(pl.ANY, 3) + place(pltpu.VMEM, 2)
        scratch += [V((count, 2, 1, 128), F32), V((count, 8, 128), F32), V((4 * width // 128 + 8, 1, 128), F32), V((8, 128), F32)]
        scratch += Everyone.scratch(count) + Everyone.scratch(count) + Scatter.scratch(layers, rows)
    else:
        outs += [S((STAGES - 1, width, width), BF), S((8, width), F32)]
    return pl.pallas_call(
        functools.partial(backward_kernel, layers),
        out_shape=outs,
        in_specs=place(pl.ANY, 2) + place(pltpu.VMEM, 3) + place(pl.ANY, 11),
        out_specs=specs,
        scratch_shapes=scratch,
        compiler_params=pltpu.CompilerParams(vmem_limit_bytes=VMEM_LIMIT, **(dict(collective_id=1, has_side_effects=True) if joined else {})),
        name="layer_backward",
    )(*args)


def adam_update(master, gradient, first, second, clip_scale, weight_decay, step_rate):
    gradient = gradient * clip_scale
    first_new = beta_first * first + (1.0 - beta_first) * gradient
    second_new = beta_second * second + (1.0 - beta_second) * gradient * gradient
    fix_first = 1.0 - beta_first**STEP
    fix_second = 1.0 - beta_second**STEP
    update_step = (
        first_new / fix_first / (jnp.sqrt(second_new / fix_second) + eps_adam)
        + weight_decay * master
    )
    master_new = master - step_rate * update_step
    return (master_new, first_new, second_new)


def adam_kernel(*refs):
    refs = list(refs)
    take = lambda n: [refs.pop(0) for _ in range(n)]
    sources, large = take(14), take(2)
    results, norm_out, large_out = take(16), take(1)[0], take(2)
    held, made = take(14), take(16)
    carried, in_sem, out_sem, large_sem = refs
    copies = [load(src, dst, in_sem.at[i]) for i, (src, dst) in enumerate(zip(sources, held))]
    outs = []
    piece = large[0].shape[0] // 4
    parts = [(i, at, pl.ds(piece * at, piece)) for i in range(2) for at in range(4)]
    passing = [load(large[i].at[rows, :], carried.at[i, rows, :], large_sem.at[i, at]) for i, at, rows in parts]
    for copy in copies[:2]:
        copy.wait()
    grads, norm = held[:2]
    norm_out[...] = norm[0:1, 0:1]
    clip_scale = jnp.minimum(1.0, clip_limit / (norm[0:1, 0:1] + 1e-06))
    for i in range(4):
        mine = [2 + i, 6 + i, 10 + i]
        for at in mine:
            copies[at].wait()
        for at, unit in enumerate(COLUMNS[i]):
            cols = slice(COL * at, COL * (at + 1))
            new = adam_update(*(held[m][:, cols] for m in mine[:1]), grads[unit], *(held[m][:, cols] for m in mine[1:]), clip_scale, decay_rate, learn_rate)
            for kind, value in enumerate((*new, new[0].astype(BF))):
                made[4 * kind + i][:, cols] = value
        outs += [load(made[4 * kind + i], results[4 * kind + i], out_sem.at[4 * kind + i]) for kind in range(4)]
    for copy, (i, at, rows) in zip(passing, parts):
        copy.wait()
        outs.append(load(carried.at[i, rows, :], large_out[i].at[rows, :], large_sem.at[i, at]))
    for copy in outs:
        copy.wait()


def adam_matrices(grads, norm, masters, firsts, seconds, large):
    shapes = [jax.ShapeDtypeStruct(m.shape, F32) for m in masters] * 3 + [jax.ShapeDtypeStruct(m.shape, BF) for m in masters]
    ins = (grads, norm, *masters, *firsts, *seconds)
    room = lambda arrays: [pltpu.VMEM(a.shape, a.dtype) for a in arrays]
    made = pl.pallas_call(
        adam_kernel,
        out_shape=[*shapes, jax.ShapeDtypeStruct((1, 1), F32), *(jax.ShapeDtypeStruct(m.shape, F32) for m in large)],
        in_specs=place(pl.ANY, 16),
        out_specs=place(pl.ANY, 16) + place(pltpu.VMEM, 1) + place(pl.ANY, 2),
        scratch_shapes=[*room(ins), *room(shapes), pltpu.VMEM((2,) + large[0].shape, F32), pltpu.SemaphoreType.DMA((14,)), pltpu.SemaphoreType.DMA((16,)), pltpu.SemaphoreType.DMA((2, 4))],
        compiler_params=pltpu.CompilerParams(vmem_limit_bytes=VMEM_LIMIT),
        name="adam",
    )(*ins, *large)
    return [made[4 * i : 4 * i + 4] for i in range(4)], made[16], made[17:]


def stage_columns(full_in, full_out, full_up, full_down):
    parts = [full_in[:, 2 * COL * (u % 3) + COL * (u // 3) :][:, :COL] for u in range(6)]
    pairs = [jnp.concatenate(parts[2 * i : 2 * i + 2], 1) for i in range(3)]
    return jnp.stack([*pairs, full_out, full_up, full_down])


COLUMNS = ((6, 9, 7, 10, 8, 11), (4, 5), (2, 3), (0, 1))


def by_matrix(units):
    return [jnp.concatenate([units[i] for i in at], 1) for at in COLUMNS]


def turned_down(kept, joined, layers, rows):
    down = kept[-1].reshape(layers, 4, rows, COL) if joined else kept[-1]
    return (*kept[:-1], down)


def shards(
    inputs,
    segments,
    starts,
    out_grad,
    proj_in,
    proj_out,
    up_proj,
    down_proj,
    gains_biases,
    first_in,
    first_out,
    first_up,
    first_down,
    first_small,
    second_in,
    second_out,
    second_up,
    second_down,
    second_small,
):
    axes = ("wide", "narrow")
    wide, narrow = lax.axis_size("wide"), lax.axis_size("narrow")
    tokens, width = inputs.shape
    share = gains_biases.shape[0]
    me = lax.axis_index("wide") * narrow + lax.axis_index("narrow")
    rows = width // wide
    joined = narrow == 2 and wide % 4 == 0 and rows % 16 == 0 and share == 160
    layers = wide // 4 if joined else 0
    rope = jnp.asarray(rope_tables())
    small_low = lax.reduce_precision(gains_biases, 8, 7)
    if joined:
        shift = lax.rem(share * me, 128)
        window = lax.dynamic_slice(jnp.pad(small_low, (96, 96)), (96 - shift,), (256,)).reshape(2, 1, 128)
        *kept, weights, vec = forward(layers, rows, inputs, out_grad, segments.T, starts.T, rope, (proj_in, proj_out, up_proj, down_proj, window))
    else:
        gathered = [lax.all_gather(m.astype(BF), axes, axis=0, tiled=True) for m in (proj_in, proj_out, up_proj, down_proj)]
        weights = stage_columns(*gathered)
        vec = lax.all_gather(small_low, axes, axis=0, tiled=True).reshape(4, width)
        vec = jnp.pad(vec, ((0, 4), (0, 0)))
        kept = forward(layers, rows, inputs, out_grad, segments.T, starts.T, rope, (weights, vec))
    made = backward(layers, rows, inputs, out_grad, starts.T, rope, vec, *turned_down(kept, joined, layers, rows), weights)
    block_out, input_grad = made[:2]
    mats, firsts, seconds = (proj_in, proj_out, up_proj, down_proj), (first_in, first_out, first_up, first_down), (second_in, second_out, second_up, second_down)
    if joined:
        shard_small = lax.dynamic_slice(made[3].reshape(256), (shift,), (share,))
        mat_news, grad_norm, (block_out, input_grad) = adam_matrices(made[2], made[4], mats, firsts, seconds, made[:2])
        grad_norm = grad_norm.reshape(())
        clip_scale = jnp.minimum(1.0, clip_limit / (grad_norm + 1e-06))
    else:
        stages = jnp.concatenate([kept[-1].reshape(1, width, width), made[2]], 0).astype(F32)
        full_grads = by_matrix([stages[i // 2][:, COL * (i % 2) :][:, :COL] for i in range(UNITS)])
        scatter = lambda m: lax.psum_scatter(m, axes, scatter_dimension=0, tiled=True)
        grads = [scatter(m) for m in full_grads]
        shard_small = scatter(jnp.concatenate([made[3][3], made[3][2], made[3][1], made[3][0]]))
        squares = sum(jnp.sum(m * m) for m in (*grads, shard_small))
        grad_norm = jnp.sqrt(lax.psum(squares, axes))
        clip_scale = jnp.minimum(1.0, clip_limit / (grad_norm + 1e-06))
        each = [adam_update(*four, clip_scale, decay_rate, learn_rate) for four in zip(mats, grads, firsts, seconds)]
        mat_news = [[new[i] for new in each] for i in range(3)]
        mat_news.append([m.astype(BF) for m in mat_news[0]])
    small_new = adam_update(gains_biases, shard_small, first_small, second_small, clip_scale, 0.0, small_rate)
    small_news = (*small_new, small_new[0].astype(BF))
    return (
        block_out,
        input_grad,
        grad_norm,
        *(part for mat, small in zip(mat_news, small_news) for part in (*mat, small)),
    )


def solution(mesh):
    split, flat = P(("wide", "narrow"), None), P(("wide", "narrow"))
    state = (split, split, split, split, flat)
    return jax.shard_map(
        shards,
        mesh=mesh,
        in_specs=(split,) * 4 + state * 3,
        out_specs=(split, split, P()) + state * 4,
        check_vma=False,
    )
```
